32 devices in a mesh: section: 4 (over y, x), row: 2 (over core), col: 4 (over z).
Axes of the slice: x: 2, y: 2, z: 4, core: 2. Of those that a mesh axis runs over, the one named last changes fastest.
Arguments:
- features: bfloat16 [2, 2, 8, 64, 192], P(None, None, 'row', 'col'), may hold values from -6 to 6
- gate_weight: bfloat16 [4, 3456, 768], P('section', 'row'), may hold values from -0.109375 to 0.109375
- gate_bias: float32 [4, 768], P('section'), may hold values from -3 to 3
Outputs:
- level_hidden: bfloat16 [4, 2, 2, 8, 64, 192], P('section', None, None, 'row', 'col')
The draws below stay inside these ranges and needn't reach their ends.
All inputs are finite; a program needn't handle non-finite values.
Results may differ from the reference program's by a relative error of at most 0.005.
Values may be sent and summed in bfloat16 or wider, within the bound.
No kernel may reach another device: no remote copies, remote signals or barrier semaphores. Data moves between devices by JAX's collectives and lax.ppermute only.
A program may use at most 64 MiB of HBM per device.

```python
import jax
import jax.numpy as jnp

C = 192
BATCH = 2
FRAMES = 2
KROWS = 3456
GATES = 768
HEIGHT = 8
WIDTH = 64


def shard_levels(own_key, extent, cuts, least, top_value):
    gain = 1.0
    for axis_at, blocks in cuts:
        draws = jax.random.uniform(jax.random.fold_in(jax.random.fold_in(own_key, 6), axis_at), (blocks,), jnp.float32, least / len(cuts), top_value / len(cuts))
        gain = gain * jnp.repeat(jnp.exp(draws), extent[axis_at] // blocks).reshape((-1,) + (1,) * (len(extent) - 1 - axis_at))
    return gain


def centred(rng, extent, scale, most, pieces=(), held_as=jnp.bfloat16):
    result = scale * jax.random.normal(rng, extent, jnp.float32)
    if pieces:
        result = result * shard_levels(rng, extent, pieces, -0.22, 0.18)
    return jnp.clip(result, -most, most).astype(held_as)


def setup_inputs(seed: int = 0) -> dict:
    keys = jax.random.split(jax.random.key(seed), 4)
    features = centred(keys[0], (BATCH, FRAMES, HEIGHT, WIDTH, C), 1.0, 6.0, ((2, 2), (3, 4)))
    gate_weight = centred(keys[1], (4, KROWS, GATES), KROWS ** -0.5, 0.109375, ((0, 4), (1, 2)))
    gate_bias = centred(keys[2], (4, GATES), 0.5, 3.0, ((0, 4),), jnp.float32)
    return dict(features=features, gate_weight=gate_weight, gate_bias=gate_bias)


def cell_update(gate_values, memory, channels):
    in_gate = jax.nn.sigmoid(gate_values[:, :channels])
    forget = jax.nn.sigmoid(gate_values[:, channels:2 * channels])
    candidate = jnp.tanh(gate_values[:, 2 * channels:3 * channels])
    out_gate = jax.nn.sigmoid(gate_values[:, 3 * channels:])
    next_memory = forget * memory + in_gate * candidate
    next_hidden = (out_gate * jnp.tanh(next_memory)).astype(jnp.bfloat16)
    return next_hidden, next_memory


def layer_step(inputs, hidden, memory, weight, gate_offset):
    joined = jnp.concatenate([inputs, hidden], axis=-1)
    batch_size, height, grid_width, channels = joined.shape
    padded = jnp.pad(joined, ((0, 0), (1, 1), (1, 1), (0, 0)))
    tap_list = []
    for row_tap in range(3):
        for col_tap in range(3):
            tap_list.append(padded[:, row_tap:row_tap + height, col_tap:col_tap + grid_width, :])
    patches = jnp.concatenate(tap_list, axis=-1).reshape(-1, 9 * channels)
    gate_values = jnp.dot(patches, weight, preferred_element_type=jnp.float32) + gate_offset
    hidden_width = hidden.shape[-1]
    next_hidden, next_memory = cell_update(gate_values, memory.reshape(-1, hidden_width), hidden_width)
    return next_hidden.reshape(hidden.shape), next_memory.reshape(memory.shape)


def reference(features, gate_weight, gate_bias):
    batch_size, frame_count, height, grid_width, channels = features.shape
    zero_hidden = jnp.zeros((batch_size, height, grid_width, channels), jnp.bfloat16)
    zero_memory = jnp.zeros((batch_size, height, grid_width, channels), jnp.float32)
    hidden, memory = zero_hidden, zero_memory
    first_level = []
    for frame_index in range(2):
        hidden, memory = layer_step(features[:, frame_index], hidden, memory, gate_weight[0], gate_bias[0])
        first_level.append(hidden)
    saved_hidden, saved_memory = hidden, memory
    hidden, memory = zero_hidden, zero_memory
    second_level = []
    for frame_index in range(2):
        hidden, memory = layer_step(first_level[frame_index], hidden, memory, gate_weight[1], gate_bias[1])
        second_level.append(hidden)
    context = hidden
    third_level = []
    for frame_index in range(2):
        hidden, memory = layer_step(context, hidden, memory, gate_weight[2], gate_bias[2])
        third_level.append(hidden)
    hidden, memory = saved_hidden, saved_memory
    fourth_level = []
    for frame_index in range(2):
        hidden, memory = layer_step(third_level[frame_index], hidden, memory, gate_weight[3], gate_bias[3])
        fourth_level.append(hidden)
    return jnp.stack([jnp.stack(first_level, 1), jnp.stack(second_level, 1),
                      jnp.stack(third_level, 1), jnp.stack(fourth_level, 1)], 0)
```

```python
import functools

import jax
import jax.numpy as jnp
from jax import lax
from jax.experimental import pallas as pl
from jax.experimental.pallas import tpu as pltpu
from jax.sharding import PartitionSpec as P

STEPS = 6
HALO = 8
TAPS = 9
BF = jnp.bfloat16
F32 = jnp.float32


def moved(block, axis, pairs):
    return lax.ppermute(block, axis, pairs)


def section_send(block, source, target):
    return lax.ppermute(block, "section", [(source, target)])


def gather_sequence(features):
    batch = features.shape[0]
    size = lax.axis_size("row")
    place = lax.axis_index("row") % batch
    mine = lax.dynamic_index_in_dim(features, place, 0, keepdims=False)
    parts = [mine]
    for k in range(1, batch):
        pairs = [(i, i - i % batch + (i % batch + k) % batch) for i in range(size)]
        sent = lax.dynamic_index_in_dim(features, (place + k) % batch, 0, keepdims=False)
        parts.append(moved(sent, "row", pairs))
    stacked = jnp.stack(parts)
    blocks = [
        lax.dynamic_index_in_dim(stacked, (place - q) % batch, 0, keepdims=False)
        for q in range(batch)
    ]
    return jnp.concatenate(blocks, axis=1)


def with_halo(array, axis, dim, stride):
    size, length = lax.axis_size(axis), array.shape[dim]
    up = [(i, i + stride) for i in range(size - stride)]
    down = [(j, i) for i, j in up]
    last = lax.slice_in_dim(array, length - HALO, length, axis=dim)
    first = lax.slice_in_dim(array, 0, HALO, axis=dim)
    before = moved(last, axis, up)
    after = moved(first, axis, down)
    return jnp.concatenate([before, array, after], axis=dim)


def sigmoid(x):
    return 0.5 * jnp.tanh(0.5 * x) + 0.5


class Step:
    def __init__(self, width, pixels, channels, shards):
        self.width, self.pixels, self.channels, self.shards = (width, pixels, channels, shards)

    def weight_copy(self, ref, wbuf, sems, tap, part):
        rows = self.channels
        dst = wbuf.at[part, pl.ds(tap * rows, rows), :]
        block = (2 * tap + part) % (2 * TAPS // self.shards)
        src = ref.at[pl.ds(block * rows, rows), :]
        return pltpu.make_async_copy(src, dst, sems.at[part, tap])

    def start_weights(self, info, w_refs, wbuf, sems, part):
        for tap in range(TAPS):
            shard = (2 * tap + part) // (2 * TAPS // self.shards)
            for which, ref in enumerate(w_refs):
                owner = lax.rem(info[1] + which, self.shards)

                @pl.when(owner == shard)
                def _():
                    self.weight_copy(ref, wbuf, sems, tap, part).start()

    def wait_weights(self, info, w_refs, wbuf, sems, part, row_tap):
        for tap in range(3 * row_tap, 3 * row_tap + 3):
            self.weight_copy(w_refs[0], wbuf, sems, tap, part).wait()

    def spread(self, value, shift_ref, wide_ref):
        width, pixels, channels = self.width, self.pixels, self.channels
        shift_ref[pl.ds(8, pixels), :] = value.astype(F32)
        for k, offset in enumerate((7, 8, 9)):
            wide_ref[pl.ds(width, pixels), pl.ds(k * channels, channels)] = shift_ref[
                pl.ds(offset, pixels), :
            ].astype(BF)

    def clear(self, shift_ref, wide_ref):
        width, pixels, channels = self.width, self.pixels, self.channels
        shift_ref[pl.ds(0, 8), :] = jnp.zeros((8, channels), F32)
        shift_ref[pl.ds(8 + pixels, 8), :] = jnp.zeros((8, channels), F32)
        wide_ref[pl.ds(0, width), :] = jnp.zeros((width, 3 * channels), BF)
        wide_ref[pl.ds(width + pixels, width), :] = jnp.zeros((width, 3 * channels), BF)

    def product(self, info, w_refs, wbuf, sems, part, wide_ref, wait):
        total = None
        span = 3 * self.channels
        for row_tap in range(3):
            if wait:
                self.wait_weights(info, w_refs, wbuf, sems, part, row_tap)
            term = jnp.dot(
                wide_ref[pl.ds(row_tap * self.width, self.pixels), :],
                wbuf[part, pl.ds(row_tap * span, span), :],
                preferred_element_type=F32,
            )
            total = term if total is None else total + term
        return total

    def update(self, info, gates_ref, bias_ref, memory_ref, hidden_out, memory_out):
        ch = self.channels
        chunk = self.width
        low, high, top, bottom = info[2], info[3], info[4], info[5]

        def body(i, carry):
            rows = pl.ds(pl.multiple_of(i * chunk, chunk), chunk)
            gates = gates_ref[rows, :] + bias_ref[...]
            in_gate = sigmoid(gates[:, :ch])
            candidate = jnp.tanh(gates[:, 2 * ch : 3 * ch])
            memory = in_gate * candidate
            if memory_ref is not None:
                forget = sigmoid(gates[:, ch : 2 * ch])
                memory = memory + forget * memory_ref[rows, :].astype(F32)
            hidden = sigmoid(gates[:, 3 * ch :]) * jnp.tanh(memory)
            column = lax.broadcasted_iota(jnp.int32, hidden.shape, 0)
            inside = (column >= low) & (column < high) & (i >= top) & (i < bottom)
            hidden_out[rows, :] = jnp.where(inside, hidden, 0.0).astype(BF)
            if memory_out is not None:
                memory_out[rows, :] = memory.astype(memory_out.dtype)
            return carry

        lax.fori_loop(0, self.pixels // chunk, body, 0)


def step_call(cfg, turn, info, shards, bias, terms, gates_in=None, memory=None, keep=None, after=None,
              memory_dtype=F32):
    pixels, channels, width = cfg.pixels, cfg.channels, cfg.width
    gate_width = 4 * channels
    arrays = [a for a, _ in terms]
    parts = [p for _, p in terms]
    needed = sorted(set(parts + ([after] if after is not None else [])))
    n_shards, n_terms = len(shards), len(terms)
    has_gates, has_memory = gates_in is not None, memory is not None
    operands = [info, bias] + list(shards) + arrays
    specs = [pl.BlockSpec(memory_space=pltpu.SMEM), pl.BlockSpec(memory_space=pltpu.VMEM)]
    specs += [pl.BlockSpec(memory_space=pl.ANY)] * n_shards
    specs += [pl.BlockSpec(memory_space=pltpu.VMEM)] * n_terms
    if has_gates:
        operands.append(gates_in)
        specs.append(pl.BlockSpec(memory_space=pltpu.VMEM))
    if has_memory:
        operands.append(memory)
        specs.append(pl.BlockSpec(memory_space=pltpu.VMEM))
    outs = [jax.ShapeDtypeStruct((pixels, channels), BF), jax.ShapeDtypeStruct((pixels, channels), memory_dtype)]
    if keep is not None:
        outs.append(jax.ShapeDtypeStruct((pixels, gate_width), F32))
    if after is not None:
        outs.append(jax.ShapeDtypeStruct((pixels, gate_width), F32))

    def kernel(*refs):
        refs = list(refs)
        info_ref, bias_ref = refs.pop(0), refs.pop(0)
        w_refs = [refs.pop(0) for _ in range(n_shards)]
        term_refs = [refs.pop(0) for _ in range(n_terms)]
        gates_ref = refs.pop(0) if has_gates else None
        memory_ref = refs.pop(0) if has_memory else None
        hidden_out, memory_out = refs.pop(0), refs.pop(0)
        keep_out = refs.pop(0) if keep is not None else None
        after_out = refs.pop(0) if after is not None else None
        wbuf, sems, shift_ref, wide_ref, sum_ref = refs

        @pl.when(info_ref[0] == turn)
        def _():
            for part in needed:
                cfg.start_weights(info_ref, w_refs, wbuf, sems, part)
            cfg.clear(shift_ref, wide_ref)
            total = gates_ref[...] if has_gates else None
            waited = set()
            for n, (ref, part) in enumerate(zip(term_refs, parts)):
                if n == 0 or term_refs[n] is not term_refs[n - 1]:
                    cfg.spread(ref[...], shift_ref, wide_ref)
                term = cfg.product(info_ref, w_refs, wbuf, sems, part, wide_ref, part not in waited)
                waited.add(part)
                total = term if total is None else total + term
                if keep == n:
                    keep_out[...] = total
            sum_ref[...] = total
            cfg.update(info_ref, sum_ref, bias_ref, memory_ref, hidden_out, memory_out)
            if after is not None:
                cfg.spread(hidden_out[...], shift_ref, wide_ref)
                after_out[...] = cfg.product(
                    info_ref, w_refs, wbuf, sems, after, wide_ref, after not in waited
                )

    products = n_terms + (after is not None)
    flops = 2 * pixels * TAPS * channels * gate_width * products
    return pl.pallas_call(
        kernel,
        out_shape=outs,
        in_specs=specs,
        out_specs=[pl.BlockSpec(memory_space=pltpu.VMEM)] * len(outs),
        scratch_shapes=[
            pltpu.VMEM((2, TAPS * channels, gate_width), BF),
            pltpu.SemaphoreType.DMA((2, TAPS)),
            pltpu.VMEM((pixels + 16, channels), F32),
            pltpu.VMEM((pixels + 2 * width, 3 * channels), BF),
            pltpu.VMEM((pixels, gate_width), F32),
        ],
        cost_estimate=pl.CostEstimate(
            flops=flops, bytes_accessed=len(needed) * TAPS * channels * gate_width * 2, transcendentals=0
        ),
        compiler_params=pltpu.CompilerParams(vmem_limit_bytes=40 * 1024 * 1024),
        name=f"step{turn}",
    )(*operands)


def local(features, gate_weight, gate_bias):
    batch, frames, tile_rows, tile_cols, channels = features.shape
    section, row, col = (lax.axis_index(a) for a in ("section", "row", "col"))
    row_size, col_size = lax.axis_size("row"), lax.axis_size("col")
    groups = row_size // batch
    place, group = row % batch, row // batch

    own_weight = gate_weight[0]
    if own_weight.shape[0] % channels == 0 and row_size == 2:
        shards = [own_weight, moved(own_weight, "row", [(0, 1), (1, 0)])]
    else:
        shards = [lax.all_gather(own_weight, "row", axis=0, tiled=True)]

    window = gather_sequence(features)
    if groups > 1:
        window = with_halo(window, "row", 1, batch)
    window = with_halo(window, "col", 2, 1)
    height, width = window.shape[1:3]
    pixels = height * width
    window = window.reshape(frames, pixels, channels)

    row_halo = HALO if groups > 1 else 0
    info = jnp.stack(
        [
            section,
            row % len(shards),
            jnp.where(col == 0, HALO, 0),
            jnp.where(col == col_size - 1, width - HALO, width),
            jnp.where(group == 0, row_halo, 0),
            jnp.where(group == groups - 1, height - row_halo, height),
        ]
    ).astype(jnp.int32)

    cfg = Step(width, pixels, channels, len(shards))
    call = functools.partial(step_call, cfg)

    h00, c00 = call(0, info, shards, gate_bias, [(window[0], 0)])
    x10 = section_send(h00, 0, 1)
    h01, c01 = call(0, info, shards, gate_bias, [(window[1], 0), (h00, 1)], memory=c00, memory_dtype=BF)
    x11 = section_send(h01, 0, 1)
    h10, c10, p11 = call(1, info, shards, gate_bias, [(x10, 0)], after=1)
    start3_h = section_send(h01, 0, 3)
    start3_c = section_send(c01, 0, 3)
    h11, c11 = call(1, info, shards, gate_bias, [(x11, 0)], gates_in=p11, memory=c10, memory_dtype=BF)
    x2 = section_send(h11, 1, 2)
    m2 = section_send(c11, 1, 2)
    h20, c20, p21 = call(2, info, shards, gate_bias, [(x2, 0), (x2, 1)], memory=m2, keep=0)
    x30 = section_send(h20, 2, 3)
    h21, _ = call(2, info, shards, gate_bias, [(h20, 1)], gates_in=p21, memory=c20)
    x31 = section_send(h21, 2, 3)
    h30, c30, p31 = call(3, info, shards, gate_bias, [(start3_h, 1), (x30, 0)], memory=start3_c, after=1)
    h31, _ = call(3, info, shards, gate_bias, [(x31, 0)], gates_in=p31, memory=c30)

    def pick(*options):
        return lax.select_n(section, *options)

    result = []
    for options in ((h00, h10, h20, h30), (h01, h11, h21, h31)):
        whole = pick(*options).reshape(height, width, channels)
        inner = whole[row_halo : height - row_halo, HALO : HALO + tile_cols]
        inner = inner.reshape(batch, tile_rows, tile_cols, channels)
        parts = [lax.dynamic_index_in_dim(inner, place, 0, keepdims=False)]
        for k in range(1, batch):
            pairs = [(i, i - i % batch + (i % batch + k) % batch) for i in range(row_size)]
            sent = lax.dynamic_index_in_dim(inner, (place + k) % batch, 0, keepdims=False)
            parts.append(moved(sent, "row", pairs))
        stacked = jnp.stack(parts)
        result.append(
            jnp.stack(
                [
                    lax.dynamic_index_in_dim(stacked, (place - q) % batch, 0, keepdims=False)
                    for q in range(batch)
                ]
            )
        )
    return jnp.stack(result, 1)[None]


def solution(mesh):
    return jax.shard_map(
        local,
        mesh=mesh,
        in_specs=(P(None, None, "row", "col", None), P("section", "row", None), P("section", None)),
        out_specs=P("section", None, None, "row", "col", None),
        check_vma=False,
    )
```

```python
import jax
import jax.numpy as jnp
from jax import lax
from jax.experimental import pallas as pl
from jax.experimental.pallas import tpu as pltpu
from jax.sharding import PartitionSpec as P

HALO = 8
TAPS = 9
BF = jnp.bfloat16
F32 = jnp.float32
VMEM = pl.BlockSpec(memory_space=pltpu.VMEM)
SMEM = pl.BlockSpec(memory_space=pltpu.SMEM)
HBM = pl.BlockSpec(memory_space=pltpu.HBM)
LIMIT = 12 * 1024 * 1024


def section_send(block, source, target):
    return lax.ppermute(block, "section", [(source, target)])


def group_pairs(size, batch, k):
    return [(i, i - i % batch + (i % batch + k) % batch) for i in range(size)]


def gather_sequence(features):
    batch = features.shape[0]
    size = lax.axis_size("row")
    place = lax.axis_index("row") % batch
    parts = [lax.dynamic_index_in_dim(features, place, 0, keepdims=False)]
    for k in range(1, batch):
        sent = lax.dynamic_index_in_dim(features, (place + k) % batch, 0, keepdims=False)
        parts.append(lax.ppermute(sent, "row", group_pairs(size, batch, k)))
    stacked = jnp.stack(parts)
    blocks = [
        lax.dynamic_index_in_dim(stacked, (place - q) % batch, 0, keepdims=False)
        for q in range(batch)
    ]
    return jnp.concatenate(blocks, axis=1)


def with_halo(array, axis, dim, stride):
    size, length = lax.axis_size(axis), array.shape[dim]
    up = [(i, i + stride) for i in range(size - stride)]
    down = [(j, i) for i, j in up]
    last = lax.slice_in_dim(array, length - HALO, length, axis=dim)
    first = lax.slice_in_dim(array, 0, HALO, axis=dim)
    before = lax.ppermute(last, axis, up)
    after = lax.ppermute(first, axis, down)
    return jnp.concatenate([before, array, after], axis=dim)


def paired_pieces(features):
    tile_cols = features.shape[3]
    row, cols = lax.axis_index("row"), lax.axis_size("col")
    partner = lax.ppermute(features, "row", [(0, 1), (1, 0)])
    edge = lax.dynamic_slice_in_dim(
        jnp.stack([features, partner]), jnp.where(row == 0, tile_cols - HALO, 0), HALO, axis=4
    )
    pairs = [(c, c + 1) for c in range(cols - 1)]
    pairs += [(cols + c + 1, cols + c) for c in range(cols - 1)]
    side = lax.ppermute(edge, ("row", "col"), pairs)
    other = lax.ppermute(side, "row", [(0, 1), (1, 0)])
    return [features, partner, side, other]


def sigmoid(x):
    return 0.5 * jnp.tanh(0.5 * x) + 0.5


class Plan:
    def __init__(self, height, width, channels, batch, tile_rows, tile_cols, row_halo):
        self.width, self.pixels, self.channels = width, height * width, channels
        self.batch, self.tile_rows, self.tile_cols, self.row_halo = (
            batch, tile_rows, tile_cols, row_halo,
        )

    def scratch(self):
        return [
            pltpu.VMEM((self.pixels + 16, self.channels), F32),
            pltpu.VMEM((self.pixels + 2 * self.width, 3 * self.channels), BF),
            pltpu.VMEM((self.pixels, 4 * self.channels), F32),
            pltpu.VMEM((self.pixels, self.channels), BF),
        ]

    def load(self, ref, frame, info, shift_ref):
        if not isinstance(ref, list):
            value = ref[...] if frame is None else ref[frame]
            shift_ref[pl.ds(8, self.pixels), :] = value.astype(F32)
            return
        own, partner, side, other = ref
        rows, width, place = self.tile_rows, self.width, info[1]
        for i in range(rows):
            for which, tile in enumerate((own, partner)):
                block = place if which == 0 else 1 - place
                start = pl.multiple_of((block * rows + i) * width, 8) + 8
                shift_ref[pl.ds(start + HALO, self.tile_cols), :] = tile[place, frame, i].astype(F32)
        first = place == 0
        for k in range(2):
            for i in range(rows):
                a = side[k, place, frame, i].astype(F32)
                b = other[k, place, frame, i].astype(F32)
                start = 8 + (k * rows + i) * width
                shift_ref[pl.ds(start, HALO), :] = jnp.where(first, a, b)
                start = 8 + ((1 - k) * rows + i) * width + HALO + self.tile_cols
                shift_ref[pl.ds(start, HALO), :] = jnp.where(first, b, a)

    def spread(self, shift_ref, wide_ref):
        width, pixels, channels = self.width, self.pixels, self.channels
        shift_ref[pl.ds(0, 8), :] = jnp.zeros((8, channels), F32)
        shift_ref[pl.ds(8 + pixels, 8), :] = jnp.zeros((8, channels), F32)
        wide_ref[pl.ds(0, width), :] = jnp.zeros((width, 3 * channels), BF)
        wide_ref[pl.ds(width + pixels, width), :] = jnp.zeros((width, 3 * channels), BF)
        for k, offset in enumerate((7, 8, 9)):
            wide_ref[pl.ds(width, pixels), pl.ds(k * channels, channels)] = shift_ref[
                pl.ds(offset, pixels), :
            ].astype(BF)

    def product(self, weight_ref, part, wide_ref):
        total = None
        span = 3 * self.channels
        for row_tap in range(3):
            term = jnp.dot(
                wide_ref[pl.ds(row_tap * self.width, self.pixels), :],
                weight_ref[part, pl.ds(row_tap * span, span), :],
                preferred_element_type=F32,
            )
            total = term if total is None else total + term
        return total

    def update(self, info, gates_ref, bias_ref, memory_ref, hidden_out, memory_out):
        ch, chunk = self.channels, self.width
        low, high, top, bottom = info[2], info[3], info[4], info[5]

        def body(i, carry):
            rows = pl.ds(pl.multiple_of(i * chunk, chunk), chunk)
            gates = gates_ref[rows, :] + bias_ref[...]
            memory = sigmoid(gates[:, :ch]) * jnp.tanh(gates[:, 2 * ch : 3 * ch])
            if memory_ref is not None:
                memory = memory + sigmoid(gates[:, ch : 2 * ch]) * memory_ref[rows, :].astype(F32)
            hidden = sigmoid(gates[:, 3 * ch :]) * jnp.tanh(memory)
            column = lax.broadcasted_iota(jnp.int32, hidden.shape, 0)
            inside = (column >= low) & (column < high) & (i >= top) & (i < bottom)
            hidden_out[rows, :] = jnp.where(inside, hidden, 0.0).astype(BF)
            if memory_out is not None:
                memory_out[rows, :] = memory.astype(memory_out.dtype)
            return carry

        lax.fori_loop(0, self.pixels // chunk, body, 0)

    def tiles(self, info, hidden_ref, outs):
        for k, out in enumerate(outs):
            block = lax.rem(info[1] + k, self.batch)
            for i in range(self.tile_rows):
                start = (self.row_halo + block * self.tile_rows + i) * self.width
                start = pl.multiple_of(start, self.width)
                out[i] = hidden_ref[pl.ds(start, self.width), :][HALO : HALO + self.tile_cols]

    def step(self, turn, info, weight, bias, terms, gates_in=None, memory=None, keep=None, after=None,
             memory_out=F32, done=None):
        pixels, channels = self.pixels, self.channels
        operands = [info, weight, bias]
        specs = [SMEM, VMEM, VMEM]
        seen = {}

        def place_of(array):
            if isinstance(array, list):
                return [place_of(a) for a in array]
            if id(array) not in seen:
                seen[id(array)] = len(operands)
                operands.append(array)
                specs.append(VMEM)
            return seen[id(array)]

        term_at = [place_of(a) for a, _, _ in terms]
        gates_at = place_of(gates_in) if gates_in is not None else None
        memory_at = place_of(memory) if memory is not None else None
        done_at = [place_of(d) for d in done] if done is not None else None
        outs, names = [], []

        def add(name, shape, dtype):
            outs.append(jax.ShapeDtypeStruct(shape, dtype))
            names.append(name)

        if done is None:
            add("hidden", (pixels, channels), BF)
        else:
            for k in range(self.batch):
                add(f"tile{k}", (self.tile_rows, self.tile_cols, channels), BF)
        if memory_out is not None:
            add("memory", (pixels, channels), memory_out)
        if keep is not None:
            add("keep", (pixels, 4 * channels), F32)
        if after is not None:
            add("after", (pixels, 4 * channels), F32)
        count = len(operands)

        def kernel(*refs):
            ins, out = refs[:count], dict(zip(names, refs[count : count + len(outs)]))
            shift_ref, wide_ref, sum_ref, hidden_ref = refs[count + len(outs) :]
            info_ref, weight_ref, bias_ref = ins[:3]

            def ref_of(at):
                return [ref_of(a) for a in at] if isinstance(at, list) else ins[at]

            @pl.when(info_ref[0] == turn)
            def _():
                total = ins[gates_at][...] if gates_at is not None else None
                last = None
                for n, ((_, frame, part), at) in enumerate(zip(terms, term_at)):
                    if (at, frame) != last:
                        self.load(ref_of(at), frame, info_ref, shift_ref)
                        self.spread(shift_ref, wide_ref)
                    last = (at, frame)
                    term = self.product(weight_ref, part, wide_ref)
                    total = term if total is None else total + term
                    if keep == n + 1:
                        out["keep"][...] = total
                sum_ref[...] = total
                hidden_to = out.get("hidden", hidden_ref)
                memory_ref = ins[memory_at] if memory_at is not None else None
                self.update(info_ref, sum_ref, bias_ref, memory_ref, hidden_to, out.get("memory"))
                if after is not None:
                    self.load(hidden_to, None, info_ref, shift_ref)
                    self.spread(shift_ref, wide_ref)
                    out["after"][...] = self.product(weight_ref, after, wide_ref)
                if done is not None:
                    self.tiles(info_ref, hidden_to, [out[f"tile{k}"] for k in range(self.batch)])

            if done is not None:
                for index, at in enumerate(done_at):

                    @pl.when(info_ref[0] == index)
                    def _():
                        self.tiles(info_ref, ins[at], [out[f"tile{k}"] for k in range(self.batch)])

        products = len(terms) + (after is not None)
        return pl.pallas_call(
            kernel,
            out_shape=outs,
            in_specs=specs,
            out_specs=[VMEM] * len(outs),
            scratch_shapes=self.scratch(),
            cost_estimate=pl.CostEstimate(
                flops=8 * pixels * TAPS * channels * channels * products,
                bytes_accessed=weight.size, transcendentals=0,
            ),
            compiler_params=pltpu.CompilerParams(vmem_limit_bytes=LIMIT),
            name=f"step{turn}",
        )(*operands)

    def partial(self, turn, info, weight, array, part):
        def kernel(info_ref, weight_ref, in_ref, out_ref, shift_ref, wide_ref, sum_ref, hidden_ref):
            @pl.when(info_ref[0] == turn)
            def _():
                self.load(in_ref, None, info_ref, shift_ref)
                self.spread(shift_ref, wide_ref)
                out_ref[...] = self.product(weight_ref, part, wide_ref)

        return pl.pallas_call(
            kernel,
            out_shape=jax.ShapeDtypeStruct((self.pixels, 4 * self.channels), F32),
            in_specs=[SMEM, VMEM, VMEM],
            out_specs=VMEM,
            scratch_shapes=self.scratch(),
            cost_estimate=pl.CostEstimate(
                flops=8 * self.pixels * TAPS * self.channels**2,
                bytes_accessed=weight.size, transcendentals=0,
            ),
            compiler_params=pltpu.CompilerParams(vmem_limit_bytes=LIMIT),
            name=f"part{turn}",
        )(info, weight, array)


def joined_weight(info, shards, channels):
    per = 2 * TAPS // len(shards)

    def kernel(info_ref, *refs):
        sources, out_ref, sems = refs[: len(shards)], refs[len(shards)], refs[len(shards) + 1]

        def copy(ref, block):
            src = ref.at[pl.ds(block % per * channels, channels), :]
            dst = out_ref.at[block % 2, pl.ds(block // 2 * channels, channels), :]
            return pltpu.make_async_copy(src, dst, sems.at[block])

        for which, ref in enumerate(sources):
            owner = lax.rem(info_ref[1] + which, len(shards))
            for shard in range(len(shards)):

                @pl.when(owner == shard)
                def _():
                    for block in range(shard * per, shard * per + per):
                        copy(ref, block).start()

        for block in range(2 * TAPS):
            copy(sources[0], block).wait()

    rows, columns = shards[0].shape[0] * len(shards) // 2, shards[0].shape[1]
    return pl.pallas_call(
        kernel,
        out_shape=jax.ShapeDtypeStruct((2, rows, columns), BF),
        in_specs=[SMEM] + [HBM] * len(shards),
        out_specs=VMEM,
        scratch_shapes=[pltpu.SemaphoreType.DMA((2 * TAPS,))],
        compiler_params=pltpu.CompilerParams(vmem_limit_bytes=LIMIT),
        name="join",
    )(info, *shards)


def local(features, gate_weight, gate_bias):
    batch, frames, tile_rows, tile_cols, channels = features.shape
    section, row, col = (lax.axis_index(a) for a in ("section", "row", "col"))
    row_size, col_size = lax.axis_size("row"), lax.axis_size("col")
    groups = row_size // batch
    place, group = row % batch, row // batch
    row_halo = HALO if groups > 1 else 0
    height, width = tile_rows * batch + 2 * row_halo, tile_cols + 2 * HALO

    if groups == 1 and batch == 2:
        pieces = paired_pieces(features)
    else:
        window = gather_sequence(features)
        if groups > 1:
            window = with_halo(window, "row", 1, batch)
        pieces = with_halo(window, "col", 2, 1).reshape(frames, height * width, channels)

    own_weight = gate_weight[0]
    if row_size == 2 and own_weight.shape[0] % channels == 0:
        shards = [own_weight, lax.ppermute(own_weight, "row", [(0, 1), (1, 0)])]
    else:
        shards = [lax.all_gather(own_weight, "row", axis=0, tiled=True)]

    info = jnp.stack(
        [
            section,
            place,
            jnp.where(col == 0, HALO, 0),
            jnp.where(col == col_size - 1, width - HALO, width),
            jnp.where(group == 0, row_halo, 0),
            jnp.where(group == groups - 1, height - row_halo, height),
        ]
    ).astype(jnp.int32)
    weight = joined_weight(info, shards, channels)
    plan = Plan(height, width, channels, batch, tile_rows, tile_cols, row_halo)

    def step(turn, *args, **kwargs):
        return plan.step(turn, info, weight, gate_bias, *args, **kwargs)

    h00, c00 = step(0, [(pieces, 0, 0)])
    x10 = section_send(h00, 0, 1)
    h01, c01 = step(0, [(pieces, 1, 0), (h00, None, 1)], memory=c00, memory_out=BF)
    x11 = section_send(h01, 0, 1)
    h10, c10, p11 = step(1, [(x10, None, 0)], after=1)
    start3_h = section_send(h01, 0, 3)
    start3_c = section_send(c01, 0, 3)
    h11, c11 = step(1, [(x11, None, 0)], gates_in=p11, memory=c10, memory_out=BF)
    x2 = section_send(h11, 1, 2)
    m2 = section_send(c11, 1, 2)
    p30 = plan.partial(3, info, weight, start3_h, 1)
    h20, c20, p21 = step(2, [(x2, None, 0), (x2, None, 1)], memory=m2, keep=1)
    x30 = section_send(h20, 2, 3)
    (h21,) = step(2, [(h20, None, 1)], gates_in=p21, memory=c20, memory_out=None)
    x31 = section_send(h21, 2, 3)
    *first, c30, p31 = step(
        3, [(x30, None, 0)], gates_in=p30, memory=start3_c, after=1, done=(h00, h10, h20)
    )
    second = step(
        3, [(x31, None, 0)], gates_in=p31, memory=c30, memory_out=None, done=(h01, h11, h21)
    )

    result = []
    for tiles in (first, second):
        parts = [tiles[0]]
        for k in range(1, batch):
            parts.append(lax.ppermute(tiles[k], "row", group_pairs(row_size, batch, k)))
        stacked = jnp.stack(parts)
        order = [
            lax.dynamic_index_in_dim(stacked, (place - q) % batch, 0, keepdims=False)
            for q in range(batch)
        ]
        result.append(jnp.stack(order))
    return jnp.stack(result, 1)[None]


def solution(mesh):
    return jax.shard_map(
        local,
        mesh=mesh,
        in_specs=(P(None, None, "row", "col", None), P("section", "row", None), P("section", None)),
        out_specs=P("section", None, None, "row", "col", None),
        check_vma=False,
    )
```

```python
import jax
import jax.numpy as jnp
from jax import lax
from jax.experimental import pallas as pl
from jax.experimental.pallas import tpu as pltpu
from jax.sharding import PartitionSpec as P


HALO = 8
TAPS = 9
BF = jnp.bfloat16
F32 = jnp.float32
VMEM = pl.BlockSpec(memory_space=pltpu.VMEM)
SMEM = pl.BlockSpec(memory_space=pltpu.SMEM)
HBM = pl.BlockSpec(memory_space=pltpu.HBM)
LIMIT = 12 * 1024 * 1024
INNER = 4


def section_send(block, source, target):
    return lax.ppermute(block, "section", [(source, target)])


def group_pairs(size, batch, k):
    return [(i, i - i % batch + (i % batch + k) % batch) for i in range(size)]


def gather_sequence(features):
    batch = features.shape[0]
    size = lax.axis_size("row")
    place = lax.axis_index("row") % batch
    parts = [lax.dynamic_index_in_dim(features, place, 0, keepdims=False)]
    for k in range(1, batch):
        sent = lax.dynamic_index_in_dim(features, (place + k) % batch, 0, keepdims=False)
        parts.append(lax.ppermute(sent, "row", group_pairs(size, batch, k)))
    stacked = jnp.stack(parts)
    blocks = [
        lax.dynamic_index_in_dim(stacked, (place - q) % batch, 0, keepdims=False)
        for q in range(batch)
    ]
    return jnp.concatenate(blocks, axis=1)


def with_halo(array, axis, dim, stride):
    size, length = lax.axis_size(axis), array.shape[dim]
    up = [(i, i + stride) for i in range(size - stride)]
    down = [(j, i) for i, j in up]
    last = lax.slice_in_dim(array, length - HALO, length, axis=dim)
    first = lax.slice_in_dim(array, 0, HALO, axis=dim)
    before = lax.ppermute(last, axis, up)
    after = lax.ppermute(first, axis, down)
    return jnp.concatenate([before, array, after], axis=dim)


def paired_pieces(features):
    tile_cols = features.shape[3]
    row, cols = lax.axis_index("row"), lax.axis_size("col")
    partner = lax.ppermute(features, "row", [(0, 1), (1, 0)])
    edge = lax.dynamic_slice_in_dim(
        jnp.stack([features, partner]), jnp.where(row == 0, tile_cols - HALO, 0), HALO, axis=4
    )
    pairs = [(c, c + 1) for c in range(cols - 1)]
    pairs += [(cols + c + 1, cols + c) for c in range(cols - 1)]
    side = lax.ppermute(edge, ("row", "col"), pairs)
    other = lax.ppermute(side, "row", [(0, 1), (1, 0)])
    return [features, partner, side, other]


def sigmoid(x):
    return 0.5 * jnp.tanh(0.5 * x) + 0.5


class Plan:
    def __init__(self, info, weight, bias, height, channels, batch, tile_rows, tile_cols, row_halo):
        self.info, self.weight, self.bias = info, weight, bias
        self.height, self.channels, self.batch = height, channels, batch
        self.tile_rows, self.tile_cols, self.row_halo = tile_rows, tile_cols, row_halo

    def load(self, ref, frame, info, stage_ref, width):
        base, channels = width + 8, self.channels
        pixels = self.height * width
        stage_ref[pl.ds(0, base), :] = jnp.zeros((base, channels), F32)
        stage_ref[pl.ds(base + pixels, base), :] = jnp.zeros((base, channels), F32)
        if not isinstance(ref, list):
            value = ref[...] if frame is None else ref[frame]
            stage_ref[pl.ds(base, pixels), :] = value.astype(F32)
            return
        own, partner, side, other = ref
        rows, place = self.tile_rows, info[1]
        for i in range(rows):
            for which, tile in enumerate((own, partner)):
                block = place if which == 0 else 1 - place
                start = pl.multiple_of((block * rows + i) * width, 8) + base + HALO
                stage_ref[pl.ds(start, self.tile_cols), :] = tile[place, frame, i].astype(F32)
        first = place == 0
        for k in range(2):
            for i in range(rows):
                a = side[k, place, frame, i].astype(F32)
                b = other[k, place, frame, i].astype(F32)
                start = base + (k * rows + i) * width
                stage_ref[pl.ds(start, HALO), :] = jnp.where(first, a, b)
                start = base + ((1 - k) * rows + i) * width + HALO + self.tile_cols
                stage_ref[pl.ds(start, HALO), :] = jnp.where(first, b, a)

    def spread(self, stage_ref, patch_ref, width, out_width):
        base, channels = width + 8, self.channels
        inset = (width - out_width) // 2
        for tap in range(TAPS):
            start = base + (tap // 3 - 1) * width + tap % 3 - 1
            if inset == 0:
                value = stage_ref[pl.ds(start, self.height * width), :]
            else:
                value = jnp.concatenate(
                    [
                        stage_ref[pl.ds(start + inset + i * width, out_width), :]
                        for i in range(self.height)
                    ]
                )
            patch_ref[:, pl.ds(tap * channels, channels)] = value.astype(BF)

    def update(self, info, gates_refs, bias_ref, memory_ref, width, halo, hidden_out, memory_out):
        ch = self.channels
        low = jnp.where(info[2] == 0, halo, 0)
        high = jnp.where(info[3] == 0, width - halo, width)
        top, bottom = info[4], info[5]
        memory_width = memory_ref.shape[0] // self.height if memory_ref is not None else width
        for i in range(self.height):
            rows = pl.ds(i * width, width)
            gates = bias_ref[...]
            for ref in gates_refs:
                gates = gates + ref[rows, :]
            memory = sigmoid(gates[:, :ch]) * jnp.tanh(gates[:, 2 * ch : 3 * ch])
            if memory_ref is not None:
                before = memory_ref[pl.ds(i * memory_width + (memory_width - width) // 2, width), :]
                memory = memory + sigmoid(gates[:, ch : 2 * ch]) * before.astype(F32)
            hidden = sigmoid(gates[:, 3 * ch :]) * jnp.tanh(memory)
            column = lax.broadcasted_iota(jnp.int32, hidden.shape, 0)
            inside = (column >= low) & (column < high)
            if self.row_halo:
                inside = inside & (i >= top) & (i < bottom)
            hidden = jnp.where(inside, hidden, 0.0)
            for out in hidden_out:
                out[rows, :] = hidden.astype(out.dtype)
            for out in memory_out:
                out[rows, :] = memory.astype(out.dtype)

    def tiles(self, info, hidden_ref, width, outs):
        halo = (width - self.tile_cols) // 2
        for k, out in enumerate(outs):
            block = lax.rem(info[1] + k, self.batch)
            for i in range(self.tile_rows):
                start = (self.row_halo + block * self.tile_rows + i) * width
                start = pl.multiple_of(start, 8)
                row = hidden_ref[pl.ds(start, width), :].astype(F32)
                out[i] = row[halo : halo + self.tile_cols].astype(BF)

    def step(self, turn, terms, width, gates_in=None, memory=None, keep=None, after=None,
             outs=(), done=None):
        channels, batch = self.channels, self.batch
        pixels = self.height * width
        halo = (width - self.tile_cols) // 2
        operands = [self.info, self.weight, self.bias]
        specs = [SMEM, VMEM, VMEM]
        seen = {}

        def place_of(array):
            if isinstance(array, list):
                return [place_of(a) for a in array]
            if id(array) not in seen:
                seen[id(array)] = len(operands)
                operands.append(array)
                specs.append(VMEM)
            return seen[id(array)]

        term_at = [place_of(t[0]) for t in terms]
        gates_at = place_of(gates_in) if gates_in is not None else None
        memory_at = place_of(memory[0]) if memory is not None else None
        done_at = [place_of(d[0]) for d in done] if done is not None else None
        shapes, names = [], []

        def add(name, shape, dtype):
            shapes.append(jax.ShapeDtypeStruct(shape, dtype))
            names.append(name)

        for name in outs:
            if name == "hidden":
                add(name, (pixels, channels), BF)
            elif name == "both":
                add(name, (2, pixels, channels), BF)
            elif name == "memory":
                add(name, (pixels, channels), F32)
            elif name == "tiles":
                for k in range(batch):
                    add(f"tile{k}", (self.tile_rows, self.tile_cols, channels), BF)
        if keep is not None:
            add("keep", (pixels, 4 * channels), F32)
        if after is not None:
            add("after", (pixels, 4 * channels), F32)
        count = len(operands)
        widest = max([t[2] for t in terms] + [width])

        def kernel(*refs):
            ins, out = refs[:count], dict(zip(names, refs[count : count + len(shapes)]))
            stage_ref, patch_ref, sum_ref, hidden_ref = refs[count + len(shapes) :]
            info_ref, weight_ref, bias_ref = ins[:3]
            tile_refs = [out[f"tile{k}"] for k in range(batch)] if "tiles" in outs else []

            def ref_of(at):
                return [ref_of(a) for a in at] if isinstance(at, list) else ins[at]

            @pl.when(info_ref[0] == turn)
            def _():
                total, last = None, None
                for n, ((_, index, span, part), at) in enumerate(zip(terms, term_at)):
                    if (at, index) != last:
                        self.load(ref_of(at), index, info_ref, stage_ref, span)
                        self.spread(stage_ref, patch_ref, span, width)
                    last = (at, index)
                    term = jnp.dot(patch_ref[...], weight_ref[part], preferred_element_type=F32)
                    total = term if total is None else total + term
                    if keep == n + 1:
                        out["keep"][...] = total
                sum_ref[...] = total
                gates_refs = [sum_ref] + ([ins[gates_at]] if gates_at is not None else [])
                memory_ref = None
                if memory is not None:
                    memory_ref = ins[memory_at]
                    if memory[1] is not None:
                        memory_ref = memory_ref.at[memory[1]]
                hidden_to, memory_to = [], []
                if after is not None or done is not None:
                    hidden_to.append(hidden_ref)
                if "hidden" in outs:
                    hidden_to.append(out["hidden"])
                if "both" in outs:
                    hidden_to.append(out["both"].at[0])
                    memory_to.append(out["both"].at[1])
                if "memory" in outs:
                    memory_to.append(out["memory"])
                self.update(
                    info_ref, gates_refs, bias_ref, memory_ref, width, halo, hidden_to, memory_to
                )
                if after is not None:
                    self.load(hidden_ref, None, info_ref, stage_ref, width)
                    self.spread(stage_ref, patch_ref, width, width)
                    out["after"][...] = jnp.dot(
                        patch_ref[...], weight_ref[after], preferred_element_type=F32
                    )
                if done is not None:
                    self.tiles(info_ref, hidden_ref, width, tile_refs)

            if done is not None:
                for section, (at, (_, index, span)) in enumerate(zip(done_at, done)):

                    @pl.when(info_ref[0] == section)
                    def _():
                        source = ins[at] if index is None else ins[at].at[index]
                        self.tiles(info_ref, source, span, tile_refs)

        return pl.pallas_call(
            kernel,
            out_shape=shapes,
            in_specs=specs,
            out_specs=[VMEM] * len(shapes),
            scratch_shapes=[
                pltpu.VMEM(((self.height + 2) * widest + 16, channels), F32),
                pltpu.VMEM((pixels, TAPS * channels), BF),
                pltpu.VMEM((pixels, 4 * channels), F32),
                pltpu.VMEM((pixels, channels), F32),
            ],
            cost_estimate=self.cost(pixels, len(terms) + (after is not None)),
            compiler_params=pltpu.CompilerParams(vmem_limit_bytes=LIMIT),
        )(*operands)

    def cost(self, pixels, products):
        return pl.CostEstimate(
            flops=8 * pixels * TAPS * self.channels * self.channels * products,
            bytes_accessed=pixels * self.channels * 2, transcendentals=0,
        )

    def partial(self, turn, array, index, width, part):
        pixels, channels = self.height * width, self.channels

        def kernel(info_ref, weight_ref, in_ref, out_ref, stage_ref, patch_ref):
            @pl.when(info_ref[0] == turn)
            def _():
                self.load(in_ref, index, info_ref, stage_ref, width)
                self.spread(stage_ref, patch_ref, width, width)
                out_ref[...] = jnp.dot(
                    patch_ref[...], weight_ref[part], preferred_element_type=F32
                )

        return pl.pallas_call(
            kernel,
            out_shape=jax.ShapeDtypeStruct((pixels, 4 * channels), F32),
            in_specs=[SMEM, VMEM, VMEM],
            out_specs=VMEM,
            scratch_shapes=[
                pltpu.VMEM(((self.height + 2) * width + 16, channels), F32),
                pltpu.VMEM((pixels, TAPS * channels), BF),
            ],
            cost_estimate=self.cost(pixels, 1),
            compiler_params=pltpu.CompilerParams(vmem_limit_bytes=LIMIT),
        )(self.info, self.weight, array)


def joined_weight(info, shards, channels):
    per = 2 * TAPS // len(shards)

    def kernel(info_ref, *refs):
        sources, out_ref, sems = refs[: len(shards)], refs[len(shards)], refs[len(shards) + 1]

        def copy(ref, block):
            src = ref.at[pl.ds(block % per * channels, channels), :]
            dst = out_ref.at[block % 2, pl.ds(block // 2 * channels, channels), :]
            return pltpu.make_async_copy(src, dst, sems.at[block])

        for which, ref in enumerate(sources):
            owner = lax.rem(info_ref[1] + which, len(shards))
            for shard in range(len(shards)):

                @pl.when(owner == shard)
                def _():
                    for block in range(shard * per, shard * per + per):
                        copy(ref, block).start()

        for block in range(2 * TAPS):
            copy(sources[0], block).wait()

    rows, columns = shards[0].shape[0] * len(shards) // 2, shards[0].shape[1]
    return pl.pallas_call(
        kernel,
        out_shape=pltpu.VMEM((2, rows, columns), BF),
        in_specs=[SMEM, HBM] + [pl.BlockSpec(memory_space=pl.ANY)] * (len(shards) - 1),
        out_specs=VMEM,
        scratch_shapes=[pltpu.SemaphoreType.DMA((2 * TAPS,))],
        compiler_params=pltpu.CompilerParams(vmem_limit_bytes=LIMIT),
        name="join",
    )(info, pltpu.with_memory_space_constraint(shards[0], pltpu.HBM), *shards[1:])


def window_levels(features, gate_weight, gate_bias):
    batch, frames, tile_rows, tile_cols, channels = features.shape
    section, row, col = (lax.axis_index(a) for a in ("section", "row", "col"))
    row_size, col_size = lax.axis_size("row"), lax.axis_size("col")
    groups = row_size // batch
    place, group = row % batch, row // batch
    row_halo = HALO if groups > 1 else 0
    height = tile_rows * batch + 2 * row_halo
    wide, narrow = tile_cols + 2 * HALO, tile_cols + 2 * INNER

    if groups == 1 and batch == 2:
        pieces = paired_pieces(features)
    else:
        window = gather_sequence(features)
        if groups > 1:
            window = with_halo(window, "row", 1, batch)
        pieces = with_halo(window, "col", 2, 1).reshape(frames, height * wide, channels)

    own_weight = gate_weight[0]
    if row_size == 2 and own_weight.shape[0] % channels == 0:
        shards = [own_weight, lax.ppermute(own_weight, "row", [(0, 1), (1, 0)])]
    else:
        shards = [lax.all_gather(own_weight, "row", axis=0, tiled=True)]

    info = jnp.stack(
        [
            section,
            place,
            col,
            col_size - 1 - col,
            jnp.where(group == 0, row_halo, 0),
            jnp.where(group == groups - 1, height - row_halo, height),
        ]
    ).astype(jnp.int32)
    weight = joined_weight(info, shards, channels)
    plan = Plan(info, weight, gate_bias, height, channels, batch, tile_rows, tile_cols, row_halo)

    h00, c00 = plan.step(0, [(pieces, 0, wide, 0)], wide, outs=("hidden", "memory"))
    x10 = section_send(h00, 0, 1)
    h01, s01 = plan.step(
        0, [(pieces, 1, wide, 0), (h00, None, wide, 1)], narrow, memory=(c00, None),
        outs=("hidden", "both"),
    )
    x11 = section_send(h01, 0, 1)
    h10, c10, p11 = plan.step(1, [(x10, None, wide, 0)], narrow, after=1, outs=("hidden", "memory"))
    start3 = section_send(s01, 0, 3)
    (s11,) = plan.step(1, [(x11, None, narrow, 0)], narrow, gates_in=p11, memory=(c10, None), outs=("both",))
    x2 = section_send(s11, 1, 2)
    p30 = plan.partial(3, start3, 0, narrow, 1)
    h20, c20, p21 = plan.step(
        2, [(x2, 0, narrow, 0), (x2, 0, narrow, 1)], narrow, memory=(x2, 1), keep=1,
        outs=("hidden", "memory"),
    )
    x30 = section_send(h20, 2, 3)
    (h21,) = plan.step(2, [(h20, None, narrow, 1)], narrow, gates_in=p21, memory=(c20, None), outs=("hidden",))
    x31 = section_send(h21, 2, 3)
    c30, *first, p31 = plan.step(
        3, [(x30, None, narrow, 0)], narrow, gates_in=p30, memory=(start3, 1), after=1,
        outs=("memory", "tiles"), done=((h00, None, wide), (h10, None, narrow), (h20, None, narrow)),
    )
    second = plan.step(
        3, [(x31, None, narrow, 0)], narrow, gates_in=p31, memory=(c30, None),
        outs=("tiles",), done=((h01, None, narrow), (s11, 0, narrow), (h21, None, narrow)),
    )

    parts = [[first[0], second[0]]]
    for k in range(1, batch):
        pairs = group_pairs(row_size, batch, k)
        parts.append([lax.ppermute(tiles[k], "row", pairs) for tiles in (first, second)])
    result = []
    for q in range(batch):
        chosen = parts[0]
        for k in range(1, batch):
            chosen = [
                jnp.where((place - q) % batch == k, other, one) for one, other in zip(chosen, parts[k])
            ]
        result += chosen
    return jnp.concatenate([r[None] for r in result]).reshape(
        1, batch, frames, tile_rows, tile_cols, channels
    )


def solution(mesh):
    return jax.shard_map(
        window_levels,
        mesh=mesh,
        in_specs=(P(None, None, "row", "col", None), P("section", "row", None), P("section", None)),
        out_specs=P("section", None, None, "row", "col", None),
        check_vma=False,
    )
```

```python
import jax
import jax.numpy as jnp
from jax import lax
from jax.experimental import pallas as pl
from jax.experimental.pallas import tpu as pltpu
from jax.sharding import PartitionSpec as P


HALO = 8
TAPS = 9
BF = jnp.bfloat16
F32 = jnp.float32
VMEM = pl.BlockSpec(memory_space=pltpu.VMEM)
HBM = pl.BlockSpec(memory_space=pltpu.HBM)
LIMIT = 12 * 1024 * 1024
INNER = 4


def section_send(block, route):
    return lax.ppermute(block, "section", [(route[i], route[(i + 1) % 4]) for i in range(4)])


def section_swap(block, pairs):
    return lax.ppermute(block, "section", [*pairs, *((b, a) for a, b in pairs)])


class Position:
    def __init__(self, batch):
        row = lax.axis_index("row")
        self.section, self.col, self.last_col = (
            lax.axis_index("section"), lax.axis_index("col"), lax.axis_size("col") - 1,
        )
        self.place, self.group = lax.rem(row, batch), lax.div(row, batch)
        self.last_group = lax.axis_size("row") // batch - 1


def group_pairs(size, batch, k):
    return [(i, i - i % batch + (i % batch + k) % batch) for i in range(size)]


def gather_sequence(features):
    batch = features.shape[0]
    size = lax.axis_size("row")
    place = lax.axis_index("row") % batch
    parts = [lax.dynamic_index_in_dim(features, place, 0, keepdims=False)]
    for k in range(1, batch):
        sent = lax.dynamic_index_in_dim(features, (place + k) % batch, 0, keepdims=False)
        parts.append(lax.ppermute(sent, "row", group_pairs(size, batch, k)))
    stacked = jnp.stack(parts)
    blocks = [
        lax.dynamic_index_in_dim(stacked, (place - q) % batch, 0, keepdims=False)
        for q in range(batch)
    ]
    return jnp.concatenate(blocks, axis=1)


def with_halo(array, axis, dim, stride):
    size, length = lax.axis_size(axis), array.shape[dim]
    up = [(i, i + stride) for i in range(size - stride)]
    down = [(j, i) for i, j in up]
    last = lax.slice_in_dim(array, length - HALO, length, axis=dim)
    first = lax.slice_in_dim(array, 0, HALO, axis=dim)
    before = lax.ppermute(last, axis, up)
    after = lax.ppermute(first, axis, down)
    return jnp.concatenate([before, array, after], axis=dim)


def paired_pieces(features):
    tile_cols = features.shape[3]
    row, cols = lax.axis_index("row"), lax.axis_size("col")
    partner = lax.ppermute(features, "row", [(0, 1), (1, 0)])
    edge = lax.dynamic_slice_in_dim(
        jnp.stack([features, partner]), jnp.where(row == 0, tile_cols - HALO, 0), HALO, axis=4
    )
    up = list(range(cols))
    ring = up + [cols + c for c in reversed(up)]
    pairs = [(ring[i], ring[(i + 1) % len(ring)]) for i in range(len(ring))]
    side = lax.ppermute(edge, ("row", "col"), pairs)
    other = lax.ppermute(side, "row", [(0, 1), (1, 0)])
    return [features, partner, side, other]


def sigmoid(x):
    return 0.5 * jnp.tanh(0.5 * x) + 0.5


class Plan:
    def __init__(self, weight, bias, height, channels, batch, tile_rows, tile_cols, row_halo):
        self.weight, self.bias = weight, bias
        self.height, self.channels, self.batch = height, channels, batch
        self.tile_rows, self.tile_cols, self.row_halo = tile_rows, tile_cols, row_halo

    def load(self, ref, frame, info, stage_ref, width):
        base, channels = width + 8, self.channels
        pixels = self.height * width
        stage_ref[pl.ds(0, base), :] = jnp.zeros((base, channels), F32)
        stage_ref[pl.ds(base + pixels, base), :] = jnp.zeros((base, channels), F32)
        if not isinstance(ref, list):
            value = ref[...] if frame is None else ref[frame]
            stage_ref[pl.ds(base, pixels), :] = value.astype(F32)
            return
        own, partner, side, other = ref
        rows, place = self.tile_rows, info.place
        for i in range(rows):
            for which, tile in enumerate((own, partner)):
                block = place if which == 0 else 1 - place
                start = pl.multiple_of((block * rows + i) * width, 8) + base + HALO
                stage_ref[pl.ds(start, self.tile_cols), :] = tile[place, frame, i].astype(F32)
        first = place == 0
        left, right = info.col > 0, info.col < info.last_col
        for k in range(2):
            for i in range(rows):
                a = side[k, place, frame, i].astype(F32)
                b = other[k, place, frame, i].astype(F32)
                start = base + (k * rows + i) * width
                stage_ref[pl.ds(start, HALO), :] = jnp.where(left, jnp.where(first, a, b), 0.0)
                start = base + ((1 - k) * rows + i) * width + HALO + self.tile_cols
                stage_ref[pl.ds(start, HALO), :] = jnp.where(right, jnp.where(first, b, a), 0.0)

    def spread(self, stage_ref, patch_ref, width, out_width):
        base, channels = width + 8, self.channels
        inset = (width - out_width) // 2
        for tap in range(TAPS):
            start = base + (tap // 3 - 1) * width + tap % 3 - 1
            if inset == 0:
                value = stage_ref[pl.ds(start, self.height * width), :]
            else:
                value = jnp.concatenate(
                    [
                        stage_ref[pl.ds(start + inset + i * width, out_width), :]
                        for i in range(self.height)
                    ]
                )
            patch_ref[:, pl.ds(tap * channels, channels)] = value.astype(BF)

    def update(self, info, gates_refs, bias_ref, memory_ref, width, halo, hidden_out, memory_out):
        ch = self.channels
        low = jnp.where(info.col == 0, halo, 0)
        high = jnp.where(info.col == info.last_col, width - halo, width)
        top = jnp.where(info.group == 0, self.row_halo, 0)
        bottom = jnp.where(info.group == info.last_group, self.height - self.row_halo, self.height)
        memory_width = memory_ref.shape[0] // self.height if memory_ref is not None else width
        for i in range(self.height):
            rows = pl.ds(i * width, width)
            gates = bias_ref[...]
            for ref in gates_refs:
                gates = gates + ref[rows, :]
            memory = sigmoid(gates[:, :ch]) * jnp.tanh(gates[:, 2 * ch : 3 * ch])
            if memory_ref is not None:
                before = memory_ref[pl.ds(i * memory_width + (memory_width - width) // 2, width), :]
                memory = memory + sigmoid(gates[:, ch : 2 * ch]) * before.astype(F32)
            hidden = sigmoid(gates[:, 3 * ch :]) * jnp.tanh(memory)
            column = lax.broadcasted_iota(jnp.int32, hidden.shape, 0)
            inside = (column >= low) & (column < high)
            if self.row_halo:
                inside = inside & (i >= top) & (i < bottom)
            hidden = jnp.where(inside, hidden, 0.0)
            for out in hidden_out:
                out[rows, :] = hidden.astype(out.dtype)
            for out in memory_out:
                out[rows, :] = memory.astype(out.dtype)

    def tiles(self, info, hidden_ref, width, outs):
        halo = (width - self.tile_cols) // 2
        for k, out in enumerate(outs):
            block = lax.rem(info.place + k, self.batch)
            for i in range(self.tile_rows):
                start = (self.row_halo + block * self.tile_rows + i) * width
                start = pl.multiple_of(start, 8)
                row = hidden_ref[pl.ds(start, width), :].astype(F32)
                out[i] = row[halo : halo + self.tile_cols].astype(BF)

    def step(self, turn, terms, width, gates_in=None, memory=None, keep=None, after=None,
             outs=(), done=None, relay=None):
        channels, batch = self.channels, self.batch
        pixels = self.height * width
        halo = (width - self.tile_cols) // 2
        operands = [self.weight, self.bias]
        specs = [VMEM, VMEM]
        seen = {}

        def place_of(array):
            if isinstance(array, list):
                return [place_of(a) for a in array]
            if id(array) not in seen:
                seen[id(array)] = len(operands)
                operands.append(array)
                specs.append(VMEM)
            return seen[id(array)]

        term_at = [place_of(t[0]) for t in terms]
        gates_at = place_of(gates_in) if gates_in is not None else None
        memory_at = place_of(memory[0]) if memory is not None else None
        done_at = [place_of(d[0]) for d in done] if done is not None else None
        relay_at = place_of(relay[1]) if relay is not None else None
        shapes, names = [], []

        def add(name, shape, dtype):
            shapes.append(jax.ShapeDtypeStruct(shape, dtype))
            names.append(name)

        for name in outs:
            if name == "hidden":
                add(name, (pixels, channels), BF)
            elif name == "both":
                add(name, (2, pixels, channels), BF)
            elif name == "memory":
                add(name, (pixels, channels), F32)
            elif name == "tiles":
                for k in range(batch):
                    add(f"tile{k}", (self.tile_rows, self.tile_cols, channels), BF)
        if keep is not None:
            add("keep", (pixels, 4 * channels), F32)
        if after is not None:
            add("after", (pixels, 4 * channels), F32)
        count = len(operands)
        widest = max([t[2] for t in terms] + [width])

        def kernel(*refs):
            ins, out = refs[:count], dict(zip(names, refs[count : count + len(shapes)]))
            stage_ref, patch_ref, sum_ref, hidden_ref = refs[count + len(shapes) :]
            weight_ref, bias_ref = ins[:2]
            info = Position(batch)
            tile_refs = [out[f"tile{k}"] for k in range(batch)] if "tiles" in outs else []

            def ref_of(at):
                return [ref_of(a) for a in at] if isinstance(at, list) else ins[at]

            @pl.when(info.section == turn)
            def _():
                total, last = None, None
                for n, ((_, index, span, part), at) in enumerate(zip(terms, term_at)):
                    if (at, index) != last:
                        self.load(ref_of(at), index, info, stage_ref, span)
                        self.spread(stage_ref, patch_ref, span, width)
                    last = (at, index)
                    term = jnp.dot(patch_ref[...], weight_ref[part], preferred_element_type=F32)
                    total = term if total is None else total + term
                    if keep == n + 1:
                        out["keep"][...] = total
                sum_ref[...] = total
                gates_refs = [sum_ref] + ([ins[gates_at]] if gates_at is not None else [])
                memory_ref = None
                if memory is not None:
                    memory_ref = ins[memory_at]
                    if memory[1] is not None:
                        memory_ref = memory_ref.at[memory[1]]
                hidden_to, memory_to = [], []
                if after is not None or done is not None:
                    hidden_to.append(hidden_ref)
                if "hidden" in outs:
                    hidden_to.append(out["hidden"])
                if "both" in outs:
                    hidden_to.append(out["both"].at[0])
                    memory_to.append(out["both"].at[1])
                if "memory" in outs:
                    memory_to.append(out["memory"])
                self.update(
                    info, gates_refs, bias_ref, memory_ref, width, halo, hidden_to, memory_to
                )
                if after is not None:
                    self.load(hidden_ref, None, info, stage_ref, width)
                    self.spread(stage_ref, patch_ref, width, width)
                    out["after"][...] = jnp.dot(
                        patch_ref[...], weight_ref[after], preferred_element_type=F32
                    )
                if done is not None:
                    self.tiles(info, hidden_ref, width, tile_refs)

            if relay is not None:

                @pl.when(info.section == relay[0])
                def _():
                    out["both"][...] = ins[relay_at][...]

            if done is not None:
                for section, (at, (_, index, span)) in enumerate(zip(done_at, done)):

                    @pl.when(info.section == section)
                    def _():
                        source = ins[at] if index is None else ins[at].at[index]
                        self.tiles(info, source, span, tile_refs)

        return pl.pallas_call(
            kernel,
            out_shape=shapes,
            in_specs=specs,
            out_specs=[VMEM] * len(shapes),
            scratch_shapes=[
                pltpu.VMEM(((self.height + 2) * widest + 16, channels), F32),
                pltpu.VMEM((pixels, TAPS * channels), BF),
                pltpu.VMEM((pixels, 4 * channels), F32),
                pltpu.VMEM((pixels, channels), F32),
            ],
            cost_estimate=self.cost(pixels, len(terms) + (after is not None)),
            compiler_params=pltpu.CompilerParams(vmem_limit_bytes=LIMIT),
        )(*operands)

    def cost(self, pixels, products):
        return pl.CostEstimate(
            flops=8 * pixels * TAPS * self.channels * self.channels * products,
            bytes_accessed=pixels * self.channels * 2, transcendentals=0,
        )

    def partial(self, turn, array, index, width, part):
        pixels, channels = self.height * width, self.channels

        def kernel(weight_ref, in_ref, out_ref, stage_ref, patch_ref):
            info = Position(self.batch)

            @pl.when(info.section == turn)
            def _():
                self.load(in_ref, index, info, stage_ref, width)
                self.spread(stage_ref, patch_ref, width, width)
                out_ref[...] = jnp.dot(
                    patch_ref[...], weight_ref[part], preferred_element_type=F32
                )

        return pl.pallas_call(
            kernel,
            out_shape=jax.ShapeDtypeStruct((pixels, 4 * channels), F32),
            in_specs=[VMEM, VMEM],
            out_specs=VMEM,
            scratch_shapes=[
                pltpu.VMEM(((self.height + 2) * width + 16, channels), F32),
                pltpu.VMEM((pixels, TAPS * channels), BF),
            ],
            cost_estimate=self.cost(pixels, 1),
            compiler_params=pltpu.CompilerParams(vmem_limit_bytes=LIMIT),
        )(self.weight, array)


def joined_weight(shards, channels):
    per = 2 * TAPS // len(shards)

    def kernel(*refs):
        sources, out_ref, sems = refs[: len(shards)], refs[len(shards)], refs[len(shards) + 1]

        def copy(ref, block):
            src = ref.at[pl.ds(block % per * channels, channels), :]
            dst = out_ref.at[block % 2, pl.ds(block // 2 * channels, channels), :]
            return pltpu.make_async_copy(src, dst, sems.at[block])

        for which, ref in enumerate(sources):
            owner = lax.rem(lax.axis_index("row") + which, len(shards))
            for shard in range(len(shards)):

                @pl.when(owner == shard)
                def _():
                    for block in range(shard * per, shard * per + per):
                        copy(ref, block).start()

        for block in range(2 * TAPS):
            copy(sources[0], block).wait()

    rows, columns = shards[0].shape[0] * len(shards) // 2, shards[0].shape[1]
    return pl.pallas_call(
        kernel,
        out_shape=pltpu.VMEM((2, rows, columns), BF),
        in_specs=[HBM] + [pl.BlockSpec(memory_space=pl.ANY)] * (len(shards) - 1),
        out_specs=VMEM,
        scratch_shapes=[pltpu.SemaphoreType.DMA((2 * TAPS,))],
        compiler_params=pltpu.CompilerParams(vmem_limit_bytes=LIMIT),
        name="join",
    )(pltpu.with_memory_space_constraint(shards[0], pltpu.HBM), *shards[1:])


def window_levels(features, gate_weight, gate_bias):
    batch, frames, tile_rows, tile_cols, channels = features.shape
    _, row, _ = (lax.axis_index(a) for a in ("section", "row", "col"))
    row_size = lax.axis_size("row")
    groups = row_size // batch
    place = row % batch
    row_halo = HALO if groups > 1 else 0
    height = tile_rows * batch + 2 * row_halo
    wide, narrow = tile_cols + 2 * HALO, tile_cols + 2 * INNER

    if groups == 1 and batch == 2:
        pieces = paired_pieces(features)
    else:
        window = gather_sequence(features)
        if groups > 1:
            window = with_halo(window, "row", 1, batch)
        pieces = with_halo(window, "col", 2, 1).reshape(frames, height * wide, channels)

    own_weight = gate_weight[0]
    if row_size == 2 and own_weight.shape[0] % channels == 0:
        shards = [own_weight, lax.ppermute(own_weight, "row", [(0, 1), (1, 0)])]
    else:
        shards = [lax.all_gather(own_weight, "row", axis=0, tiled=True)]

    weight = joined_weight(shards, channels)
    plan = Plan(weight, gate_bias, height, channels, batch, tile_rows, tile_cols, row_halo)

    h00, c00 = plan.step(0, [(pieces, 0, wide, 0)], wide, outs=("hidden", "memory"))
    x10 = section_send(h00, (0, 1, 2, 3))
    h01, s01 = plan.step(
        0, [(pieces, 1, wide, 0), (h00, None, wide, 1)], narrow, memory=(c00, None),
        outs=("hidden", "both"),
    )
    x11 = section_send(h01, (0, 1, 2, 3))
    h10, c10, p11 = plan.step(1, [(x10, None, wide, 0)], narrow, after=1, outs=("hidden", "memory"))
    (s11,) = plan.step(
        1, [(x11, None, narrow, 0)], narrow, gates_in=p11, memory=(c10, None), outs=("both",),
        relay=(0, s01),
    )
    x2 = section_swap(s11, ((1, 2), (0, 3)))
    p30 = plan.partial(3, x2, 0, narrow, 1)
    h20, c20, p21 = plan.step(
        2, [(x2, 0, narrow, 0), (x2, 0, narrow, 1)], narrow, memory=(x2, 1), keep=1,
        outs=("hidden", "memory"),
    )
    x30 = section_send(h20, (0, 1, 2, 3))
    (h21,) = plan.step(2, [(h20, None, narrow, 1)], narrow, gates_in=p21, memory=(c20, None), outs=("hidden",))
    x31 = section_send(h21, (0, 1, 2, 3))
    c30, *first, p31 = plan.step(
        3, [(x30, None, narrow, 0)], narrow, gates_in=p30, memory=(x2, 1), after=1,
        outs=("memory", "tiles"), done=((h00, None, wide), (h10, None, narrow), (h20, None, narrow)),
    )
    second = plan.step(
        3, [(x31, None, narrow, 0)], narrow, gates_in=p31, memory=(c30, None),
        outs=("tiles",), done=((h01, None, narrow), (s11, 0, narrow), (h21, None, narrow)),
    )

    parts = [[first[0], second[0]]]
    for k in range(1, batch):
        pairs = group_pairs(row_size, batch, k)
        parts.append([lax.ppermute(tiles[k], "row", pairs) for tiles in (first, second)])
    result = []
    for q in range(batch):
        chosen = parts[0]
        for k in range(1, batch):
            chosen = [
                jnp.where((place - q) % batch == k, other, one) for one, other in zip(chosen, parts[k])
            ]
        result += chosen
    return jnp.concatenate([r[None] for r in result]).reshape(
        1, batch, frames, tile_rows, tile_cols, channels
    )


def solution(mesh):
    return jax.shard_map(
        window_levels,
        mesh=mesh,
        in_specs=(P(None, None, "row", "col", None), P("section", "row", None), P("section", None)),
        out_specs=P("section", None, None, "row", "col", None),
        check_vma=False,
    )
```

```python
import jax
import jax.numpy as jnp
from jax import lax
from jax.experimental import pallas as pl
from jax.experimental.pallas import tpu as pltpu
from jax.sharding import PartitionSpec as P


HALO = 8
TAPS = 9
BF = jnp.bfloat16
F32 = jnp.float32
VMEM = pl.BlockSpec(memory_space=pltpu.VMEM)
HBM = pl.BlockSpec(memory_space=pltpu.HBM)
LIMIT = 12 * 1024 * 1024
MIDDLE = 6
INNER = 4


def section_send(block, route):
    return lax.ppermute(block, "section", [(route[i], route[(i + 1) % 4]) for i in range(4)])


def section_swap(block, pairs):
    return lax.ppermute(block, "section", [*pairs, *((b, a) for a, b in pairs)])


class Position:
    def __init__(self, batch):
        row = lax.axis_index("row")
        self.section, self.col, self.last_col = (
            lax.axis_index("section"), lax.axis_index("col"), lax.axis_size("col") - 1,
        )
        self.place, self.group = lax.rem(row, batch), lax.div(row, batch)
        self.last_group = lax.axis_size("row") // batch - 1


def group_pairs(size, batch, k):
    return [(i, i - i % batch + (i % batch + k) % batch) for i in range(size)]


def gather_sequence(features):
    batch = features.shape[0]
    size = lax.axis_size("row")
    place = lax.axis_index("row") % batch
    parts = [lax.dynamic_index_in_dim(features, place, 0, keepdims=False)]
    for k in range(1, batch):
        sent = lax.dynamic_index_in_dim(features, (place + k) % batch, 0, keepdims=False)
        parts.append(lax.ppermute(sent, "row", group_pairs(size, batch, k)))
    stacked = jnp.stack(parts)
    blocks = [
        lax.dynamic_index_in_dim(stacked, (place - q) % batch, 0, keepdims=False)
        for q in range(batch)
    ]
    return jnp.concatenate(blocks, axis=1)


def with_halo(array, axis, dim, stride):
    size, length = lax.axis_size(axis), array.shape[dim]
    up = [(i, i + stride) for i in range(size - stride)]
    down = [(j, i) for i, j in up]
    last = lax.slice_in_dim(array, length - HALO, length, axis=dim)
    first = lax.slice_in_dim(array, 0, HALO, axis=dim)
    before = lax.ppermute(last, axis, up)
    after = lax.ppermute(first, axis, down)
    return jnp.concatenate([before, array, after], axis=dim)


def paired_pieces(features):
    batch, frames, tile_rows, tile_cols, channels = features.shape
    cols = lax.axis_size("col")
    partner = lax.ppermute(features, "row", [(0, 1), (1, 0)])

    def kernel(own_ref, partner_ref, out_ref):
        right = lax.axis_index("row") == 0
        for which, ref in enumerate((own_ref, partner_ref)):
            for frame in range(frames):
                for i in range(tile_rows):
                    for b in range(batch):
                        row = ref[b, frame, i].astype(F32)
                        side = jnp.where(right, row[tile_cols - HALO :], row[:HALO])
                        out_ref[which, frame, i, :, pl.ds(b * channels, channels)] = side.astype(BF)

    edge = pl.pallas_call(
        kernel,
        out_shape=jax.ShapeDtypeStruct((2, frames, tile_rows, HALO, batch * channels), BF),
        in_specs=[VMEM, VMEM],
        out_specs=VMEM,
        compiler_params=pltpu.CompilerParams(vmem_limit_bytes=LIMIT),
        name="edge",
    )(features, partner)
    up = list(range(cols))
    ring = up + [cols + c for c in reversed(up)]
    pairs = [(ring[i], ring[(i + 1) % len(ring)]) for i in range(len(ring))]
    side = lax.ppermute(edge, ("row", "col"), pairs)
    other = lax.ppermute(side, "row", [(0, 1), (1, 0)])
    return [features, partner, side, other]


def sigmoid(x):
    return 0.5 * jnp.tanh(0.5 * x) + 0.5


class Plan:
    def __init__(self, weight, bias, height, channels, batch, tile_rows, tile_cols, row_halo):
        self.weight, self.bias = weight, bias
        self.height, self.channels, self.batch = height, channels, batch
        self.tile_rows, self.tile_cols, self.row_halo = tile_rows, tile_cols, row_halo

    def base(self, width):
        return -(-width // 8) * 8 + 8

    def frame(self, stage_ref, width):
        base, pixels = self.base(width), self.height * width
        stage_ref[pl.ds(0, base), :] = jnp.zeros((base, self.channels), F32)
        stage_ref[pl.ds(base + pixels, base), :] = jnp.zeros((base, self.channels), F32)

    def load(self, ref, index, info, stage_ref, width):
        self.frame(stage_ref, width)
        base, channels, pixels = self.base(width), self.channels, self.height * width
        if not isinstance(ref, list):
            value = ref[...] if index is None else ref[index]
            if value.shape[-1] == channels:
                stage_ref[pl.ds(base, pixels), :] = value.astype(F32)
            else:
                half = pixels // 2
                for k in range(2):
                    part = value[:, k * channels : (k + 1) * channels]
                    stage_ref[pl.ds(base + k * half, half), :] = part.astype(F32)
            return
        own, partner, side, other = ref
        rows, place = self.tile_rows, info.place
        for i in range(rows):
            for which, tile in enumerate((own, partner)):
                block = place if which == 0 else 1 - place
                start = pl.multiple_of((block * rows + i) * width, 8) + base + HALO
                stage_ref[pl.ds(start, self.tile_cols), :] = tile[place, index, i].astype(F32)
        first = place == 0
        left, right = info.col > 0, info.col < info.last_col

        def mine(piece, k, i):
            value = piece[k, index, i].astype(F32)
            return jnp.where(first, value[:, :channels], value[:, channels:])

        for k in range(2):
            for i in range(rows):
                a, b = mine(side, k, i), mine(other, k, i)
                start = base + (k * rows + i) * width
                stage_ref[pl.ds(start, HALO), :] = jnp.where(left, jnp.where(first, a, b), 0.0)
                start = base + ((1 - k) * rows + i) * width + HALO + self.tile_cols
                stage_ref[pl.ds(start, HALO), :] = jnp.where(right, jnp.where(first, b, a), 0.0)

    def spread(self, stage_ref, patch_ref, width, out_width):
        base, channels = self.base(width), self.channels
        inset = (width - out_width) // 2
        pixels = self.height * out_width
        for tap in range(TAPS):
            start = base + (tap // 3 - 1) * width + tap % 3 - 1
            if inset == 0:
                value = stage_ref[pl.ds(start, pixels), :]
            else:
                value = jnp.concatenate(
                    [
                        stage_ref[pl.ds(start + inset + i * width, out_width), :]
                        for i in range(self.height)
                    ]
                )
            patch_ref[pl.ds(0, pixels), pl.ds(tap * channels, channels)] = value.astype(BF)

    def product(self, weight_ref, part, patch_ref, width):
        return jnp.dot(
            patch_ref[pl.ds(0, self.height * width), :],
            weight_ref[part],
            preferred_element_type=F32,
        )

    def split(self, i, width):
        half = self.height // 2
        return pl.ds(i % half * width, width), pl.ds(i // half * self.channels, self.channels)

    def update(self, info, gates_refs, bias_ref, memory, width, stage_ref, plain_out, packed_out):
        ch = self.channels
        halo, base = (width - self.tile_cols) // 2, self.base(width)
        low = jnp.where(info.col == 0, halo, 0)
        high = jnp.where(info.col == info.last_col, width - halo, width)
        top = jnp.where(info.group == 0, self.row_halo, 0)
        bottom = jnp.where(info.group == info.last_group, self.height - self.row_halo, self.height)
        for i in range(self.height):
            rows = pl.ds(i * width, width)
            gates = bias_ref[...]
            for ref in gates_refs:
                gates = gates + ref[rows, :]
            cell = sigmoid(gates[:, :ch]) * jnp.tanh(gates[:, 2 * ch : 3 * ch])
            if memory is not None:
                ref, span = memory
                if ref.shape[-1] == ch:
                    before = ref[pl.ds(i * span + (span - width) // 2, width), :]
                else:
                    before = ref[self.split(i, width)]
                cell = cell + sigmoid(gates[:, ch : 2 * ch]) * before.astype(F32)
            hidden = sigmoid(gates[:, 3 * ch :]) * jnp.tanh(cell)
            column = lax.broadcasted_iota(jnp.int32, hidden.shape, 0)
            inside = (column >= low) & (column < high)
            if self.row_halo:
                inside = inside & (i >= top) & (i < bottom)
            stage_ref[pl.ds(base + i * width, width), :] = jnp.where(inside, hidden, 0.0)
            if plain_out is not None:
                plain_out[rows, :] = cell
            if packed_out is not None:
                packed_out[self.split(i, width)] = cell.astype(BF)

    def pack(self, stage_ref, width, out_ref):
        half, channels = self.height * width // 2, self.channels
        for k in range(2):
            value = stage_ref[pl.ds(self.base(width) + k * half, half), :]
            out_ref[:, pl.ds(k * channels, channels)] = value.astype(BF)

    def tiles(self, info, read, width, frame, outs):
        halo = (width - self.tile_cols) // 2
        for i in range(self.tile_rows):
            rows = [
                read(self.row_halo + b * self.tile_rows + i).astype(F32)[halo : halo + self.tile_cols]
                for b in range(self.batch)
            ]
            for k, out in enumerate(outs):
                value = rows[0]
                for b in range(1, self.batch):
                    value = jnp.where(lax.rem(info.place + k, self.batch) == b, rows[b], value)
                out[frame, i] = value.astype(BF)

    def step(self, turn, terms, width, gates_in=None, memory=None, keep=None, after=None, outs=(),
             done=None, relay=None):
        channels, batch = self.channels, self.batch
        pixels = self.height * width
        operands = [self.weight, self.bias]
        specs = [VMEM, VMEM]
        seen = {}

        def place_of(array):
            if array is None:
                return None
            if isinstance(array, list):
                return [place_of(a) for a in array]
            if id(array) not in seen:
                seen[id(array)] = len(operands)
                operands.append(array)
                specs.append(VMEM)
            return seen[id(array)]

        term_at = [place_of(t[0]) for t in terms]
        gates_at = place_of(gates_in)
        memory_at = place_of(memory[0]) if memory is not None else None
        done_at = [[place_of(f[0]) for f in frames] for frames in done] if done else None
        relay_at = place_of(relay[1]) if relay is not None else None
        shapes, names = [], []

        def add(name, shape, dtype):
            shapes.append(jax.ShapeDtypeStruct(shape, dtype))
            names.append(name)

        for name in outs:
            if name == "hidden":
                add(name, (pixels // 2, 2 * channels), BF)
            elif name == "both":
                add(name, (2, pixels // 2, 2 * channels), BF)
            elif name == "memory":
                add(name, (pixels, channels), F32)
            elif name == "tiles":
                for k in range(batch):
                    add(f"tile{k}", (len(done[0]), self.tile_rows, self.tile_cols, channels), BF)
        if keep is not None:
            add("keep", (pixels, 4 * channels), F32)
        if after is not None:
            add("after", (self.height * after[1], 4 * channels), F32)
        count = len(operands)
        widest = max([t[2] for t in terms] + [width])

        def kernel(*refs):
            ins, out = refs[:count], dict(zip(names, refs[count : count + len(shapes)]))
            stage_ref, patch_ref, sum_ref = refs[count + len(shapes) :]
            weight_ref, bias_ref = ins[:2]
            info = Position(batch)

            def ref_of(at):
                return [ref_of(a) for a in at] if isinstance(at, list) else ins[at]

            @pl.when(info.section == turn)
            def _():
                total, last = None, None
                for n, ((_, index, span, part), at) in enumerate(zip(terms, term_at)):
                    if (at, index) != last:
                        self.load(ref_of(at), index, info, stage_ref, span)
                        self.spread(stage_ref, patch_ref, span, width)
                    last = (at, index)
                    term = self.product(weight_ref, part, patch_ref, width)
                    total = term if total is None else total + term
                    if keep == n + 1:
                        out["keep"][...] = total
                sum_ref[...] = total
                gates_refs = [sum_ref] + ([ins[gates_at]] if gates_at is not None else [])
                before = None
                if memory is not None:
                    ref = ins[memory_at]
                    before = (ref if memory[1] is None else ref.at[memory[1]], memory[2])
                both = out.get("both")
                self.update(
                    info, gates_refs, bias_ref, before, width, stage_ref, out.get("memory"),
                    both.at[1] if both is not None else None,
                )
                if "hidden" in out:
                    self.pack(stage_ref, width, out["hidden"])
                if both is not None:
                    self.pack(stage_ref, width, both.at[0])
                if after is not None:
                    self.frame(stage_ref, width)
                    self.spread(stage_ref, patch_ref, width, after[1])
                    out["after"][...] = self.product(weight_ref, after[0], patch_ref, after[1])

            if relay is not None:

                @pl.when(info.section == relay[0])
                def _():
                    out["both"][...] = ins[relay_at][...]

            if done is not None:
                tile_refs = [out[f"tile{k}"] for k in range(batch)]
                for section, frames in enumerate(done):

                    @pl.when(info.section == section)
                    def _():
                        for frame, (array, index, span) in enumerate(frames):
                            if array is None:

                                def read(i):
                                    return stage_ref[pl.ds(self.base(width) + i * width, width), :]

                                self.tiles(info, read, width, frame, tile_refs)
                                continue
                            source = ins[done_at[section][frame]]
                            source = source if index is None else source.at[index]
                            self.tiles(
                                info, lambda i: source[self.split(i, span)], span, frame, tile_refs
                            )

        return pl.pallas_call(
            kernel,
            out_shape=shapes,
            in_specs=specs,
            out_specs=[VMEM] * len(shapes),
            scratch_shapes=[
                pltpu.VMEM((self.height * widest + 2 * self.base(widest), channels), F32),
                pltpu.VMEM((pixels, TAPS * channels), BF),
                pltpu.VMEM((pixels, 4 * channels), F32),
            ],
            cost_estimate=self.cost(pixels, len(terms) + (after is not None)),
            compiler_params=pltpu.CompilerParams(vmem_limit_bytes=LIMIT),
        )(*operands)

    def cost(self, pixels, products):
        return pl.CostEstimate(
            flops=8 * pixels * TAPS * self.channels * self.channels * products,
            bytes_accessed=pixels * self.channels * 2, transcendentals=0,
        )

    def partial(self, turn, array, index, width, part):
        pixels, channels = self.height * width, self.channels

        def kernel(weight_ref, in_ref, out_ref, stage_ref, patch_ref):
            info = Position(self.batch)

            @pl.when(info.section == turn)
            def _():
                self.load(in_ref, index, info, stage_ref, width)
                self.spread(stage_ref, patch_ref, width, width)
                out_ref[...] = self.product(weight_ref, part, patch_ref, width)

        return pl.pallas_call(
            kernel,
            out_shape=jax.ShapeDtypeStruct((pixels, 4 * channels), F32),
            in_specs=[VMEM, VMEM],
            out_specs=VMEM,
            scratch_shapes=[
                pltpu.VMEM((pixels + 2 * self.base(width), channels), F32),
                pltpu.VMEM((pixels, TAPS * channels), BF),
            ],
            cost_estimate=self.cost(pixels, 1),
            compiler_params=pltpu.CompilerParams(vmem_limit_bytes=LIMIT),
        )(self.weight, array)


def joined_weight(shards, channels):
    per = 2 * TAPS // len(shards)
    rows, columns = shards[0].shape[0] * len(shards) // 2, shards[0].shape[1]
    joined = None
    for which, shard in enumerate(shards):

        def kernel(*refs):
            in_ref, out_ref, sems = refs[-3:]

            def copy(block):
                src = in_ref.at[pl.ds(block % per * channels, channels), :]
                dst = out_ref.at[block % 2, pl.ds(block // 2 * channels, channels), :]
                return pltpu.make_async_copy(src, dst, sems.at[block % per])

            owner = lax.rem(lax.axis_index("row") + which, len(shards))
            for index in range(len(shards)):

                @pl.when(owner == index)
                def _():
                    for block in range(index * per, index * per + per):
                        copy(block).start()
                    for block in range(index * per, index * per + per):
                        copy(block).wait()

        source = pltpu.with_memory_space_constraint(shard, pltpu.HBM) if which == 0 else shard
        joined = pl.pallas_call(
            kernel,
            out_shape=pltpu.VMEM((2, rows, columns), BF),
            in_specs=([] if joined is None else [VMEM])
            + [HBM if which == 0 else pl.BlockSpec(memory_space=pl.ANY)],
            out_specs=VMEM,
            scratch_shapes=[pltpu.SemaphoreType.DMA((per,))],
            input_output_aliases={} if joined is None else {0: 0},
            compiler_params=pltpu.CompilerParams(vmem_limit_bytes=LIMIT),
        )(*([] if joined is None else [joined]), source)
    return joined


def window_levels(features, gate_weight, gate_bias):
    batch, frames, tile_rows, tile_cols, channels = features.shape
    _, row, _ = (lax.axis_index(a) for a in ("section", "row", "col"))
    row_size = lax.axis_size("row")
    groups = row_size // batch
    place = row % batch
    row_halo = HALO if groups > 1 else 0
    height = tile_rows * batch + 2 * row_halo
    wide, middle, narrow = (tile_cols + 2 * k for k in (HALO, MIDDLE, INNER))

    if groups == 1 and batch == 2:
        pieces = paired_pieces(features)
    else:
        window = gather_sequence(features)
        if groups > 1:
            window = with_halo(window, "row", 1, batch)
        pieces = with_halo(window, "col", 2, 1).reshape(frames, height * wide, channels)

    own_weight = gate_weight[0]
    if row_size == 2 and own_weight.shape[0] % channels == 0:
        shards = [own_weight, lax.ppermute(own_weight, "row", [(0, 1), (1, 0)])]
    else:
        shards = [lax.all_gather(own_weight, "row", axis=0, tiled=True)]

    weight = joined_weight(shards, channels)
    plan = Plan(weight, gate_bias, height, channels, batch, tile_rows, tile_cols, row_halo)

    cycle = (0, 1, 2, 3)
    h00, c00 = plan.step(0, [(pieces, 0, wide, 0)], middle, outs=("hidden", "memory"))
    x10 = section_send(h00, cycle)
    h01, s01 = plan.step(
        0, [(pieces, 1, wide, 0), (h00, None, middle, 1)], narrow, memory=(c00, None, middle),
        outs=("hidden", "both"),
    )
    x11 = section_send(h01, cycle)
    h10, c10, p11 = plan.step(
        1, [(x10, None, middle, 0)], narrow, after=(1, narrow), outs=("hidden", "memory")
    )
    (s11,) = plan.step(
        1, [(x11, None, narrow, 0)], narrow, gates_in=p11, memory=(c10, None, narrow), outs=("both",),
        relay=(0, s01),
    )
    x2 = section_swap(s11, ((1, 2), (0, 3)))
    p30 = plan.partial(3, x2, 0, narrow, 1)
    h20, c20, p21 = plan.step(
        2, [(x2, 0, narrow, 0), (x2, 0, narrow, 1)], narrow, memory=(x2, 1, narrow), keep=1,
        outs=("hidden", "memory"),
    )
    x30 = section_send(h20, cycle)
    (h21,) = plan.step(
        2, [(h20, None, narrow, 1)], narrow, gates_in=p21, memory=(c20, None, narrow), outs=("hidden",)
    )
    x31 = section_send(h21, cycle)
    h30, c30, p31 = plan.step(
        3, [(x30, None, narrow, 0)], narrow, gates_in=p30, memory=(x2, 1, narrow),
        after=(1, tile_cols), outs=("hidden", "memory"),
    )
    tiles = plan.step(
        3, [(x31, None, narrow, 0)], tile_cols, gates_in=p31, memory=(c30, None, narrow),
        outs=("tiles",),
        done=(
            ((h00, None, middle), (h01, None, narrow)),
            ((h10, None, narrow), (s11, 0, narrow)),
            ((h20, None, narrow), (h21, None, narrow)),
            ((h30, None, narrow), (None, None, tile_cols)),
        ),
    )

    parts = [tiles[0]]
    for k in range(1, batch):
        parts.append(lax.ppermute(tiles[k], "row", group_pairs(row_size, batch, k)))
    result = []
    for q in range(batch):
        chosen = parts[0]
        for k in range(1, batch):
            chosen = jnp.where((place - q) % batch == k, parts[k], chosen)
        result.append(chosen)
    return jnp.stack(result)[None]


def solution(mesh):
    return jax.shard_map(
        window_levels,
        mesh=mesh,
        in_specs=(P(None, None, "row", "col", None), P("section", "row", None), P("section", None)),
        out_specs=P("section", None, None, "row", "col", None),
        check_vma=False,
    )
```

```python
import jax
import jax.numpy as jnp
from jax import lax
from jax.experimental import pallas as pl
from jax.experimental.pallas import tpu as pltpu
from jax.sharding import PartitionSpec as P


HALO = 8
TAPS = 9
BF = jnp.bfloat16
F32 = jnp.float32
VMEM = pl.BlockSpec(memory_space=pltpu.VMEM)
HBM = pl.BlockSpec(memory_space=pltpu.HBM)
LIMIT = 12 * 1024 * 1024
MIDDLE = 6
INNER = 4


def section_send(block, route):
    return lax.ppermute(block, "section", [(route[i], route[(i + 1) % 4]) for i in range(4)])


class Position:
    def __init__(self, batch):
        row = lax.axis_index("row")
        self.section, self.col, self.last_col = (
            lax.axis_index("section"), lax.axis_index("col"), lax.axis_size("col") - 1,
        )
        self.place, self.group = lax.rem(row, batch), lax.div(row, batch)
        self.last_group = lax.axis_size("row") // batch - 1


def group_pairs(size, batch, k):
    return [(i, i - i % batch + (i % batch + k) % batch) for i in range(size)]


def gather_sequence(features):
    batch = features.shape[0]
    size = lax.axis_size("row")
    place = lax.axis_index("row") % batch
    parts = [lax.dynamic_index_in_dim(features, place, 0, keepdims=False)]
    for k in range(1, batch):
        sent = lax.dynamic_index_in_dim(features, (place + k) % batch, 0, keepdims=False)
        parts.append(lax.ppermute(sent, "row", group_pairs(size, batch, k)))
    stacked = jnp.stack(parts)
    blocks = [
        lax.dynamic_index_in_dim(stacked, (place - q) % batch, 0, keepdims=False)
        for q in range(batch)
    ]
    return jnp.concatenate(blocks, axis=1)


def with_halo(array, axis, dim, stride):
    size, length = lax.axis_size(axis), array.shape[dim]
    up = [(i, i + stride) for i in range(size - stride)]
    down = [(j, i) for i, j in up]
    last = lax.slice_in_dim(array, length - HALO, length, axis=dim)
    first = lax.slice_in_dim(array, 0, HALO, axis=dim)
    before = lax.ppermute(last, axis, up)
    after = lax.ppermute(first, axis, down)
    return jnp.concatenate([before, array, after], axis=dim)


def paired_pieces(features):
    batch, frames, tile_rows, tile_cols, channels = features.shape
    cols = lax.axis_size("col")
    partner = lax.ppermute(features, "row", [(0, 1), (1, 0)])

    def take(in_ref, out_ref, sem):
        copy = pltpu.make_async_copy(in_ref, out_ref, sem)
        copy.start()
        copy.wait()

    own = pl.pallas_call(
        take,
        out_shape=pltpu.VMEM(features.shape, features.dtype),
        in_specs=[HBM],
        out_specs=VMEM,
        scratch_shapes=[pltpu.SemaphoreType.DMA(())],
        compiler_params=pltpu.CompilerParams(vmem_limit_bytes=LIMIT),
        name="take",
    )(pltpu.with_memory_space_constraint(features, pltpu.HBM))

    def kernel(own_ref, partner_ref, out_ref):
        right = lax.axis_index("row") == 0
        for which, ref in enumerate((own_ref, partner_ref)):
            for frame in range(frames):
                for i in range(tile_rows):
                    for b in range(batch):
                        row = ref[b, frame, i].astype(F32)
                        side = jnp.where(right, row[tile_cols - HALO :], row[:HALO])
                        out_ref[which, frame, i, :, pl.ds(b * channels, channels)] = side.astype(BF)

    edge = pl.pallas_call(
        kernel,
        out_shape=jax.ShapeDtypeStruct((2, frames, tile_rows, HALO, batch * channels), BF),
        in_specs=[VMEM, VMEM],
        out_specs=VMEM,
        compiler_params=pltpu.CompilerParams(vmem_limit_bytes=LIMIT),
        name="edge",
    )(own, partner)
    up = list(range(cols))
    ring = up + [cols + c for c in reversed(up)]
    pairs = [(ring[i], ring[(i + 1) % len(ring)]) for i in range(len(ring))]
    side = lax.ppermute(edge, ("row", "col"), pairs)
    other = lax.ppermute(side, "row", [(0, 1), (1, 0)])
    return [own, partner, side, other]


def sigmoid(x):
    return 0.5 * jnp.tanh(0.5 * x) + 0.5


class Plan:
    def __init__(self, weight, bias, height, channels, batch, tile_rows, tile_cols, row_halo):
        self.weight, self.bias = weight, bias
        self.height, self.channels, self.batch = height, channels, batch
        self.tile_rows, self.tile_cols, self.row_halo = tile_rows, tile_cols, row_halo

    def base(self, width):
        return -(-width // 8) * 8 + 8

    def frame(self, stage_ref, width):
        base, pixels = self.base(width), self.height * width
        stage_ref[pl.ds(0, base), :] = jnp.zeros((base, self.channels), F32)
        stage_ref[pl.ds(base + pixels, base), :] = jnp.zeros((base, self.channels), F32)

    def load(self, ref, index, info, stage_ref, width):
        self.frame(stage_ref, width)
        base, channels, pixels = self.base(width), self.channels, self.height * width
        if not isinstance(ref, list):
            value = ref[...] if index is None else ref[index]
            if value.shape[-1] == channels:
                stage_ref[pl.ds(base, pixels), :] = value.astype(F32)
            else:
                half = pixels // 2
                for k in range(2):
                    part = value[:, k * channels : (k + 1) * channels]
                    stage_ref[pl.ds(base + k * half, half), :] = part.astype(F32)
            return
        own, partner, side, other = ref
        rows, place = self.tile_rows, info.place
        for i in range(rows):
            for which, tile in enumerate((own, partner)):
                block = place if which == 0 else 1 - place
                start = pl.multiple_of((block * rows + i) * width, 8) + base + HALO
                stage_ref[pl.ds(start, self.tile_cols), :] = tile[place, index, i].astype(F32)
        first = place == 0
        left, right = info.col > 0, info.col < info.last_col

        def mine(piece, k, i):
            value = piece[k, index, i].astype(F32)
            return jnp.where(first, value[:, :channels], value[:, channels:])

        for k in range(2):
            for i in range(rows):
                a, b = mine(side, k, i), mine(other, k, i)
                start = base + (k * rows + i) * width
                stage_ref[pl.ds(start, HALO), :] = jnp.where(left, jnp.where(first, a, b), 0.0)
                start = base + ((1 - k) * rows + i) * width + HALO + self.tile_cols
                stage_ref[pl.ds(start, HALO), :] = jnp.where(right, jnp.where(first, b, a), 0.0)

    def spread(self, stage_ref, patch_ref, width, out_width):
        base, channels = self.base(width), self.channels
        inset = (width - out_width) // 2
        pixels = self.height * out_width
        for tap in range(TAPS):
            start = base + (tap // 3 - 1) * width + tap % 3 - 1
            if inset == 0:
                value = stage_ref[pl.ds(start, pixels), :]
            else:
                value = jnp.concatenate(
                    [
                        stage_ref[pl.ds(start + inset + i * width, out_width), :]
                        for i in range(self.height)
                    ]
                )
            patch_ref[pl.ds(0, pixels), pl.ds(tap * channels, channels)] = value.astype(BF)

    def product(self, weight_ref, part, patch_ref, width):
        return jnp.dot(
            patch_ref[pl.ds(0, self.height * width), :],
            weight_ref[part],
            preferred_element_type=F32,
        )

    def split(self, i, width):
        half = self.height // 2
        return pl.ds(i % half * width, width), pl.ds(i // half * self.channels, self.channels)

    def update(self, info, gates_refs, bias_ref, memory, width, stage_ref, plain_out, packed_out):
        ch = self.channels
        halo, base = (width - self.tile_cols) // 2, self.base(width)
        low = jnp.where(info.col == 0, halo, 0)
        high = jnp.where(info.col == info.last_col, width - halo, width)
        top = jnp.where(info.group == 0, self.row_halo, 0)
        bottom = jnp.where(info.group == info.last_group, self.height - self.row_halo, self.height)
        for i in range(self.height):
            rows = pl.ds(i * width, width)
            gates = bias_ref[...]
            for ref in gates_refs:
                gates = gates + ref[rows, :]
            cell = sigmoid(gates[:, :ch]) * jnp.tanh(gates[:, 2 * ch : 3 * ch])
            if memory is not None:
                ref, span = memory
                if ref.shape[-1] == ch:
                    before = ref[pl.ds(i * span + (span - width) // 2, width), :]
                else:
                    before = ref[self.split(i, width)]
                cell = cell + sigmoid(gates[:, ch : 2 * ch]) * before.astype(F32)
            hidden = sigmoid(gates[:, 3 * ch :]) * jnp.tanh(cell)
            column = lax.broadcasted_iota(jnp.int32, hidden.shape, 0)
            inside = (column >= low) & (column < high)
            if self.row_halo:
                inside = inside & (i >= top) & (i < bottom)
            stage_ref[pl.ds(base + i * width, width), :] = jnp.where(inside, hidden, 0.0)
            if plain_out is not None:
                plain_out[rows, :] = cell
            if packed_out is not None:
                packed_out[self.split(i, width)] = cell.astype(BF)

    def pack(self, stage_ref, width, out_ref):
        half, channels = self.height * width // 2, self.channels
        for k in range(2):
            value = stage_ref[pl.ds(self.base(width) + k * half, half), :]
            out_ref[:, pl.ds(k * channels, channels)] = value.astype(BF)

    def tiles(self, info, read, width, frame, outs):
        halo = (width - self.tile_cols) // 2
        for i in range(self.tile_rows):
            rows = [
                read(self.row_halo + b * self.tile_rows + i).astype(F32)[halo : halo + self.tile_cols]
                for b in range(self.batch)
            ]
            for k, out in enumerate(outs):
                value = rows[0]
                for b in range(1, self.batch):
                    value = jnp.where(lax.rem(info.place + k, self.batch) == b, rows[b], value)
                out[frame, i] = value.astype(BF)

    def step(self, turn, terms, width, gates_in=None, memory=None, keep=None, after=None, outs=(),
             done=None, relay=None):
        channels, batch = self.channels, self.batch
        pixels = self.height * width
        operands = [self.weight, self.bias]
        specs = [VMEM, VMEM]
        seen = {}

        def place_of(array):
            if array is None:
                return None
            if isinstance(array, list):
                return [place_of(a) for a in array]
            if id(array) not in seen:
                seen[id(array)] = len(operands)
                operands.append(array)
                specs.append(VMEM)
            return seen[id(array)]

        term_at = [place_of(t[0]) for t in terms]
        gates_at = place_of(gates_in)
        memory_at = place_of(memory[0]) if memory is not None else None
        done_at = [[place_of(f[0]) for f in frames] for frames in done] if done else None
        relay_at = place_of(relay[1]) if relay is not None else None
        shapes, names = [], []

        def add(name, shape, dtype):
            shapes.append(jax.ShapeDtypeStruct(shape, dtype))
            names.append(name)

        for name in outs:
            if name == "hidden":
                add(name, (pixels // 2, 2 * channels), BF)
            elif name == "both":
                add(name, (2, pixels // 2, 2 * channels), BF)
            elif name == "memory":
                add(name, (pixels, channels), F32)
            elif name == "tiles":
                for k in range(batch):
                    add(f"tile{k}", (len(done[0]), self.tile_rows, self.tile_cols, channels), BF)
        if keep is not None:
            add("keep", (pixels, 4 * channels), F32)
        if after is not None:
            add("after", (self.height * after[1], 4 * channels), F32)
        count = len(operands)
        widest = max([t[2] for t in terms] + [width])

        def kernel(*refs):
            ins, out = refs[:count], dict(zip(names, refs[count : count + len(shapes)]))
            stage_ref, patch_ref, sum_ref = refs[count + len(shapes) :]
            weight_ref, bias_ref = ins[:2]
            info = Position(batch)

            def ref_of(at):
                return [ref_of(a) for a in at] if isinstance(at, list) else ins[at]

            @pl.when(info.section == turn)
            def _():
                total, last = None, None
                for n, ((_, index, span, part), at) in enumerate(zip(terms, term_at)):
                    if (at, index) != last:
                        self.load(ref_of(at), index, info, stage_ref, span)
                        self.spread(stage_ref, patch_ref, span, width)
                    last = (at, index)
                    term = self.product(weight_ref, part, patch_ref, width)
                    total = term if total is None else total + term
                    if keep == n + 1:
                        out["keep"][...] = total
                sum_ref[...] = total
                gates_refs = [sum_ref] + ([ins[gates_at]] if gates_at is not None else [])
                before = None
                if memory is not None:
                    ref = ins[memory_at]
                    before = (ref if memory[1] is None else ref.at[memory[1]], memory[2])
                both = out.get("both")
                self.update(
                    info, gates_refs, bias_ref, before, width, stage_ref, out.get("memory"),
                    both.at[1] if both is not None else None,
                )
                if "hidden" in out:
                    self.pack(stage_ref, width, out["hidden"])
                if both is not None:
                    self.pack(stage_ref, width, both.at[0])
                if after is not None:
                    self.frame(stage_ref, width)
                    self.spread(stage_ref, patch_ref, width, after[1])
                    out["after"][...] = self.product(weight_ref, after[0], patch_ref, after[1])

            if relay is not None:

                @pl.when(info.section == relay[0])
                def _():
                    out["both"][...] = ins[relay_at][...]

            if done is not None:
                tile_refs = [out[f"tile{k}"] for k in range(batch)]
                for section, frames in enumerate(done):

                    @pl.when(info.section == section)
                    def _():
                        for frame, (array, index, span) in enumerate(frames):
                            if array is None:

                                def read(i):
                                    return stage_ref[pl.ds(self.base(width) + i * width, width), :]

                                self.tiles(info, read, width, frame, tile_refs)
                                continue
                            source = ins[done_at[section][frame]]
                            source = source if index is None else source.at[index]
                            self.tiles(
                                info, lambda i: source[self.split(i, span)], span, frame, tile_refs
                            )

        return pl.pallas_call(
            kernel,
            out_shape=shapes,
            in_specs=specs,
            out_specs=[VMEM] * len(shapes),
            scratch_shapes=[
                pltpu.VMEM((self.height * widest + 2 * self.base(widest), channels), F32),
                pltpu.VMEM((pixels, TAPS * channels), BF),
                pltpu.VMEM((pixels, 4 * channels), F32),
            ],
            cost_estimate=self.cost(pixels, len(terms) + (after is not None)),
            compiler_params=pltpu.CompilerParams(vmem_limit_bytes=LIMIT),
        )(*operands)

    def cost(self, pixels, products):
        return pl.CostEstimate(
            flops=8 * pixels * TAPS * self.channels * self.channels * products,
            bytes_accessed=pixels * self.channels * 2, transcendentals=0,
        )

    def partial(self, turn, array, index, width, part):
        pixels, channels = self.height * width, self.channels

        def kernel(weight_ref, in_ref, out_ref, stage_ref, patch_ref):
            info = Position(self.batch)

            @pl.when(info.section == turn)
            def _():
                self.load(in_ref, index, info, stage_ref, width)
                self.spread(stage_ref, patch_ref, width, width)
                out_ref[...] = self.product(weight_ref, part, patch_ref, width)

        return pl.pallas_call(
            kernel,
            out_shape=jax.ShapeDtypeStruct((pixels, 4 * channels), F32),
            in_specs=[VMEM, VMEM],
            out_specs=VMEM,
            scratch_shapes=[
                pltpu.VMEM((pixels + 2 * self.base(width), channels), F32),
                pltpu.VMEM((pixels, TAPS * channels), BF),
            ],
            cost_estimate=self.cost(pixels, 1),
            compiler_params=pltpu.CompilerParams(vmem_limit_bytes=LIMIT),
        )(self.weight, array)


def joined_weight(shards, channels):
    per = 2 * TAPS // len(shards)
    rows, columns = shards[0].shape[0] * len(shards) // 2, shards[0].shape[1]
    joined = None
    for which, shard in enumerate(shards):

        def kernel(*refs):
            in_ref, out_ref, sems = refs[-3:]

            def copy(block):
                src = in_ref.at[pl.ds(block % per * channels, channels), :]
                dst = out_ref.at[block % 2, pl.ds(block // 2 * channels, channels), :]
                return pltpu.make_async_copy(src, dst, sems.at[block % per])

            owner = lax.rem(lax.axis_index("row") + which, len(shards))
            for index in range(len(shards)):

                @pl.when(owner == index)
                def _():
                    for block in range(index * per, index * per + per):
                        copy(block).start()
                    for block in range(index * per, index * per + per):
                        copy(block).wait()

        source = pltpu.with_memory_space_constraint(shard, pltpu.HBM) if which == 0 else shard
        joined = pl.pallas_call(
            kernel,
            out_shape=pltpu.VMEM((2, rows, columns), BF),
            in_specs=([] if joined is None else [VMEM])
            + [HBM if which == 0 else pl.BlockSpec(memory_space=pl.ANY)],
            out_specs=VMEM,
            scratch_shapes=[pltpu.SemaphoreType.DMA((per,))],
            input_output_aliases={} if joined is None else {0: 0},
            compiler_params=pltpu.CompilerParams(vmem_limit_bytes=LIMIT),
        )(*([] if joined is None else [joined]), source)
    return joined


def window_levels(features, gate_weight, gate_bias):
    batch, frames, tile_rows, tile_cols, channels = features.shape
    _, row, _ = (lax.axis_index(a) for a in ("section", "row", "col"))
    row_size = lax.axis_size("row")
    groups = row_size // batch
    place = row % batch
    row_halo = HALO if groups > 1 else 0
    height = tile_rows * batch + 2 * row_halo
    wide, middle, narrow = (tile_cols + 2 * k for k in (HALO, MIDDLE, INNER))

    if groups == 1 and batch == 2:
        pieces = paired_pieces(features)
    else:
        window = gather_sequence(features)
        if groups > 1:
            window = with_halo(window, "row", 1, batch)
        pieces = with_halo(window, "col", 2, 1).reshape(frames, height * wide, channels)

    own_weight = gate_weight[0]
    if row_size == 2 and own_weight.shape[0] % channels == 0:
        shards = [own_weight, lax.ppermute(own_weight, "row", [(0, 1), (1, 0)])]
    else:
        shards = [lax.all_gather(own_weight, "row", axis=0, tiled=True)]

    weight = joined_weight(shards, channels)
    plan = Plan(weight, gate_bias, height, channels, batch, tile_rows, tile_cols, row_halo)

    from_first, from_second, from_third = (0, 1, 3, 2), (1, 2, 0, 3), (2, 3, 1, 0)
    h00, c00 = plan.step(0, [(pieces, 0, wide, 0)], middle, outs=("hidden", "memory"))
    x10 = section_send(h00, from_first)
    h01, s01 = plan.step(
        0, [(pieces, 1, wide, 0), (h00, None, middle, 1)], narrow, memory=(c00, None, middle),
        outs=("hidden", "both"),
    )
    x11 = section_send(h01, from_first)
    h10, c10, p11 = plan.step(
        1, [(x10, None, middle, 0)], narrow, after=(1, narrow), outs=("hidden", "memory")
    )
    (s11,) = plan.step(
        1, [(x11, None, narrow, 0)], narrow, gates_in=p11, memory=(c10, None, narrow), outs=("both",),
        relay=(0, s01),
    )
    x2 = section_send(s11, from_second)
    p30 = plan.partial(3, x2, 0, narrow, 1)
    h20, c20, p21 = plan.step(
        2, [(x2, 0, narrow, 0), (x2, 0, narrow, 1)], narrow, memory=(x2, 1, narrow), keep=1,
        outs=("hidden", "memory"),
    )
    x30 = section_send(h20, from_third)
    (h21,) = plan.step(
        2, [(h20, None, narrow, 1)], narrow, gates_in=p21, memory=(c20, None, narrow), outs=("hidden",)
    )
    x31 = section_send(h21, from_third)
    h30, c30, p31 = plan.step(
        3, [(x30, None, narrow, 0)], narrow, gates_in=p30, memory=(x2, 1, narrow),
        after=(1, tile_cols), outs=("hidden", "memory"),
    )
    tiles = plan.step(
        3, [(x31, None, narrow, 0)], tile_cols, gates_in=p31, memory=(c30, None, narrow),
        outs=("tiles",),
        done=(
            ((h00, None, middle), (h01, None, narrow)),
            ((h10, None, narrow), (s11, 0, narrow)),
            ((h20, None, narrow), (h21, None, narrow)),
            ((h30, None, narrow), (None, None, tile_cols)),
        ),
    )

    parts = [tiles[0]]
    for k in range(1, batch):
        parts.append(lax.ppermute(tiles[k], "row", group_pairs(row_size, batch, k)))
    result = []
    for q in range(batch):
        chosen = parts[0]
        for k in range(1, batch):
            chosen = jnp.where((place - q) % batch == k, parts[k], chosen)
        result.append(chosen)
    return jnp.stack(result)[None]


def solution(mesh):
    return jax.shard_map(
        window_levels,
        mesh=mesh,
        in_specs=(P(None, None, "row", "col", None), P("section", "row", None), P("section", None)),
        out_specs=P("section", None, None, "row", "col", None),
        check_vma=False,
    )
```

```python
import jax
import jax.numpy as jnp
from jax import lax
from jax.experimental import pallas as pl
from jax.experimental.pallas import tpu as pltpu
from jax.sharding import PartitionSpec as P


HALO = 8
TAPS = 9
LANES = 128
BF = jnp.bfloat16
F32 = jnp.float32
VMEM = pl.BlockSpec(memory_space=pltpu.VMEM)
HBM = pl.BlockSpec(memory_space=pltpu.HBM)
LIMIT = 12 * 1024 * 1024
STEPS = 6


def section_send(block, *routes):
    pairs = [(r[i], r[(i + 1) % len(r)]) for r in routes for i in range(len(r))]
    return lax.ppermute(block, "section", pairs)


class Position:
    def __init__(self, batch):
        row = lax.axis_index("row")
        self.section, self.col, self.last_col = (
            lax.axis_index("section"), lax.axis_index("col"), lax.axis_size("col") - 1,
        )
        self.place, self.group = lax.rem(row, batch), lax.div(row, batch)
        self.last_group = lax.axis_size("row") // batch - 1


def group_pairs(size, batch, k):
    return [(i, i - i % batch + (i % batch + k) % batch) for i in range(size)]


def gather_sequence(features):
    batch = features.shape[0]
    size = lax.axis_size("row")
    place = lax.axis_index("row") % batch
    parts = [lax.dynamic_index_in_dim(features, place, 0, keepdims=False)]
    for k in range(1, batch):
        sent = lax.dynamic_index_in_dim(features, (place + k) % batch, 0, keepdims=False)
        parts.append(lax.ppermute(sent, "row", group_pairs(size, batch, k)))
    stacked = jnp.stack(parts)
    blocks = [
        lax.dynamic_index_in_dim(stacked, (place - q) % batch, 0, keepdims=False)
        for q in range(batch)
    ]
    return jnp.concatenate(blocks, axis=1)


def with_halo(array, axis, dim, stride):
    size, length = lax.axis_size(axis), array.shape[dim]
    up = [(i, i + stride) for i in range(size - stride)]
    down = [(j, i) for i, j in up]
    last = lax.slice_in_dim(array, length - HALO, length, axis=dim)
    first = lax.slice_in_dim(array, 0, HALO, axis=dim)
    before = lax.ppermute(last, axis, up)
    after = lax.ppermute(first, axis, down)
    return jnp.concatenate([before, array, after], axis=dim)


def paired_pieces(features):
    batch, frames, tile_rows, tile_cols, channels = features.shape
    cols = lax.axis_size("col")
    partner = lax.ppermute(features, "row", [(0, 1), (1, 0)])

    def take(in_ref, out_ref, sem):
        copy = pltpu.make_async_copy(in_ref, out_ref, sem)
        copy.start()
        copy.wait()

    own = pl.pallas_call(
        take,
        out_shape=pltpu.VMEM(features.shape, features.dtype),
        in_specs=[HBM],
        out_specs=VMEM,
        scratch_shapes=[pltpu.SemaphoreType.DMA(())],
        compiler_params=pltpu.CompilerParams(vmem_limit_bytes=LIMIT),
        name="take",
    )(pltpu.with_memory_space_constraint(features, pltpu.HBM))

    def kernel(own_ref, partner_ref, out_ref):
        right = lax.axis_index("row") == 0
        for which, ref in enumerate((own_ref, partner_ref)):
            for frame in range(frames):
                for i in range(tile_rows):
                    for b in range(batch):
                        row = ref[b, frame, i].astype(F32)
                        side = jnp.where(right, row[tile_cols - HALO :], row[:HALO])
                        out_ref[which, frame, i, :, pl.ds(b * channels, channels)] = side.astype(BF)

    edge = pl.pallas_call(
        kernel,
        out_shape=jax.ShapeDtypeStruct((2, frames, tile_rows, HALO, batch * channels), BF),
        in_specs=[VMEM, VMEM],
        out_specs=VMEM,
        compiler_params=pltpu.CompilerParams(vmem_limit_bytes=LIMIT),
        name="edge",
    )(own, partner)
    up = list(range(cols))
    ring = up + [cols + c for c in reversed(up)]
    pairs = [(ring[i], ring[(i + 1) % len(ring)]) for i in range(len(ring))]
    side = lax.ppermute(edge, ("row", "col"), pairs)
    other = lax.ppermute(side, "row", [(0, 1), (1, 0)])
    return [own, partner, side, other]


def sigmoid(x):
    return 0.5 * jnp.tanh(0.5 * x) + 0.5


class Plan:
    def __init__(self, weight, bias, height, channels, batch, tile_rows, tile_cols, row_halo):
        self.weight, self.bias = weight, bias
        self.height, self.channels, self.batch = height, channels, batch
        self.tile_rows, self.tile_cols, self.row_halo = tile_rows, tile_cols, row_halo

    def lanes(self):
        return [(k, min(LANES, self.channels - k)) for k in range(0, self.channels, LANES)]

    def load(self, ref, index, info, stage_ref, turn_ref, cols):
        channels, height = self.channels, self.height
        pixels = cols * height
        if not isinstance(ref, list):
            value = ref[...] if index is None else ref[index]
            if value.shape[-1] == channels:
                stage_ref[pl.ds(8, pixels), :] = value.astype(F32)
            else:
                half = pixels // 2
                for k in range(2):
                    part = value[:, k * channels : (k + 1) * channels]
                    stage_ref[pl.ds(8 + k * half, half), :] = part.astype(F32)
            return
        own, partner, side, other = ref
        rows, place, tile_cols = self.tile_rows, info.place, self.tile_cols
        first = place == 0
        left, right = info.col > 0, info.col < info.last_col

        def put(value, row, col):
            count = value.shape[0]
            for n, (lane, width) in enumerate(self.lanes()):
                part = value[:, lane : lane + width]
                if width < LANES:
                    part = jnp.concatenate([part, jnp.zeros((count, LANES - width), F32)], axis=1)
                turn_ref[n, pl.ds(col * height + row, count, stride=height), :] = part

        def mine(piece, k, i):
            value = piece[k, index, i].astype(F32)
            return jnp.where(first, value[:, :channels], value[:, channels:])

        for i in range(rows):
            a, b = own[place, index, i].astype(F32), partner[place, index, i].astype(F32)
            put(jnp.where(first, a, b), i, HALO)
            put(jnp.where(first, b, a), rows + i, HALO)
            for k in range(2):
                a, b = mine(side, k, i), mine(other, k, i)
                put(jnp.where(left, jnp.where(first, a, b), 0.0), k * rows + i, 0)
                put(jnp.where(right, jnp.where(first, b, a), 0.0), (1 - k) * rows + i, HALO + tile_cols)
        for n, (lane, width) in enumerate(self.lanes()):
            value = turn_ref[n, pl.ds(0, pixels), :]
            stage_ref[pl.ds(8, pixels), pl.ds(lane, width)] = value[:, :width]

    def spread(self, stage_ref, shift_ref, patch_ref, cols, out_cols):
        channels, height = self.channels, self.height
        inset = (cols - out_cols) // 2
        used = (out_cols + 2) * height
        start = 8 + (inset - 1) * height
        row = lax.broadcasted_iota(jnp.int32, (out_cols + 2, height, channels), 1)
        for k, offset in enumerate((-1, 1)):
            value = stage_ref[pl.ds(start + offset, used), :].reshape(out_cols + 2, height, channels)
            value = jnp.where(row == (0 if k == 0 else height - 1), 0.0, value)
            shift_ref[k, pl.ds(0, used), :] = value.reshape(used, channels)
        pixels = out_cols * height
        for tap in range(TAPS):
            row_tap, col_tap = tap // 3, tap % 3
            if row_tap == 1:
                value = stage_ref[pl.ds(start + col_tap * height, pixels), :]
            else:
                value = shift_ref[row_tap // 2, pl.ds(col_tap * height, pixels), :]
            patch_ref[pl.ds(0, pixels), pl.ds(tap * channels, channels)] = value.astype(BF)

    def product(self, weight_ref, part, patch_ref, cols):
        return jnp.dot(
            patch_ref[pl.ds(0, cols * self.height), :], weight_ref[part], preferred_element_type=F32
        )

    def update(self, info, gates, bias_ref, memory, cols, stage_ref, cell_ref):
        ch, height = self.channels, self.height
        halo = (cols - self.tile_cols) // 2
        pieces = [(0, halo, info.col > 0)]
        pieces += [(halo + c, 4, None) for c in range(0, self.tile_cols, 4)]
        pieces += [(cols - halo, halo, info.col < info.last_col)]

        def part(ref, ref_cols, col, count):
            return ref[pl.ds((col + (ref_cols - cols) // 2) * height, count * height), :]

        for col, count, inside in pieces:
            if count == 0:
                continue
            total = bias_ref[...]
            for ref, ref_cols in gates:
                total = total + part(ref, ref_cols, col, count)
            cell = sigmoid(total[:, :ch]) * jnp.tanh(total[:, 2 * ch : 3 * ch])
            if memory is not None:
                before = part(*memory, col, count).astype(F32)
                cell = cell + sigmoid(total[:, ch : 2 * ch]) * before
            hidden = sigmoid(total[:, 3 * ch :]) * jnp.tanh(cell)
            if inside is not None:
                hidden = jnp.where(inside, hidden, 0.0)
            if self.row_halo:
                row = lax.broadcasted_iota(jnp.int32, (count, height, ch), 1)
                top = jnp.where(info.group == 0, self.row_halo, 0)
                bottom = jnp.where(info.group == info.last_group, height - self.row_halo, height)
                hidden = hidden.reshape(count, height, ch)
                hidden = jnp.where((row >= top) & (row < bottom), hidden, 0.0)
                hidden = hidden.reshape(count * height, ch)
            stage_ref[pl.ds(8 + col * height, count * height), :] = hidden
            if cell_ref is not None:
                cell_ref[pl.ds(col * height, count * height), :] = cell

    def pack(self, source_ref, offset, cols, out_ref, out_cols):
        half, channels = out_cols * self.height // 2, self.channels
        start = offset + (cols - out_cols) // 2 * self.height
        for k in range(2):
            value = source_ref[pl.ds(start + k * half, half), :]
            out_ref[:, pl.ds(k * channels, channels)] = value.astype(BF)

    def tiles(self, info, stage_ref, turn_ref, cols, frame, outs):
        halo, pixels = (cols - self.tile_cols) // 2, self.tile_cols * self.height
        for n, (lane, width) in enumerate(self.lanes()):
            value = stage_ref[pl.ds(8 + halo * self.height, pixels), pl.ds(lane, width)]
            if width < LANES:
                value = jnp.concatenate([value, jnp.zeros((pixels, LANES - width), F32)], axis=1)
            turn_ref[n, pl.ds(0, pixels), :] = value
        for i in range(self.tile_rows):
            rows = []
            for b in range(self.batch):
                start = self.row_halo + b * self.tile_rows + i
                row = [
                    turn_ref[n, pl.ds(start, self.tile_cols, stride=self.height), :][:, :width]
                    for n, (_, width) in enumerate(self.lanes())
                ]
                rows.append(jnp.concatenate(row, axis=1))
            for k, out in enumerate(outs):
                value = rows[0]
                for b in range(1, self.batch):
                    value = jnp.where(lax.rem(info.place + k, self.batch) == b, rows[b], value)
                out[frame, i] = value.astype(BF)

    def scratch(self, widest, cols):
        pixels, channels = cols * self.height, self.channels
        return [
            pltpu.VMEM((widest * self.height + 16, channels), F32),
            pltpu.VMEM((2, (cols + 2) * self.height, channels), F32),
            pltpu.VMEM((pixels, TAPS * channels), BF),
            pltpu.VMEM((pixels, 4 * channels), F32),
            pltpu.VMEM((widest * self.height + 16, channels), F32),
            pltpu.VMEM((len(self.lanes()), widest * self.height, LANES), F32),
        ]

    def step(self, turn, terms, cols, gates_in=None, memory=None, keep=None, after=None, outs=(),
             both_cols=None, done=None, relay=None):
        channels, batch, height = self.channels, self.batch, self.height
        pixels = height * cols
        operands = [self.weight, self.bias]
        specs = [VMEM, VMEM]
        seen = {}

        def place_of(array):
            if array is None:
                return None
            if isinstance(array, list):
                return [place_of(a) for a in array]
            if id(array) not in seen:
                seen[id(array)] = len(operands)
                operands.append(array)
                specs.append(VMEM)
            return seen[id(array)]

        term_at = [place_of(t[0]) for t in terms]
        gates_at = place_of(gates_in[0]) if gates_in is not None else None
        memory_at = place_of(memory[0]) if memory is not None else None
        done_at = [[place_of(f[0]) for f in frames] for frames in done] if done else None
        relay_at = place_of(relay[1]) if relay is not None else None
        shapes, names = [], []

        def add(name, shape, dtype):
            shapes.append(jax.ShapeDtypeStruct(shape, dtype))
            names.append(name)

        for name in outs:
            if name == "hidden":
                add(name, (pixels // 2, 2 * channels), BF)
            elif name == "both":
                add(name, (2, both_cols * height // 2, 2 * channels), BF)
            elif name == "memory":
                add(name, (pixels, channels), F32)
            elif name == "tiles":
                for k in range(batch):
                    add(f"tile{k}", (len(done[0]), self.tile_rows, self.tile_cols, channels), BF)
        if keep is not None:
            add("keep", (pixels, 4 * channels), F32)
        if after is not None:
            add("after", (height * after[1], 4 * channels), F32)
        count = len(operands)
        widest = max([t[2] for t in terms] + [f[2] for frames in done or () for f in frames] + [cols])
        if memory is not None:
            widest = max(widest, memory[2])

        def kernel(*refs):
            ins, out = refs[:count], dict(zip(names, refs[count : count + len(shapes)]))
            stage_ref, shift_ref, patch_ref, sum_ref, before_ref, turn_ref = refs[count + len(shapes) :]
            weight_ref, bias_ref = ins[:2]
            info = Position(batch)

            def ref_of(at):
                return [ref_of(a) for a in at] if isinstance(at, list) else ins[at]

            @pl.when(info.section == turn)
            def _():
                total, last = None, None
                for n, ((_, index, span, part), at) in enumerate(zip(terms, term_at)):
                    if (at, index) != last:
                        self.load(ref_of(at), index, info, stage_ref, turn_ref, span)
                        self.spread(stage_ref, shift_ref, patch_ref, span, cols)
                    last = (at, index)
                    term = self.product(weight_ref, part, patch_ref, cols)
                    total = term if total is None else total + term
                    if keep == n + 1:
                        out["keep"][...] = total
                sum_ref[...] = total
                gates = [(sum_ref, cols)]
                if gates_in is not None:
                    gates.append((ins[gates_at], gates_in[1]))
                before = None
                if memory is not None:
                    ref = ins[memory_at]
                    if ref.shape[-1] == channels:
                        before = (ref, memory[2])
                    else:
                        self.load(ref, memory[1], info, before_ref, None, memory[2])
                        before = (before_ref.at[pl.ds(8, memory[2] * height), :], memory[2])
                both = out.get("both")
                cell_ref = out.get("memory", before_ref.at[pl.ds(0, pixels), :] if both is not None else None)
                self.update(info, gates, bias_ref, before, cols, stage_ref, cell_ref)
                if "hidden" in out:
                    self.pack(stage_ref, 8, cols, out["hidden"], cols)
                if both is not None:
                    self.pack(stage_ref, 8, cols, both.at[0], both_cols)
                    self.pack(cell_ref, 0, cols, both.at[1], both_cols)
                if after is not None:
                    self.spread(stage_ref, shift_ref, patch_ref, cols, after[1])
                    out["after"][...] = self.product(weight_ref, after[0], patch_ref, after[1])

            if relay is not None:

                @pl.when(info.section == relay[0])
                def _():
                    out["both"][...] = ins[relay_at][...]

            if done is not None:
                tile_refs = [out[f"tile{k}"] for k in range(batch)]
                for section, frames in enumerate(done):

                    @pl.when(info.section == section)
                    def _():
                        for frame, (array, index, span) in reversed(list(enumerate(frames))):
                            if array is not None:
                                source = ins[done_at[section][frame]]
                                self.load(source, index, info, stage_ref, None, span)
                            self.tiles(info, stage_ref, turn_ref, span, frame, tile_refs)

        return pl.pallas_call(
            kernel,
            out_shape=shapes,
            in_specs=specs,
            out_specs=[VMEM] * len(shapes),
            scratch_shapes=self.scratch(widest, cols),
            cost_estimate=self.cost(pixels, len(terms) + (after is not None)),
            compiler_params=pltpu.CompilerParams(vmem_limit_bytes=LIMIT),
        )(*operands)

    def cost(self, pixels, products):
        return pl.CostEstimate(
            flops=8 * pixels * TAPS * self.channels * self.channels * products,
            bytes_accessed=pixels * self.channels * 2, transcendentals=0,
        )

    def partial(self, turn, array, index, cols, out_cols, part):
        pixels, channels = self.height * out_cols, self.channels

        def kernel(weight_ref, in_ref, out_ref, stage_ref, shift_ref, patch_ref, *unused):
            info = Position(self.batch)

            @pl.when(info.section == turn)
            def _():
                self.load(in_ref, index, info, stage_ref, None, cols)
                self.spread(stage_ref, shift_ref, patch_ref, cols, out_cols)
                out_ref[...] = self.product(weight_ref, part, patch_ref, out_cols)

        return pl.pallas_call(
            kernel,
            out_shape=jax.ShapeDtypeStruct((pixels, 4 * channels), F32),
            in_specs=[VMEM, VMEM],
            out_specs=VMEM,
            scratch_shapes=self.scratch(cols, out_cols),
            cost_estimate=self.cost(pixels, 1),
            compiler_params=pltpu.CompilerParams(vmem_limit_bytes=LIMIT),
        )(self.weight, array)


def joined_weight(shards, channels):
    per = 2 * TAPS // len(shards)
    rows, columns = shards[0].shape[0] * len(shards) // 2, shards[0].shape[1]
    joined = None
    for which, shard in enumerate(shards):

        def kernel(*refs):
            in_ref, out_ref, sems = refs[-3:]

            def copy(block):
                src = in_ref.at[pl.ds(block % per * channels, channels), :]
                dst = out_ref.at[block % 2, pl.ds(block // 2 * channels, channels), :]
                return pltpu.make_async_copy(src, dst, sems.at[block % per])

            owner = lax.rem(lax.axis_index("row") + which, len(shards))
            for index in range(len(shards)):

                @pl.when(owner == index)
                def _():
                    for block in range(index * per, index * per + per):
                        copy(block).start()
                    for block in range(index * per, index * per + per):
                        copy(block).wait()

        source = pltpu.with_memory_space_constraint(shard, pltpu.HBM) if which == 0 else shard
        joined = pl.pallas_call(
            kernel,
            out_shape=pltpu.VMEM((2, rows, columns), BF),
            in_specs=([] if joined is None else [VMEM])
            + [HBM if which == 0 else pl.BlockSpec(memory_space=pl.ANY)],
            out_specs=VMEM,
            scratch_shapes=[pltpu.SemaphoreType.DMA((per,))],
            input_output_aliases={} if joined is None else {0: 0},
            compiler_params=pltpu.CompilerParams(vmem_limit_bytes=LIMIT),
        )(*([] if joined is None else [joined]), source)
    return joined


def window_levels(features, gate_weight, gate_bias):
    batch, frames, tile_rows, tile_cols, channels = features.shape
    _, row, _ = (lax.axis_index(a) for a in ("section", "row", "col"))
    row_size = lax.axis_size("row")
    groups = row_size // batch
    place = row % batch
    row_halo = HALO if groups > 1 else 0
    height = tile_rows * batch + 2 * row_halo
    wide, good = tile_cols + 2 * HALO, [tile_cols + 2 * k for k in range(STEPS)]

    if groups == 1 and batch == 2:
        pieces = paired_pieces(features)
    else:
        window = gather_sequence(features)
        if groups > 1:
            window = with_halo(window, "row", 1, batch)
        window = jnp.swapaxes(with_halo(window, "col", 2, 1), 1, 2)
        pieces = window.reshape(frames, height * wide, channels)

    own_weight = gate_weight[0]
    if row_size == 2 and own_weight.shape[0] % channels == 0:
        shards = [own_weight, lax.ppermute(own_weight, "row", [(0, 1), (1, 0)])]
    else:
        shards = [lax.all_gather(own_weight, "row", axis=0, tiled=True)]

    weight = joined_weight(shards, channels)
    plan = Plan(weight, gate_bias, height, channels, batch, tile_rows, tile_cols, row_halo)

    h00, c00 = plan.step(0, [(pieces, 0, wide, 0)], good[5], outs=("hidden", "memory"))
    x10 = section_send(h00, (0, 1, 3, 2))
    h01, s01 = plan.step(
        0, [(pieces, 1, wide, 0), (h00, None, good[5], 1)], good[4], memory=(c00, None, good[5]),
        outs=("hidden", "both"), both_cols=good[3],
    )
    x11 = section_send(h01, (0, 1, 3, 2))
    h10, c10, p11 = plan.step(
        1, [(x10, None, good[5], 0)], good[4], after=(1, good[3]), outs=("hidden", "memory")
    )
    (s11,) = plan.step(
        1, [(x11, None, good[4], 0)], good[3], gates_in=(p11, good[3]), memory=(c10, None, good[4]),
        outs=("both",), both_cols=good[3], relay=(0, s01),
    )
    x2 = section_send(s11, (1, 2, 0, 3))
    p30 = plan.partial(3, x2, 0, good[3], good[1], 1)
    h20, c20, p21 = plan.step(
        2, [(x2, 0, good[3], 0), (x2, 0, good[3], 1)], good[2], memory=(x2, 1, good[3]), keep=1,
        outs=("hidden", "memory"),
    )
    x30 = section_send(h20, (2, 3), (0, 1))
    (h21,) = plan.step(
        2, [(h20, None, good[2], 1)], good[1], gates_in=(p21, good[2]), memory=(c20, None, good[2]),
        outs=("hidden",),
    )
    x31 = section_send(h21, (2, 3), (0, 1))
    h30, c30, p31 = plan.step(
        3, [(x30, None, good[2], 0)], good[1], gates_in=(p30, good[1]), memory=(x2, 1, good[3]),
        after=(1, good[0]), outs=("hidden", "memory"),
    )
    tiles = plan.step(
        3, [(x31, None, good[1], 0)], good[0], gates_in=(p31, good[0]), memory=(c30, None, good[1]),
        outs=("tiles",),
        done=(
            ((h00, None, good[5]), (h01, None, good[4])),
            ((h10, None, good[4]), (s11, 0, good[3])),
            ((h20, None, good[2]), (h21, None, good[1])),
            ((h30, None, good[1]), (None, None, good[0])),
        ),
    )

    parts = [tiles[0]]
    for k in range(1, batch):
        parts.append(lax.ppermute(tiles[k], "row", group_pairs(row_size, batch, k)))
    result = []
    for q in range(batch):
        chosen = parts[0]
        for k in range(1, batch):
            chosen = jnp.where((place - q) % batch == k, parts[k], chosen)
        result.append(chosen)
    return jnp.stack(result)[None]


def solution(mesh):
    return jax.shard_map(
        window_levels,
        mesh=mesh,
        in_specs=(P(None, None, "row", "col", None), P("section", "row", None), P("section", None)),
        out_specs=P("section", None, None, "row", "col", None),
        check_vma=False,
    )
```

```python
import jax
import jax.numpy as jnp
from jax import lax
from jax.experimental import pallas as pl
from jax.experimental.pallas import tpu as pltpu
from jax.sharding import PartitionSpec as P


HALO = 8
TAPS = 9
LANES = 128
BF = jnp.bfloat16
F32 = jnp.float32
VMEM = pl.BlockSpec(memory_space=pltpu.VMEM)
HBM = pl.BlockSpec(memory_space=pltpu.HBM)
LIMIT = 12 * 1024 * 1024
STEPS = 6


def section_send(block, *routes):
    pairs = [(r[i], r[(i + 1) % len(r)]) for r in routes for i in range(len(r))]
    return lax.ppermute(block, "section", pairs)


class Position:
    def __init__(self, batch):
        row = lax.axis_index("row")
        self.section, self.col, self.last_col = (
            lax.axis_index("section"), lax.axis_index("col"), lax.axis_size("col") - 1,
        )
        self.place, self.group = lax.rem(row, batch), lax.div(row, batch)
        self.last_group = lax.axis_size("row") // batch - 1


def group_pairs(size, batch, k):
    return [(i, i - i % batch + (i % batch + k) % batch) for i in range(size)]


def gather_sequence(features):
    batch = features.shape[0]
    size = lax.axis_size("row")
    place = lax.axis_index("row") % batch
    parts = [lax.dynamic_index_in_dim(features, place, 0, keepdims=False)]
    for k in range(1, batch):
        sent = lax.dynamic_index_in_dim(features, (place + k) % batch, 0, keepdims=False)
        parts.append(lax.ppermute(sent, "row", group_pairs(size, batch, k)))
    stacked = jnp.stack(parts)
    blocks = [
        lax.dynamic_index_in_dim(stacked, (place - q) % batch, 0, keepdims=False)
        for q in range(batch)
    ]
    return jnp.concatenate(blocks, axis=1)


def with_halo(array, axis, dim, stride):
    size, length = lax.axis_size(axis), array.shape[dim]
    up = [(i, i + stride) for i in range(size - stride)]
    down = [(j, i) for i, j in up]
    last = lax.slice_in_dim(array, length - HALO, length, axis=dim)
    first = lax.slice_in_dim(array, 0, HALO, axis=dim)
    before = lax.ppermute(last, axis, up)
    after = lax.ppermute(first, axis, down)
    return jnp.concatenate([before, array, after], axis=dim)


def paired_pieces(features):
    batch, frames, tile_rows, tile_cols, channels = features.shape
    cols = lax.axis_size("col")
    partner = lax.ppermute(features, "row", [(0, 1), (1, 0)])

    def take(in_ref, out_ref, sem):
        copy = pltpu.make_async_copy(in_ref, out_ref, sem)
        copy.start()
        copy.wait()

    own = pl.pallas_call(
        take,
        out_shape=pltpu.VMEM(features.shape, features.dtype),
        in_specs=[HBM],
        out_specs=VMEM,
        scratch_shapes=[pltpu.SemaphoreType.DMA(())],
        compiler_params=pltpu.CompilerParams(vmem_limit_bytes=LIMIT),
        name="take",
    )(pltpu.with_memory_space_constraint(features, pltpu.HBM))

    def kernel(own_ref, partner_ref, out_ref):
        right = lax.axis_index("row") == 0
        for which, ref in enumerate((own_ref, partner_ref)):
            for frame in range(frames):
                for i in range(tile_rows):
                    for b in range(batch):
                        row = ref[b, frame, i].astype(F32)
                        side = jnp.where(right, row[tile_cols - HALO :], row[:HALO])
                        out_ref[which, frame, i, :, pl.ds(b * channels, channels)] = side.astype(BF)

    edge = pl.pallas_call(
        kernel,
        out_shape=jax.ShapeDtypeStruct((2, frames, tile_rows, HALO, batch * channels), BF),
        in_specs=[VMEM, VMEM],
        out_specs=VMEM,
        compiler_params=pltpu.CompilerParams(vmem_limit_bytes=LIMIT),
        name="edge",
    )(own, partner)
    up = list(range(cols))
    ring = up + [cols + c for c in reversed(up)]
    pairs = [(ring[i], ring[(i + 1) % len(ring)]) for i in range(len(ring))]
    side = lax.ppermute(edge, ("row", "col"), pairs)
    other = lax.ppermute(side, "row", [(0, 1), (1, 0)])
    return [own, partner, side, other]


def sigmoid(x):
    return 0.5 * jnp.tanh(0.5 * x) + 0.5


class Plan:
    def __init__(self, weight, bias, height, channels, batch, tile_rows, tile_cols, row_halo):
        self.weight, self.bias = weight, bias
        self.height, self.channels, self.batch = height, channels, batch
        self.tile_rows, self.tile_cols, self.row_halo = tile_rows, tile_cols, row_halo

    def lanes(self):
        return [(k, min(LANES, self.channels - k)) for k in range(0, self.channels, LANES)]

    def load(self, ref, index, info, stage_ref, turn_ref, cols):
        channels, height = self.channels, self.height
        pixels = cols * height
        if not isinstance(ref, list):
            value = ref[...] if index is None else ref[index]
            if value.shape[-1] == channels:
                stage_ref[pl.ds(8, pixels), :] = value.astype(F32)
            else:
                half = pixels // 2
                for k in range(2):
                    part = value[:, k * channels : (k + 1) * channels]
                    stage_ref[pl.ds(8 + k * half, half), :] = part.astype(F32)
            return
        own, partner, side, other = ref
        rows, place, tile_cols = self.tile_rows, info.place, self.tile_cols
        first = place == 0
        left, right = info.col > 0, info.col < info.last_col

        def put(value, row, col):
            count = value.shape[0]
            for n, (lane, width) in enumerate(self.lanes()):
                part = value[:, lane : lane + width]
                if width < LANES:
                    part = jnp.concatenate([part, jnp.zeros((count, LANES - width), F32)], axis=1)
                turn_ref[n, pl.ds(col * height + row, count, stride=height), :] = part

        def mine(piece, k, i):
            value = piece[k, index, i].astype(F32)
            return jnp.where(first, value[:, :channels], value[:, channels:])

        for i in range(rows):
            a, b = own[place, index, i].astype(F32), partner[place, index, i].astype(F32)
            put(jnp.where(first, a, b), i, HALO)
            put(jnp.where(first, b, a), rows + i, HALO)
            for k in range(2):
                a, b = mine(side, k, i), mine(other, k, i)
                put(jnp.where(left, jnp.where(first, a, b), 0.0), k * rows + i, 0)
                put(jnp.where(right, jnp.where(first, b, a), 0.0), (1 - k) * rows + i, HALO + tile_cols)
        for n, (lane, width) in enumerate(self.lanes()):
            value = turn_ref[n, pl.ds(0, pixels), :]
            stage_ref[pl.ds(8, pixels), pl.ds(lane, width)] = value[:, :width]

    def spread(self, stage_ref, shift_ref, patch_ref, cols, out_cols):
        channels, height = self.channels, self.height
        inset = (cols - out_cols) // 2
        used = (out_cols + 2) * height
        start = 8 + (inset - 1) * height
        row = lax.broadcasted_iota(jnp.int32, (out_cols + 2, height, channels), 1)
        for k, offset in enumerate((-1, 1)):
            value = stage_ref[pl.ds(start + offset, used), :].reshape(out_cols + 2, height, channels)
            value = jnp.where(row == (0 if k == 0 else height - 1), 0.0, value)
            shift_ref[k, pl.ds(0, used), :] = value.reshape(used, channels)
        pixels = out_cols * height
        for tap in range(TAPS):
            row_tap, col_tap = tap // 3, tap % 3
            if row_tap == 1:
                value = stage_ref[pl.ds(start + col_tap * height, pixels), :]
            else:
                value = shift_ref[row_tap // 2, pl.ds(col_tap * height, pixels), :]
            patch_ref[pl.ds(0, pixels), pl.ds(tap * channels, channels)] = value.astype(BF)

    def ranges(self):
        split = self.channels // LANES * LANES * 4
        return (0, split), (split, 4 * self.channels - split)

    def product(self, weight_ref, part, patch_ref, cols, lane, width):
        return jnp.dot(
            patch_ref[pl.ds(0, cols * self.height), :],
            weight_ref[part, :, pl.ds(lane, width)],
            preferred_element_type=F32,
        )

    def cell(self, total, before):
        width = total.shape[-1] // 4
        if width % LANES == 0:
            gate = [total[:, k * width : (k + 1) * width] for k in range(4)]
            cell = sigmoid(gate[0]) * jnp.tanh(gate[2])
            if before is not None:
                cell = cell + sigmoid(gate[1]) * before
            return sigmoid(gate[3]) * jnp.tanh(cell), cell
        first, second = sigmoid(total[:, : 2 * width]), total[:, 2 * width :]
        low = lax.broadcasted_iota(jnp.int32, second.shape, 1) < width
        scale = jnp.where(low, 1.0, 0.5)
        second = scale * jnp.tanh(scale * second) + jnp.where(low, 0.0, 0.5)
        cell = (first * second)[:, :width]
        if before is not None:
            cell = cell + pltpu.roll(first, width, 1)[:, :width] * before
        return pltpu.roll(second, width, 1)[:, :width] * jnp.tanh(cell), cell

    def update(self, info, gates, bias_ref, memory, cols, stage_ref, cell_ref, lane, width):
        ch, height = width // 4, self.height
        first = lane // 4
        bias = gate_order(bias_ref[...], self.channels)[:, lane : lane + width]
        halo = (cols - self.tile_cols) // 2
        pieces = [(0, halo, info.col > 0)]
        pieces += [(halo + c, 4, None) for c in range(0, self.tile_cols, 4)]
        pieces += [(cols - halo, halo, info.col < info.last_col)]

        def part(ref, ref_cols, col, count, lane, width):
            start = (col + (ref_cols - cols) // 2) * height
            return ref[pl.ds(start, count * height), pl.ds(lane, width)]

        for col, count, inside in pieces:
            if count == 0:
                continue
            total = bias
            for ref, ref_cols in gates:
                total = total + part(ref, ref_cols, col, count, lane, width)
            before = None
            if memory is not None:
                before = part(*memory, col, count, first, ch).astype(F32)
            hidden, cell = self.cell(total, before)
            if inside is not None:
                hidden = jnp.where(inside, hidden, 0.0)
            if self.row_halo:
                row = lax.broadcasted_iota(jnp.int32, (count, height, ch), 1)
                top = jnp.where(info.group == 0, self.row_halo, 0)
                bottom = jnp.where(info.group == info.last_group, height - self.row_halo, height)
                hidden = hidden.reshape(count, height, ch)
                hidden = jnp.where((row >= top) & (row < bottom), hidden, 0.0)
                hidden = hidden.reshape(count * height, ch)
            stage_ref[pl.ds(8 + col * height, count * height), pl.ds(first, ch)] = hidden
            if cell_ref is not None:
                cell_ref[pl.ds(col * height, count * height), pl.ds(first, ch)] = cell

    def pack(self, source_ref, offset, cols, out_ref, out_cols):
        half, channels = out_cols * self.height // 2, self.channels
        start = offset + (cols - out_cols) // 2 * self.height
        for k in range(2):
            value = source_ref[pl.ds(start + k * half, half), :]
            out_ref[:, pl.ds(k * channels, channels)] = value.astype(BF)

    def tiles(self, info, stage_ref, turn_ref, cols, frame, outs):
        halo, pixels = (cols - self.tile_cols) // 2, self.tile_cols * self.height
        for n, (lane, width) in enumerate(self.lanes()):
            value = stage_ref[pl.ds(8 + halo * self.height, pixels), pl.ds(lane, width)]
            if width < LANES:
                value = jnp.concatenate([value, jnp.zeros((pixels, LANES - width), F32)], axis=1)
            turn_ref[n, pl.ds(0, pixels), :] = value
        for i in range(self.tile_rows):
            rows = []
            for b in range(self.batch):
                start = self.row_halo + b * self.tile_rows + i
                row = [
                    turn_ref[n, pl.ds(start, self.tile_cols, stride=self.height), :][:, :width]
                    for n, (_, width) in enumerate(self.lanes())
                ]
                rows.append(jnp.concatenate(row, axis=1))
            for k, out in enumerate(outs):
                value = rows[0]
                for b in range(1, self.batch):
                    value = jnp.where(lax.rem(info.place + k, self.batch) == b, rows[b], value)
                out[frame, i] = value.astype(BF)

    def scratch(self, widest, cols, patches=1):
        pixels, channels = cols * self.height, self.channels
        return [
            pltpu.VMEM((widest * self.height + 16, channels), F32),
            pltpu.VMEM((2, (cols + 2) * self.height, channels), F32),
            pltpu.VMEM((pixels, 4 * channels), F32),
            pltpu.VMEM((widest * self.height + 16, channels), F32),
            pltpu.VMEM((len(self.lanes()), widest * self.height, LANES), F32),
        ] + [pltpu.VMEM((pixels, TAPS * channels), BF)] * patches

    def step(self, turn, terms, cols, gates_in=None, memory=None, keep=None, after=None, outs=(),
             both_cols=None, done=None, relay=None):
        channels, batch, height = self.channels, self.batch, self.height
        pixels = height * cols
        operands = [self.weight, self.bias]
        specs = [VMEM, VMEM]
        seen = {}

        def place_of(array):
            if array is None:
                return None
            if isinstance(array, list):
                return [place_of(a) for a in array]
            if id(array) not in seen:
                seen[id(array)] = len(operands)
                operands.append(array)
                specs.append(VMEM)
            return seen[id(array)]

        term_at = [place_of(t[0]) for t in terms]
        gates_at = place_of(gates_in[0]) if gates_in is not None else None
        memory_at = place_of(memory[0]) if memory is not None else None
        done_at = [[place_of(f[0]) for f in frames] for frames in done] if done else None
        relay_at = place_of(relay[1]) if relay is not None else None
        shapes, names = [], []

        def add(name, shape, dtype):
            shapes.append(jax.ShapeDtypeStruct(shape, dtype))
            names.append(name)

        for name in outs:
            if name == "hidden":
                add(name, (pixels // 2, 2 * channels), BF)
            elif name == "both":
                add(name, (2, both_cols * height // 2, 2 * channels), BF)
            elif name == "memory":
                add(name, (pixels, channels), F32)
            elif name == "tiles":
                for k in range(batch):
                    add(f"tile{k}", (len(done[0]), self.tile_rows, self.tile_cols, channels), BF)
        if keep is not None:
            add("keep", (pixels, 4 * channels), F32)
        if after is not None:
            add("after", (height * after[1], 4 * channels), F32)
        count = len(operands)
        widest = max([t[2] for t in terms] + [f[2] for frames in done or () for f in frames] + [cols])
        if memory is not None:
            widest = max(widest, memory[2])

        def kernel(*refs):
            ins, out = refs[:count], dict(zip(names, refs[count : count + len(shapes)]))
            stage_ref, shift_ref, sum_ref, before_ref, turn_ref, *patch_refs = refs[
                count + len(shapes) :
            ]
            weight_ref, bias_ref = ins[:2]
            info = Position(batch)

            def ref_of(at):
                return [ref_of(a) for a in at] if isinstance(at, list) else ins[at]

            @pl.when(info.section == turn)
            def _():
                last, patches = None, []
                for (_, index, span, part), at in zip(terms, term_at):
                    if (at, index) != last:
                        patches.append(patch_refs[len(patches)])
                        self.load(ref_of(at), index, info, stage_ref, turn_ref, span)
                        self.spread(stage_ref, shift_ref, patches[-1], span, cols)
                    else:
                        patches.append(patches[-1])
                    last = (at, index)
                for lane, wide in self.ranges():
                    total = None
                    for n, (_, _, _, part) in enumerate(terms):
                        term = self.product(weight_ref, part, patches[n], cols, lane, wide)
                        total = term if total is None else total + term
                        if keep == n + 1:
                            out["keep"][:, pl.ds(lane, wide)] = total
                    sum_ref[:, pl.ds(lane, wide)] = total
                gates = [(sum_ref, cols)]
                if gates_in is not None:
                    gates.append((ins[gates_at], gates_in[1]))
                before = None
                if memory is not None:
                    ref = ins[memory_at]
                    if ref.shape[-1] == channels:
                        before = (ref, memory[2])
                    else:
                        self.load(ref, memory[1], info, before_ref, None, memory[2])
                        before = (before_ref.at[pl.ds(8, memory[2] * height), :], memory[2])
                both = out.get("both")
                cell_ref = out.get("memory", before_ref.at[pl.ds(0, pixels), :] if both is not None else None)
                for lane, wide in self.ranges():
                    self.update(
                        info, gates, bias_ref, before, cols, stage_ref, cell_ref, lane, wide
                    )
                if "hidden" in out:
                    self.pack(stage_ref, 8, cols, out["hidden"], cols)
                if both is not None:
                    self.pack(stage_ref, 8, cols, both.at[0], both_cols)
                    self.pack(cell_ref, 0, cols, both.at[1], both_cols)
                if after is not None:
                    self.spread(stage_ref, shift_ref, patch_refs[0], cols, after[1])
                    out["after"][...] = self.product(
                        weight_ref, after[0], patch_refs[0], after[1], 0, 4 * channels
                    )

            if relay is not None:

                @pl.when(info.section == relay[0])
                def _():
                    out["both"][...] = ins[relay_at][...]

            if done is not None:
                tile_refs = [out[f"tile{k}"] for k in range(batch)]
                for section, frames in enumerate(done):

                    @pl.when(info.section == section)
                    def _():
                        for frame, (array, index, span) in reversed(list(enumerate(frames))):
                            if array is not None:
                                source = ins[done_at[section][frame]]
                                self.load(source, index, info, stage_ref, None, span)
                            self.tiles(info, stage_ref, turn_ref, span, frame, tile_refs)

        return pl.pallas_call(
            kernel,
            out_shape=shapes,
            in_specs=specs,
            out_specs=[VMEM] * len(shapes),
            scratch_shapes=self.scratch(widest, cols, len(set(map(id, (t[0] for t in terms))))),
            cost_estimate=self.cost(pixels, len(terms) + (after is not None)),
            compiler_params=pltpu.CompilerParams(vmem_limit_bytes=LIMIT),
        )(*operands)

    def cost(self, pixels, products):
        return pl.CostEstimate(
            flops=8 * pixels * TAPS * self.channels * self.channels * products,
            bytes_accessed=pixels * self.channels * 2, transcendentals=0,
        )

    def partial(self, turn, array, index, cols, out_cols, part):
        pixels, channels = self.height * out_cols, self.channels

        def kernel(weight_ref, in_ref, out_ref, stage_ref, shift_ref, *rest):
            patch_ref = rest[-1]
            info = Position(self.batch)

            @pl.when(info.section == turn)
            def _():
                self.load(in_ref, index, info, stage_ref, None, cols)
                self.spread(stage_ref, shift_ref, patch_ref, cols, out_cols)
                out_ref[...] = self.product(
                    weight_ref, part, patch_ref, out_cols, 0, 4 * channels
                )

        return pl.pallas_call(
            kernel,
            out_shape=jax.ShapeDtypeStruct((pixels, 4 * channels), F32),
            in_specs=[VMEM, VMEM],
            out_specs=VMEM,
            scratch_shapes=self.scratch(cols, out_cols),
            cost_estimate=self.cost(pixels, 1),
            compiler_params=pltpu.CompilerParams(vmem_limit_bytes=LIMIT),
        )(self.weight, array)


def gate_order(value, channels):
    whole = channels // LANES * LANES
    gates = [value[:, k * channels : (k + 1) * channels] for k in range(4)]
    return jnp.concatenate([g[:, :whole] for g in gates] + [g[:, whole:] for g in gates], axis=1)


def joined_weight(shards, channels):
    per = 2 * TAPS // len(shards)
    rows, columns = shards[0].shape[0] * len(shards) // 2, shards[0].shape[1]
    joined = None
    for which, shard in enumerate(shards):

        def kernel(*refs, which=which):
            first = lax.rem(lax.axis_index("row") + which, len(shards)) * per
            if which == 0:
                in_ref, out_ref, held_ref, sems = refs

                def copy(j):
                    block = pl.ds(j * channels, channels)
                    return pltpu.make_async_copy(in_ref.at[block], held_ref.at[block], sems.at[j])

                for j in range(per):
                    copy(j).start()
            else:
                _, held_ref, out_ref = refs

            for j in range(per):
                if which == 0:
                    copy(j).wait()
                block = first + j
                value = gate_order(held_ref[pl.ds(j * channels, channels), :], channels)
                tap = pl.multiple_of(lax.div(block, 2) * channels, 16)
                out_ref[lax.rem(block, 2), pl.ds(tap, channels), :] = value

        source = pltpu.with_memory_space_constraint(shard, pltpu.HBM) if which == 0 else shard
        scratch = [pltpu.VMEM(shard.shape, BF), pltpu.SemaphoreType.DMA((per,))]
        joined = pl.pallas_call(
            kernel,
            out_shape=pltpu.VMEM((2, rows, columns), BF),
            in_specs=[HBM] if joined is None else [VMEM, VMEM],
            out_specs=VMEM,
            scratch_shapes=scratch if which == 0 else [],
            input_output_aliases={} if joined is None else {0: 0},
            compiler_params=pltpu.CompilerParams(vmem_limit_bytes=LIMIT),
        )(*([] if joined is None else [joined]), source)
    return joined


def window_levels(features, gate_weight, gate_bias):
    batch, frames, tile_rows, tile_cols, channels = features.shape
    _, row, _ = (lax.axis_index(a) for a in ("section", "row", "col"))
    row_size = lax.axis_size("row")
    groups = row_size // batch
    place = row % batch
    row_halo = HALO if groups > 1 else 0
    height = tile_rows * batch + 2 * row_halo
    wide, good = tile_cols + 2 * HALO, [tile_cols + 2 * k for k in range(STEPS)]

    if groups == 1 and batch == 2:
        pieces = paired_pieces(features)
    else:
        window = gather_sequence(features)
        if groups > 1:
            window = with_halo(window, "row", 1, batch)
        window = jnp.swapaxes(with_halo(window, "col", 2, 1), 1, 2)
        pieces = window.reshape(frames, height * wide, channels)

    own_weight = gate_weight[0]
    if row_size == 2 and own_weight.shape[0] % channels == 0:
        shards = [own_weight, lax.ppermute(own_weight, "row", [(0, 1), (1, 0)])]
    else:
        shards = [lax.all_gather(own_weight, "row", axis=0, tiled=True)]

    weight = joined_weight(shards, channels)
    weight = pltpu.with_memory_space_constraint(weight, pltpu.VMEM)
    plan = Plan(weight, gate_bias, height, channels, batch, tile_rows, tile_cols, row_halo)

    h00, c00 = plan.step(0, [(pieces, 0, wide, 0)], good[5], outs=("hidden", "memory"))
    x10 = section_send(h00, (0, 1, 3, 2))
    h01, s01 = plan.step(
        0, [(pieces, 1, wide, 0), (h00, None, good[5], 1)], good[4], memory=(c00, None, good[5]),
        outs=("hidden", "both"), both_cols=good[3],
    )
    x11 = section_send(h01, (0, 1, 3, 2))
    h10, c10, p11 = plan.step(
        1, [(x10, None, good[5], 0)], good[4], after=(1, good[3]), outs=("hidden", "memory")
    )
    (s11,) = plan.step(
        1, [(x11, None, good[4], 0)], good[3], gates_in=(p11, good[3]), memory=(c10, None, good[4]),
        outs=("both",), both_cols=good[3], relay=(0, s01),
    )
    x2 = section_send(s11, (1, 2, 0, 3))
    p30 = plan.partial(3, x2, 0, good[3], good[1], 1)
    h20, c20, p21 = plan.step(
        2, [(x2, 0, good[3], 0), (x2, 0, good[3], 1)], good[2], memory=(x2, 1, good[3]), keep=1,
        outs=("hidden", "memory"),
    )
    x30 = section_send(h20, (2, 3), (0, 1))
    (h21,) = plan.step(
        2, [(h20, None, good[2], 1)], good[1], gates_in=(p21, good[2]), memory=(c20, None, good[2]),
        outs=("hidden",),
    )
    x31 = section_send(h21, (2, 3), (0, 1))
    h30, c30, p31 = plan.step(
        3, [(x30, None, good[2], 0)], good[1], gates_in=(p30, good[1]), memory=(x2, 1, good[3]),
        after=(1, good[0]), outs=("hidden", "memory"),
    )
    tiles = plan.step(
        3, [(x31, None, good[1], 0)], good[0], gates_in=(p31, good[0]), memory=(c30, None, good[1]),
        outs=("tiles",),
        done=(
            ((h00, None, good[5]), (h01, None, good[4])),
            ((h10, None, good[4]), (s11, 0, good[3])),
            ((h20, None, good[2]), (h21, None, good[1])),
            ((h30, None, good[1]), (None, None, good[0])),
        ),
    )

    parts = [tiles[0]]
    for k in range(1, batch):
        parts.append(lax.ppermute(tiles[k], "row", group_pairs(row_size, batch, k)))
    result = []
    for q in range(batch):
        chosen = parts[0]
        for k in range(1, batch):
            chosen = jnp.where((place - q) % batch == k, parts[k], chosen)
        result.append(chosen)
    return jnp.stack(result)[None]


def solution(mesh):
    return jax.shard_map(
        window_levels,
        mesh=mesh,
        in_specs=(P(None, None, "row", "col", None), P("section", "row", None), P("section", None)),
        out_specs=P("section", None, None, "row", "col", None),
        check_vma=False,
    )
```

```python
import jax
import jax.numpy as jnp
from jax import lax
from jax.experimental import pallas as pl
from jax.experimental.pallas import tpu as pltpu
from jax.sharding import PartitionSpec as P


HALO = 8
TAPS = 9
LANES = 128
BF = jnp.bfloat16
F32 = jnp.float32
VMEM = pl.BlockSpec(memory_space=pltpu.VMEM)
HBM = pl.BlockSpec(memory_space=pltpu.HBM)
LIMIT = 12 * 1024 * 1024
STEPS = 6


def section_send(block, batch, *routes):
    size = lax.axis_size("row")
    pairs = []
    for route in routes:
        for i, source in enumerate(route):
            target = route[(i + 1) % len(route)]
            for row in range(size):
                place = row % batch
                moved = row - place + (place + target - source) % batch
                pairs.append((source * size + row, target * size + moved))
    return lax.ppermute(block, ("section", "row"), pairs)


class Position:
    def __init__(self, batch):
        row = lax.axis_index("row")
        self.section, self.col, self.last_col = (
            lax.axis_index("section"), lax.axis_index("col"), lax.axis_size("col") - 1,
        )
        self.place, self.group = lax.rem(row, batch), lax.div(row, batch)
        self.last_group = lax.axis_size("row") // batch - 1


def group_pairs(size, batch, k):
    return [(i, i - i % batch + (i % batch + k) % batch) for i in range(size)]


def gather_sequence(features):
    batch = features.shape[0]
    size = lax.axis_size("row")
    place = lax.axis_index("row") % batch
    parts = [lax.dynamic_index_in_dim(features, place, 0, keepdims=False)]
    for k in range(1, batch):
        sent = lax.dynamic_index_in_dim(features, (place + k) % batch, 0, keepdims=False)
        parts.append(lax.ppermute(sent, "row", group_pairs(size, batch, k)))
    stacked = jnp.stack(parts)
    blocks = [
        lax.dynamic_index_in_dim(stacked, (place - q) % batch, 0, keepdims=False)
        for q in range(batch)
    ]
    return jnp.concatenate(blocks, axis=1)


def with_halo(array, axis, dim, stride):
    size, length = lax.axis_size(axis), array.shape[dim]
    up = [(i, i + stride) for i in range(size - stride)]
    down = [(j, i) for i, j in up]
    last = lax.slice_in_dim(array, length - HALO, length, axis=dim)
    first = lax.slice_in_dim(array, 0, HALO, axis=dim)
    before = lax.ppermute(last, axis, up)
    after = lax.ppermute(first, axis, down)
    return jnp.concatenate([before, array, after], axis=dim)


def paired_pieces(features):
    batch, frames, tile_rows, tile_cols, channels = features.shape
    cols = lax.axis_size("col")
    partner = lax.ppermute(features, "row", [(0, 1), (1, 0)])

    def take(in_ref, out_ref, sem):
        copy = pltpu.make_async_copy(in_ref, out_ref, sem)
        copy.start()
        copy.wait()

    own = pl.pallas_call(
        take,
        out_shape=pltpu.VMEM(features.shape, features.dtype),
        in_specs=[HBM],
        out_specs=VMEM,
        scratch_shapes=[pltpu.SemaphoreType.DMA(())],
        compiler_params=pltpu.CompilerParams(vmem_limit_bytes=LIMIT),
        name="take",
    )(pltpu.with_memory_space_constraint(features, pltpu.HBM))

    def kernel(own_ref, partner_ref, out_ref):
        right = lax.axis_index("row") == 0
        for which, ref in enumerate((own_ref, partner_ref)):
            for frame in range(frames):
                for i in range(tile_rows):
                    for b in range(batch):
                        row = ref[b, frame, i].astype(F32)
                        side = jnp.where(right, row[tile_cols - HALO :], row[:HALO])
                        out_ref[which, frame, i, :, pl.ds(b * channels, channels)] = side.astype(BF)

    edge = pl.pallas_call(
        kernel,
        out_shape=jax.ShapeDtypeStruct((2, frames, tile_rows, HALO, batch * channels), BF),
        in_specs=[VMEM, VMEM],
        out_specs=VMEM,
        compiler_params=pltpu.CompilerParams(vmem_limit_bytes=LIMIT),
        name="edge",
    )(own, partner)
    up = list(range(cols))
    ring = up + [cols + c for c in reversed(up)]
    pairs = [(ring[i], ring[(i + 1) % len(ring)]) for i in range(len(ring))]
    side = lax.ppermute(edge, ("row", "col"), pairs)
    other = lax.ppermute(side, "row", [(0, 1), (1, 0)])
    return [own, partner, side, other]


def sigmoid(x):
    return 0.5 * jnp.tanh(0.5 * x) + 0.5


class Plan:
    def __init__(self, weight, bias, height, channels, batch, tile_rows, tile_cols, row_halo):
        self.weight, self.bias = weight, bias
        self.height, self.channels, self.batch = height, channels, batch
        self.tile_rows, self.tile_cols, self.row_halo = tile_rows, tile_cols, row_halo

    def lanes(self):
        return [(k, min(LANES, self.channels - k)) for k in range(0, self.channels, LANES)]

    def load(self, ref, index, info, stage_ref, turn_ref, cols):
        channels, height = self.channels, self.height
        pixels = cols * height
        if not isinstance(ref, list):
            value = ref[...] if index is None else ref[index]
            if value.shape[-1] == channels:
                stage_ref[pl.ds(8, pixels), :] = value.astype(F32)
            else:
                half = pixels // 2
                for k in range(2):
                    part = value[:, k * channels : (k + 1) * channels]
                    stage_ref[pl.ds(8 + k * half, half), :] = part.astype(F32)
            return
        own, partner, side, other = ref
        rows, place, tile_cols = self.tile_rows, info.place, self.tile_cols
        first = place == 0
        left, right = info.col > 0, info.col < info.last_col

        def put(value, row, col):
            count = value.shape[0]
            for n, (lane, width) in enumerate(self.lanes()):
                part = value[:, lane : lane + width]
                if width < LANES:
                    part = jnp.concatenate([part, jnp.zeros((count, LANES - width), F32)], axis=1)
                turn_ref[n, pl.ds(col * height + row, count, stride=height), :] = part

        def mine(piece, k, i):
            value = piece[k, index, i].astype(F32)
            return jnp.where(first, value[:, :channels], value[:, channels:])

        for i in range(rows):
            a, b = own[place, index, i].astype(F32), partner[place, index, i].astype(F32)
            put(jnp.where(first, a, b), i, HALO)
            put(jnp.where(first, b, a), rows + i, HALO)
            for k in range(2):
                a, b = mine(side, k, i), mine(other, k, i)
                put(jnp.where(left, jnp.where(first, a, b), 0.0), k * rows + i, 0)
                put(jnp.where(right, jnp.where(first, b, a), 0.0), (1 - k) * rows + i, HALO + tile_cols)
        for n, (lane, width) in enumerate(self.lanes()):
            value = turn_ref[n, pl.ds(0, pixels), :]
            stage_ref[pl.ds(8, pixels), pl.ds(lane, width)] = value[:, :width]

    def spread(self, stage_ref, shift_ref, patch_ref, cols, out_cols):
        channels, height = self.channels, self.height
        inset = (cols - out_cols) // 2
        used = (out_cols + 2) * height
        start = 8 + (inset - 1) * height
        row = lax.broadcasted_iota(jnp.int32, (out_cols + 2, height, channels), 1)
        for k, offset in enumerate((-1, 1)):
            value = stage_ref[pl.ds(start + offset, used), :].reshape(out_cols + 2, height, channels)
            value = jnp.where(row == (0 if k == 0 else height - 1), 0.0, value)
            shift_ref[k, pl.ds(0, used), :] = value.reshape(used, channels)
        pixels = out_cols * height
        for tap in range(TAPS):
            row_tap, col_tap = tap // 3, tap % 3
            if row_tap == 1:
                value = stage_ref[pl.ds(start + col_tap * height, pixels), :]
            else:
                value = shift_ref[row_tap // 2, pl.ds(col_tap * height, pixels), :]
            patch_ref[pl.ds(0, pixels), pl.ds(tap * channels, channels)] = value.astype(BF)

    def ranges(self):
        split = self.channels // LANES * LANES * 4
        return (0, split), (split, 4 * self.channels - split)

    def product(self, weight_ref, part, patch_ref, cols, lane, width):
        return jnp.dot(
            patch_ref[pl.ds(0, cols * self.height), :],
            weight_ref[part, :, pl.ds(lane, width)],
            preferred_element_type=F32,
        )

    def cell(self, total, before):
        width = total.shape[-1] // 4
        if width % LANES == 0:
            gate = [total[:, k * width : (k + 1) * width] for k in range(4)]
            cell = sigmoid(gate[0]) * jnp.tanh(gate[2])
            if before is not None:
                cell = cell + sigmoid(gate[1]) * before
            return sigmoid(gate[3]) * jnp.tanh(cell), cell
        first, second = sigmoid(total[:, : 2 * width]), total[:, 2 * width :]
        low = lax.broadcasted_iota(jnp.int32, second.shape, 1) < width
        scale = jnp.where(low, 1.0, 0.5)
        second = scale * jnp.tanh(scale * second) + jnp.where(low, 0.0, 0.5)
        cell = (first * second)[:, :width]
        if before is not None:
            cell = cell + pltpu.roll(first, width, 1)[:, :width] * before
        return pltpu.roll(second, width, 1)[:, :width] * jnp.tanh(cell), cell

    def update(self, info, gates, bias_ref, memory, cols, stage_ref, cell_ref, lane, width):
        ch, height = width // 4, self.height
        first = lane // 4
        bias = gate_order(bias_ref[...], self.channels)[:, lane : lane + width]
        halo = (cols - self.tile_cols) // 2
        pieces = [(0, halo, info.col > 0)]
        pieces += [(halo + c, 4, None) for c in range(0, self.tile_cols, 4)]
        pieces += [(cols - halo, halo, info.col < info.last_col)]

        def part(ref, ref_cols, col, count, lane, width):
            start = (col + (ref_cols - cols) // 2) * height
            return ref[pl.ds(start, count * height), pl.ds(lane, width)]

        for col, count, inside in pieces:
            if count == 0:
                continue
            total = bias
            for ref, ref_cols in gates:
                total = total + part(ref, ref_cols, col, count, lane, width)
            before = None
            if memory is not None:
                before = part(*memory, col, count, first, ch).astype(F32)
            hidden, cell = self.cell(total, before)
            if inside is not None:
                hidden = jnp.where(inside, hidden, 0.0)
            if self.row_halo:
                row = lax.broadcasted_iota(jnp.int32, (count, height, ch), 1)
                top = jnp.where(info.group == 0, self.row_halo, 0)
                bottom = jnp.where(info.group == info.last_group, height - self.row_halo, height)
                hidden = hidden.reshape(count, height, ch)
                hidden = jnp.where((row >= top) & (row < bottom), hidden, 0.0)
                hidden = hidden.reshape(count * height, ch)
            stage_ref[pl.ds(8 + col * height, count * height), pl.ds(first, ch)] = hidden
            if cell_ref is not None:
                cell_ref[pl.ds(col * height, count * height), pl.ds(first, ch)] = cell

    def pack(self, source_ref, offset, cols, out_ref, out_cols):
        half, channels = out_cols * self.height // 2, self.channels
        start = offset + (cols - out_cols) // 2 * self.height
        for k in range(2):
            value = source_ref[pl.ds(start + k * half, half), :]
            out_ref[:, pl.ds(k * channels, channels)] = value.astype(BF)

    def tiles(self, info, stage_ref, turn_ref, cols, frame, outs):
        halo, pixels = (cols - self.tile_cols) // 2, self.tile_cols * self.height
        for n, (lane, width) in enumerate(self.lanes()):
            value = stage_ref[pl.ds(8 + halo * self.height, pixels), pl.ds(lane, width)]
            if width < LANES:
                value = jnp.concatenate([value, jnp.zeros((pixels, LANES - width), F32)], axis=1)
            turn_ref[n, pl.ds(0, pixels), :] = value
        for i in range(self.tile_rows):
            rows = []
            for b in range(self.batch):
                start = self.row_halo + b * self.tile_rows + i
                row = [
                    turn_ref[n, pl.ds(start, self.tile_cols, stride=self.height), :][:, :width]
                    for n, (_, width) in enumerate(self.lanes())
                ]
                rows.append(jnp.concatenate(row, axis=1))
            for k, out in enumerate(outs):
                value = rows[0]
                for b in range(1, self.batch):
                    value = jnp.where(lax.rem(info.place + k, self.batch) == b, rows[b], value)
                out[frame, i] = value.astype(BF)

    def scratch(self, widest, cols, patches=1):
        pixels, channels = cols * self.height, self.channels
        return [
            pltpu.VMEM((widest * self.height + 16, channels), F32),
            pltpu.VMEM((2, (cols + 2) * self.height, channels), F32),
            pltpu.VMEM((pixels, 4 * channels), F32),
            pltpu.VMEM((widest * self.height + 16, channels), F32),
            pltpu.VMEM((len(self.lanes()), widest * self.height, LANES), F32),
        ] + [pltpu.VMEM((pixels, TAPS * channels), BF)] * patches

    def step(self, turn, terms, cols, gates_in=None, memory=None, keep=None, after=None, outs=(),
             both_cols=None, done=None, relay=None):
        channels, batch, height = self.channels, self.batch, self.height
        pixels = height * cols
        operands = [self.weight, self.bias]
        specs = [VMEM, VMEM]
        seen = {}

        def place_of(array):
            if array is None:
                return None
            if isinstance(array, list):
                return [place_of(a) for a in array]
            if id(array) not in seen:
                seen[id(array)] = len(operands)
                operands.append(array)
                specs.append(VMEM)
            return seen[id(array)]

        term_at = [place_of(t[0]) for t in terms]
        gates_at = place_of(gates_in[0]) if gates_in is not None else None
        memory_at = place_of(memory[0]) if memory is not None else None
        done_at = [[place_of(f[0]) for f in frames] for frames in done] if done else None
        relay_at = place_of(relay[1]) if relay is not None else None
        shapes, names = [], []

        def add(name, shape, dtype):
            shapes.append(jax.ShapeDtypeStruct(shape, dtype))
            names.append(name)

        for name in outs:
            if name == "hidden":
                add(name, (pixels // 2, 2 * channels), BF)
            elif name == "both":
                add(name, (2, both_cols * height // 2, 2 * channels), BF)
            elif name == "memory":
                add(name, (pixels, channels), F32)
            elif name == "tiles":
                for k in range(batch):
                    add(f"tile{k}", (len(done[0]), self.tile_rows, self.tile_cols, channels), BF)
        if keep is not None:
            add("keep", (pixels, 4 * channels), F32)
        if after is not None:
            add("after", (height * after[1], 4 * channels), F32)
        count = len(operands)
        widest = max([t[2] for t in terms] + [f[2] for frames in done or () for f in frames] + [cols])
        if memory is not None:
            widest = max(widest, memory[2])

        def kernel(*refs):
            ins, out = refs[:count], dict(zip(names, refs[count : count + len(shapes)]))
            stage_ref, shift_ref, sum_ref, before_ref, turn_ref, *patch_refs = refs[
                count + len(shapes) :
            ]
            weight_ref, bias_ref = ins[:2]
            info = Position(batch)

            def ref_of(at):
                return [ref_of(a) for a in at] if isinstance(at, list) else ins[at]

            @pl.when(info.section == turn)
            def _():
                last, patches = None, []
                for (_, index, span, part), at in zip(terms, term_at):
                    if (at, index) != last:
                        patches.append(patch_refs[len(patches)])
                        self.load(ref_of(at), index, info, stage_ref, turn_ref, span)
                        self.spread(stage_ref, shift_ref, patches[-1], span, cols)
                    else:
                        patches.append(patches[-1])
                    last = (at, index)
                for lane, wide in self.ranges():
                    total = None
                    for n, (_, _, _, part) in enumerate(terms):
                        term = self.product(weight_ref, part, patches[n], cols, lane, wide)
                        total = term if total is None else total + term
                        if keep == n + 1:
                            out["keep"][:, pl.ds(lane, wide)] = total
                    sum_ref[:, pl.ds(lane, wide)] = total
                gates = [(sum_ref, cols)]
                if gates_in is not None:
                    gates.append((ins[gates_at], gates_in[1]))
                before = None
                if memory is not None:
                    ref = ins[memory_at]
                    if ref.shape[-1] == channels:
                        before = (ref, memory[2])
                    else:
                        self.load(ref, memory[1], info, before_ref, None, memory[2])
                        before = (before_ref.at[pl.ds(8, memory[2] * height), :], memory[2])
                both = out.get("both")
                cell_ref = out.get("memory", before_ref.at[pl.ds(0, pixels), :] if both is not None else None)
                for lane, wide in self.ranges():
                    self.update(
                        info, gates, bias_ref, before, cols, stage_ref, cell_ref, lane, wide
                    )
                if "hidden" in out:
                    self.pack(stage_ref, 8, cols, out["hidden"], cols)
                if both is not None:
                    self.pack(stage_ref, 8, cols, both.at[0], both_cols)
                    self.pack(cell_ref, 0, cols, both.at[1], both_cols)
                if after is not None:
                    self.spread(stage_ref, shift_ref, patch_refs[0], cols, after[1])
                    out["after"][...] = self.product(
                        weight_ref, after[0], patch_refs[0], after[1], 0, 4 * channels
                    )

            if relay is not None:

                @pl.when(info.section == relay[0])
                def _():
                    out["both"][...] = ins[relay_at][...]

            if done is not None:
                tile_refs = [out[f"tile{k}"] for k in range(batch)]
                for section, frames in enumerate(done):

                    @pl.when(info.section == section)
                    def _():
                        for frame, (array, index, span) in reversed(list(enumerate(frames))):
                            if array is not None:
                                source = ins[done_at[section][frame]]
                                self.load(source, index, info, stage_ref, None, span)
                            self.tiles(info, stage_ref, turn_ref, span, frame, tile_refs)

        return pl.pallas_call(
            kernel,
            out_shape=shapes,
            in_specs=specs,
            out_specs=[VMEM] * len(shapes),
            scratch_shapes=self.scratch(widest, cols, len(set(map(id, (t[0] for t in terms))))),
            cost_estimate=self.cost(pixels, len(terms) + (after is not None)),
            compiler_params=pltpu.CompilerParams(vmem_limit_bytes=LIMIT),
        )(*operands)

    def cost(self, pixels, products):
        return pl.CostEstimate(
            flops=8 * pixels * TAPS * self.channels * self.channels * products,
            bytes_accessed=pixels * self.channels * 2, transcendentals=0,
        )

    def partial(self, turn, array, index, cols, out_cols, part):
        pixels, channels = self.height * out_cols, self.channels

        def kernel(weight_ref, in_ref, out_ref, stage_ref, shift_ref, *rest):
            patch_ref = rest[-1]
            info = Position(self.batch)

            @pl.when(info.section == turn)
            def _():
                self.load(in_ref, index, info, stage_ref, None, cols)
                self.spread(stage_ref, shift_ref, patch_ref, cols, out_cols)
                out_ref[...] = self.product(
                    weight_ref, part, patch_ref, out_cols, 0, 4 * channels
                )

        return pl.pallas_call(
            kernel,
            out_shape=jax.ShapeDtypeStruct((pixels, 4 * channels), F32),
            in_specs=[VMEM, VMEM],
            out_specs=VMEM,
            scratch_shapes=self.scratch(cols, out_cols),
            cost_estimate=self.cost(pixels, 1),
            compiler_params=pltpu.CompilerParams(vmem_limit_bytes=LIMIT),
        )(self.weight, array)


def gate_order(value, channels):
    whole = channels // LANES * LANES
    gates = [value[:, k * channels : (k + 1) * channels] for k in range(4)]
    return jnp.concatenate([g[:, :whole] for g in gates] + [g[:, whole:] for g in gates], axis=1)


def joined_weight(shards, channels):
    per = 2 * TAPS // len(shards)
    rows, columns = shards[0].shape[0] * len(shards) // 2, shards[0].shape[1]
    joined = None
    for which, shard in enumerate(shards):

        def kernel(*refs, which=which):
            first = lax.rem(lax.axis_index("row") + which, len(shards)) * per
            if which == 0:
                in_ref, out_ref, held_ref, sems = refs

                def copy(j):
                    block = pl.ds(j * channels, channels)
                    return pltpu.make_async_copy(in_ref.at[block], held_ref.at[block], sems.at[j])

                for j in range(per):
                    copy(j).start()
            else:
                _, held_ref, out_ref = refs

            for j in range(per):
                if which == 0:
                    copy(j).wait()
                block = first + j
                value = gate_order(held_ref[pl.ds(j * channels, channels), :], channels)
                tap = pl.multiple_of(lax.div(block, 2) * channels, 16)
                out_ref[lax.rem(block, 2), pl.ds(tap, channels), :] = value

        source = pltpu.with_memory_space_constraint(shard, pltpu.HBM) if which == 0 else shard
        scratch = [pltpu.VMEM(shard.shape, BF), pltpu.SemaphoreType.DMA((per,))]
        joined = pl.pallas_call(
            kernel,
            out_shape=pltpu.VMEM((2, rows, columns), BF),
            in_specs=[HBM] if joined is None else [VMEM, VMEM],
            out_specs=VMEM,
            scratch_shapes=scratch if which == 0 else [],
            input_output_aliases={} if joined is None else {0: 0},
            compiler_params=pltpu.CompilerParams(vmem_limit_bytes=LIMIT),
        )(*([] if joined is None else [joined]), source)
    return joined


def window_levels(features, gate_weight, gate_bias):
    batch, frames, tile_rows, tile_cols, channels = features.shape
    section, row, _ = (lax.axis_index(a) for a in ("section", "row", "col"))
    row_size = lax.axis_size("row")
    groups = row_size // batch
    place = row % batch
    row_halo = HALO if groups > 1 else 0
    height = tile_rows * batch + 2 * row_halo
    wide, good = tile_cols + 2 * HALO, [tile_cols + 2 * k for k in range(STEPS)]

    if groups == 1 and batch == 2:
        pieces = paired_pieces(features)
    else:
        window = gather_sequence(features)
        if groups > 1:
            window = with_halo(window, "row", 1, batch)
        window = jnp.swapaxes(with_halo(window, "col", 2, 1), 1, 2)
        pieces = window.reshape(frames, height * wide, channels)

    own_weight = gate_weight[0]
    if row_size == 2 and own_weight.shape[0] % channels == 0:
        shards = [own_weight, lax.ppermute(own_weight, "row", [(0, 1), (1, 0)])]
    else:
        shards = [lax.all_gather(own_weight, "row", axis=0, tiled=True)]

    weight = joined_weight(shards, channels)
    weight = pltpu.with_memory_space_constraint(weight, pltpu.VMEM)
    plan = Plan(weight, gate_bias, height, channels, batch, tile_rows, tile_cols, row_halo)

    h00, c00 = plan.step(0, [(pieces, 0, wide, 0)], good[5], outs=("hidden", "memory"))
    x10 = section_send(h00, batch, (0, 1, 3, 2))
    h01, s01 = plan.step(
        0, [(pieces, 1, wide, 0), (h00, None, good[5], 1)], good[4], memory=(c00, None, good[5]),
        outs=("hidden", "both"), both_cols=good[3],
    )
    x11 = section_send(h01, batch, (0, 1, 3, 2))
    h10, c10, p11 = plan.step(
        1, [(x10, None, good[5], 0)], good[4], after=(1, good[3]), outs=("hidden", "memory")
    )
    (s11,) = plan.step(
        1, [(x11, None, good[4], 0)], good[3], gates_in=(p11, good[3]), memory=(c10, None, good[4]),
        outs=("both",), both_cols=good[3], relay=(0, s01),
    )
    x2 = section_send(s11, batch, (1, 2, 0, 3))
    p30 = plan.partial(3, x2, 0, good[3], good[1], 1)
    h20, c20, p21 = plan.step(
        2, [(x2, 0, good[3], 0), (x2, 0, good[3], 1)], good[2], memory=(x2, 1, good[3]), keep=1,
        outs=("hidden", "memory"),
    )
    x30 = section_send(h20, batch, (2, 3, 1), (0,))
    (h21,) = plan.step(
        2, [(h20, None, good[2], 1)], good[1], gates_in=(p21, good[2]), memory=(c20, None, good[2]),
        outs=("hidden",),
    )
    h21, p30 = lax.optimization_barrier((h21, p30))
    x31 = section_send(h21, batch, (2, 3), (0,), (1,))
    h30, c30, p31 = plan.step(
        3, [(x30, None, good[2], 0)], good[1], gates_in=(p30, good[1]), memory=(x2, 1, good[3]),
        after=(1, good[0]), outs=("hidden", "memory"),
    )
    tiles = plan.step(
        3, [(x31, None, good[1], 0)], good[0], gates_in=(p31, good[0]), memory=(c30, None, good[1]),
        outs=("tiles",),
        done=(
            ((h00, None, good[5]), (h01, None, good[4])),
            ((h10, None, good[4]), (s11, 0, good[3])),
            ((h20, None, good[2]), (h21, None, good[1])),
            ((h30, None, good[1]), (None, None, good[0])),
        ),
    )

    parts = [tiles[0]]
    for k in range(1, batch):
        parts.append(lax.ppermute(tiles[k], "row", group_pairs(row_size, batch, k)))
    result = []
    for q in range(batch):
        chosen = parts[0]
        for k in range(1, batch):
            chosen = jnp.where((place - section - q) % batch == k, parts[k], chosen)
        result.append(chosen)
    return jnp.stack(result)[None]


def solution(mesh):
    return jax.shard_map(
        window_levels,
        mesh=mesh,
        in_specs=(P(None, None, "row", "col", None), P("section", "row", None), P("section", None)),
        out_specs=P("section", None, None, "row", "col", None),
        check_vma=False,
    )
```

```python
import jax
import jax.numpy as jnp
from jax import lax
from jax.experimental import pallas as pl
from jax.experimental.pallas import tpu as pltpu
from jax.sharding import PartitionSpec as P


HALO = 8
TAPS = 9
LANES = 128
BF = jnp.bfloat16
F32 = jnp.float32
VMEM = pl.BlockSpec(memory_space=pltpu.VMEM)
HBM = pl.BlockSpec(memory_space=pltpu.HBM)
LIMIT = 12 * 1024 * 1024
STEPS = 6


def section_send(block, *routes):
    pairs = [(r[i], r[(i + 1) % len(r)]) for r in routes for i in range(len(r))]
    return lax.ppermute(block, "section", pairs)


class Position:
    def __init__(self, batch):
        row = lax.axis_index("row")
        self.section, self.col, self.last_col = (
            lax.axis_index("section"), lax.axis_index("col"), lax.axis_size("col") - 1,
        )
        self.place, self.group = lax.rem(row, batch), lax.div(row, batch)
        self.last_group = lax.axis_size("row") // batch - 1


def group_pairs(size, batch, k):
    return [(i, i - i % batch + (i % batch + k) % batch) for i in range(size)]


def gather_sequence(features):
    batch = features.shape[0]
    size = lax.axis_size("row")
    place = lax.axis_index("row") % batch
    parts = [lax.dynamic_index_in_dim(features, place, 0, keepdims=False)]
    for k in range(1, batch):
        sent = lax.dynamic_index_in_dim(features, (place + k) % batch, 0, keepdims=False)
        parts.append(lax.ppermute(sent, "row", group_pairs(size, batch, k)))
    stacked = jnp.stack(parts)
    blocks = [
        lax.dynamic_index_in_dim(stacked, (place - q) % batch, 0, keepdims=False)
        for q in range(batch)
    ]
    return jnp.concatenate(blocks, axis=1)


def with_halo(array, axis, dim, stride):
    size, length = lax.axis_size(axis), array.shape[dim]
    up = [(i, i + stride) for i in range(size - stride)]
    down = [(j, i) for i, j in up]
    last = lax.slice_in_dim(array, length - HALO, length, axis=dim)
    first = lax.slice_in_dim(array, 0, HALO, axis=dim)
    before = lax.ppermute(last, axis, up)
    after = lax.ppermute(first, axis, down)
    return jnp.concatenate([before, array, after], axis=dim)


def paired_pieces(features):
    batch, frames, tile_rows, tile_cols, channels = features.shape
    cols = lax.axis_size("col")
    partner = lax.ppermute(features, "row", [(0, 1), (1, 0)])

    def take(in_ref, out_ref, sem):
        copy = pltpu.make_async_copy(in_ref, out_ref, sem)
        copy.start()
        copy.wait()

    own = pl.pallas_call(
        take,
        out_shape=pltpu.VMEM(features.shape, features.dtype),
        in_specs=[HBM],
        out_specs=VMEM,
        scratch_shapes=[pltpu.SemaphoreType.DMA(())],
        compiler_params=pltpu.CompilerParams(vmem_limit_bytes=LIMIT),
        name="take",
    )(pltpu.with_memory_space_constraint(features, pltpu.HBM))

    def kernel(own_ref, partner_ref, out_ref):
        right = lax.axis_index("row") == 0
        for which, ref in enumerate((own_ref, partner_ref)):
            for frame in range(frames):
                for i in range(tile_rows):
                    for b in range(batch):
                        row = ref[b, frame, i].astype(F32)
                        side = jnp.where(right, row[tile_cols - HALO :], row[:HALO])
                        out_ref[which, frame, i, :, pl.ds(b * channels, channels)] = side.astype(BF)

    edge = pl.pallas_call(
        kernel,
        out_shape=jax.ShapeDtypeStruct((2, frames, tile_rows, HALO, batch * channels), BF),
        in_specs=[VMEM, VMEM],
        out_specs=VMEM,
        compiler_params=pltpu.CompilerParams(vmem_limit_bytes=LIMIT),
        name="edge",
    )(own, partner)
    up = list(range(cols))
    ring = up + [cols + c for c in reversed(up)]
    pairs = [(ring[i], ring[(i + 1) % len(ring)]) for i in range(len(ring))]
    side = lax.ppermute(edge, ("row", "col"), pairs)
    other = lax.ppermute(side, "row", [(0, 1), (1, 0)])
    return [own, partner, side, other]


def sigmoid(x):
    return 0.5 * jnp.tanh(0.5 * x) + 0.5


class Plan:
    def __init__(self, weight, bias, height, channels, batch, tile_rows, tile_cols, row_halo):
        self.weight, self.bias = weight, bias
        self.height, self.channels, self.batch = height, channels, batch
        self.tile_rows, self.tile_cols, self.row_halo = tile_rows, tile_cols, row_halo

    def lanes(self):
        return [(k, min(LANES, self.channels - k)) for k in range(0, self.channels, LANES)]

    def load(self, ref, index, info, stage_ref, turn_ref, cols):
        channels, height = self.channels, self.height
        pixels = cols * height
        if not isinstance(ref, list):
            value = ref[...] if index is None else ref[index]
            if value.shape[-1] == channels:
                stage_ref[pl.ds(8, pixels), :] = value.astype(F32)
            else:
                half = pixels // 2
                for k in range(2):
                    part = value[:, k * channels : (k + 1) * channels]
                    stage_ref[pl.ds(8 + k * half, half), :] = part.astype(F32)
            return
        own, partner, side, other = ref
        rows, place, tile_cols = self.tile_rows, info.place, self.tile_cols
        first = place == 0
        left, right = info.col > 0, info.col < info.last_col

        def put(value, row, col):
            count = value.shape[0]
            for n, (lane, width) in enumerate(self.lanes()):
                part = value[:, lane : lane + width]
                if width < LANES:
                    part = jnp.concatenate([part, jnp.zeros((count, LANES - width), F32)], axis=1)
                turn_ref[n, pl.ds(col * height + row, count, stride=height), :] = part

        def mine(piece, k, i):
            value = piece[k, index, i].astype(F32)
            return jnp.where(first, value[:, :channels], value[:, channels:])

        for i in range(rows):
            a, b = own[place, index, i].astype(F32), partner[place, index, i].astype(F32)
            put(jnp.where(first, a, b), i, HALO)
            put(jnp.where(first, b, a), rows + i, HALO)
            for k in range(2):
                a, b = mine(side, k, i), mine(other, k, i)
                put(jnp.where(left, jnp.where(first, a, b), 0.0), k * rows + i, 0)
                put(jnp.where(right, jnp.where(first, b, a), 0.0), (1 - k) * rows + i, HALO + tile_cols)
        for n, (lane, width) in enumerate(self.lanes()):
            value = turn_ref[n, pl.ds(0, pixels), :]
            stage_ref[pl.ds(8, pixels), pl.ds(lane, width)] = value[:, :width]

    def spread(self, stage_ref, shift_ref, patch_ref, cols, out_cols):
        channels, height = self.channels, self.height
        inset = (cols - out_cols) // 2
        used = (out_cols + 2) * height
        start = 8 + (inset - 1) * height
        row = lax.broadcasted_iota(jnp.int32, (out_cols + 2, height, channels), 1)
        for k, offset in enumerate((-1, 1)):
            value = stage_ref[pl.ds(start + offset, used), :].reshape(out_cols + 2, height, channels)
            value = jnp.where(row == (0 if k == 0 else height - 1), 0.0, value)
            shift_ref[k, pl.ds(0, used), :] = value.reshape(used, channels)
        pixels = out_cols * height
        for tap in range(TAPS):
            row_tap, col_tap = tap // 3, tap % 3
            if row_tap == 1:
                value = stage_ref[pl.ds(start + col_tap * height, pixels), :]
            else:
                value = shift_ref[row_tap // 2, pl.ds(col_tap * height, pixels), :]
            patch_ref[pl.ds(0, pixels), pl.ds(tap * channels, channels)] = value.astype(BF)

    def ranges(self):
        split = self.channels // LANES * LANES * 4
        return (0, split), (split, 4 * self.channels - split)

    def product(self, weight_ref, part, patch_ref, cols, lane, width):
        return jnp.dot(
            patch_ref[pl.ds(0, cols * self.height), :],
            weight_ref[part, :, pl.ds(lane, width)],
            preferred_element_type=F32,
        )

    def cell(self, total, before):
        width = total.shape[-1] // 4
        if width % LANES == 0:
            gate = [total[:, k * width : (k + 1) * width] for k in range(4)]
            cell = sigmoid(gate[0]) * jnp.tanh(gate[2])
            if before is not None:
                cell = cell + sigmoid(gate[1]) * before
            return sigmoid(gate[3]) * jnp.tanh(cell), cell
        first, second = sigmoid(total[:, : 2 * width]), total[:, 2 * width :]
        low = lax.broadcasted_iota(jnp.int32, second.shape, 1) < width
        scale = jnp.where(low, 1.0, 0.5)
        second = scale * jnp.tanh(scale * second) + jnp.where(low, 0.0, 0.5)
        cell = (first * second)[:, :width]
        if before is not None:
            cell = cell + pltpu.roll(first, width, 1)[:, :width] * before
        return pltpu.roll(second, width, 1)[:, :width] * jnp.tanh(cell), cell

    def update(self, info, gates, bias_ref, memory, cols, stage_ref, cell_ref, lane, width):
        ch, height = width // 4, self.height
        first = lane // 4
        bias = gate_order(bias_ref[...], self.channels)[:, lane : lane + width]
        halo = (cols - self.tile_cols) // 2
        pieces = [(0, halo, info.col > 0)]
        pieces += [(halo + c, 4, None) for c in range(0, self.tile_cols, 4)]
        pieces += [(cols - halo, halo, info.col < info.last_col)]

        def part(ref, ref_cols, col, count, lane, width):
            start = (col + (ref_cols - cols) // 2) * height
            return ref[pl.ds(start, count * height), pl.ds(lane, width)]

        for col, count, inside in pieces:
            if count == 0:
                continue
            total = bias
            for ref, ref_cols in gates:
                total = total + part(ref, ref_cols, col, count, lane, width)
            before = None
            if memory is not None:
                before = part(*memory, col, count, first, ch).astype(F32)
            hidden, cell = self.cell(total, before)
            if inside is not None:
                hidden = jnp.where(inside, hidden, 0.0)
            if self.row_halo:
                row = lax.broadcasted_iota(jnp.int32, (count, height, ch), 1)
                top = jnp.where(info.group == 0, self.row_halo, 0)
                bottom = jnp.where(info.group == info.last_group, height - self.row_halo, height)
                hidden = hidden.reshape(count, height, ch)
                hidden = jnp.where((row >= top) & (row < bottom), hidden, 0.0)
                hidden = hidden.reshape(count * height, ch)
            stage_ref[pl.ds(8 + col * height, count * height), pl.ds(first, ch)] = hidden
            if cell_ref is not None:
                cell_ref[pl.ds(col * height, count * height), pl.ds(first, ch)] = cell

    def pack(self, source_ref, offset, cols, out_ref, out_cols):
        half, channels = out_cols * self.height // 2, self.channels
        start = offset + (cols - out_cols) // 2 * self.height
        for k in range(2):
            value = source_ref[pl.ds(start + k * half, half), :]
            out_ref[:, pl.ds(k * channels, channels)] = value.astype(BF)

    def tiles(self, info, stage_ref, turn_ref, cols, frame, outs):
        halo, pixels = (cols - self.tile_cols) // 2, self.tile_cols * self.height
        for n, (lane, width) in enumerate(self.lanes()):
            value = stage_ref[pl.ds(8 + halo * self.height, pixels), pl.ds(lane, width)]
            if width < LANES:
                value = jnp.concatenate([value, jnp.zeros((pixels, LANES - width), F32)], axis=1)
            turn_ref[n, pl.ds(0, pixels), :] = value
        for i in range(self.tile_rows):
            rows = []
            for b in range(self.batch):
                start = self.row_halo + b * self.tile_rows + i
                row = [
                    turn_ref[n, pl.ds(start, self.tile_cols, stride=self.height), :][:, :width]
                    for n, (_, width) in enumerate(self.lanes())
                ]
                rows.append(jnp.concatenate(row, axis=1))
            for k, out in enumerate(outs):
                value = rows[0]
                for b in range(1, self.batch):
                    value = jnp.where(lax.rem(info.place + k, self.batch) == b, rows[b], value)
                out[frame, i] = value.astype(BF)

    def scratch(self, widest, cols, patches=1):
        pixels, channels = cols * self.height, self.channels
        return [
            pltpu.VMEM((widest * self.height + 16, channels), F32),
            pltpu.VMEM((2, (cols + 2) * self.height, channels), F32),
            pltpu.VMEM((pixels, 4 * channels), F32),
            pltpu.VMEM((widest * self.height + 16, channels), F32),
            pltpu.VMEM((len(self.lanes()), widest * self.height, LANES), F32),
        ] + [pltpu.VMEM((pixels, TAPS * channels), BF)] * patches

    def step(self, turn, terms, cols, gates_in=None, memory=None, keep=None, after=None, outs=(),
             both_cols=None, done=None, relay=None):
        channels, batch, height = self.channels, self.batch, self.height
        pixels = height * cols
        operands = [self.weight, self.bias]
        specs = [VMEM, VMEM]
        seen = {}

        def place_of(array):
            if array is None:
                return None
            if isinstance(array, list):
                return [place_of(a) for a in array]
            if id(array) not in seen:
                seen[id(array)] = len(operands)
                operands.append(array)
                specs.append(VMEM)
            return seen[id(array)]

        term_at = [place_of(t[0]) for t in terms]
        gates_at = place_of(gates_in[0]) if gates_in is not None else None
        memory_at = place_of(memory[0]) if memory is not None else None
        done_at = [[place_of(f[0]) for f in frames] for frames in done] if done else None
        relay_at = place_of(relay[1]) if relay is not None else None
        shapes, names = [], []

        def add(name, shape, dtype):
            shapes.append(jax.ShapeDtypeStruct(shape, dtype))
            names.append(name)

        for name in outs:
            if name == "hidden":
                add(name, (pixels // 2, 2 * channels), BF)
            elif name == "both":
                add(name, (2, both_cols * height // 2, 2 * channels), BF)
            elif name == "memory":
                add(name, (pixels, channels), F32)
            elif name == "tiles":
                for k in range(batch):
                    add(f"tile{k}", (len(done[0]), self.tile_rows, self.tile_cols, channels), BF)
        if keep is not None:
            add("keep", (pixels, 4 * channels), F32)
        if after is not None:
            add("after", (height * after[1], 4 * channels), F32)
        count = len(operands)
        widest = max([t[2] for t in terms] + [f[2] for frames in done or () for f in frames] + [cols])
        if memory is not None:
            widest = max(widest, memory[2])

        def kernel(*refs):
            ins, out = refs[:count], dict(zip(names, refs[count : count + len(shapes)]))
            stage_ref, shift_ref, sum_ref, before_ref, turn_ref, *patch_refs = refs[
                count + len(shapes) :
            ]
            weight_ref, bias_ref = ins[:2]
            info = Position(batch)

            def ref_of(at):
                return [ref_of(a) for a in at] if isinstance(at, list) else ins[at]

            @pl.when(info.section == turn)
            def _():
                last, patches = None, []
                for (_, index, span, part), at in zip(terms, term_at):
                    if (at, index) != last:
                        patches.append(patch_refs[len(patches)])
                        self.load(ref_of(at), index, info, stage_ref, turn_ref, span)
                        self.spread(stage_ref, shift_ref, patches[-1], span, cols)
                    else:
                        patches.append(patches[-1])
                    last = (at, index)
                for lane, wide in self.ranges():
                    total = None
                    for n, (_, _, _, part) in enumerate(terms):
                        term = self.product(weight_ref, part, patches[n], cols, lane, wide)
                        total = term if total is None else total + term
                        if keep == n + 1:
                            out["keep"][:, pl.ds(lane, wide)] = total
                    sum_ref[:, pl.ds(lane, wide)] = total
                gates = [(sum_ref, cols)]
                if gates_in is not None:
                    gates.append((ins[gates_at], gates_in[1]))
                before = None
                if memory is not None:
                    ref = ins[memory_at]
                    if ref.shape[-1] == channels:
                        before = (ref, memory[2])
                    else:
                        self.load(ref, memory[1], info, before_ref, None, memory[2])
                        before = (before_ref.at[pl.ds(8, memory[2] * height), :], memory[2])
                both = out.get("both")
                cell_ref = out.get("memory", before_ref.at[pl.ds(0, pixels), :] if both is not None else None)
                for lane, wide in self.ranges():
                    self.update(
                        info, gates, bias_ref, before, cols, stage_ref, cell_ref, lane, wide
                    )
                if "hidden" in out:
                    self.pack(stage_ref, 8, cols, out["hidden"], cols)
                if both is not None:
                    self.pack(stage_ref, 8, cols, both.at[0], both_cols)
                    self.pack(cell_ref, 0, cols, both.at[1], both_cols)
                if after is not None:
                    self.spread(stage_ref, shift_ref, patch_refs[0], cols, after[1])
                    out["after"][...] = self.product(
                        weight_ref, after[0], patch_refs[0], after[1], 0, 4 * channels
                    )

            if relay is not None:

                @pl.when(info.section == relay[0])
                def _():
                    out["both"][...] = ins[relay_at][...]

            if done is not None:
                tile_refs = [out[f"tile{k}"] for k in range(batch)]
                for section, frames in enumerate(done):

                    @pl.when(info.section == section)
                    def _():
                        for frame, (array, index, span) in reversed(list(enumerate(frames))):
                            if array is not None:
                                source = ins[done_at[section][frame]]
                                self.load(source, index, info, stage_ref, None, span)
                            self.tiles(info, stage_ref, turn_ref, span, frame, tile_refs)

        return pl.pallas_call(
            kernel,
            out_shape=shapes,
            in_specs=specs,
            out_specs=[VMEM] * len(shapes),
            scratch_shapes=self.scratch(widest, cols, len(set(map(id, (t[0] for t in terms))))),
            cost_estimate=self.cost(pixels, len(terms) + (after is not None)),
            compiler_params=pltpu.CompilerParams(vmem_limit_bytes=LIMIT),
        )(*operands)

    def cost(self, pixels, products):
        return pl.CostEstimate(
            flops=8 * pixels * TAPS * self.channels * self.channels * products,
            bytes_accessed=pixels * self.channels * 2, transcendentals=0,
        )

    def partial(self, turn, array, index, cols, out_cols, part):
        pixels, channels = self.height * out_cols, self.channels

        def kernel(weight_ref, in_ref, out_ref, stage_ref, shift_ref, *rest):
            patch_ref = rest[-1]
            info = Position(self.batch)

            @pl.when(info.section == turn)
            def _():
                self.load(in_ref, index, info, stage_ref, None, cols)
                self.spread(stage_ref, shift_ref, patch_ref, cols, out_cols)
                out_ref[...] = self.product(
                    weight_ref, part, patch_ref, out_cols, 0, 4 * channels
                )

        return pl.pallas_call(
            kernel,
            out_shape=jax.ShapeDtypeStruct((pixels, 4 * channels), F32),
            in_specs=[VMEM, VMEM],
            out_specs=VMEM,
            scratch_shapes=self.scratch(cols, out_cols),
            cost_estimate=self.cost(pixels, 1),
            compiler_params=pltpu.CompilerParams(vmem_limit_bytes=LIMIT),
        )(self.weight, array)


def gate_order(value, channels):
    whole = channels // LANES * LANES
    gates = [value[:, k * channels : (k + 1) * channels] for k in range(4)]
    return jnp.concatenate([g[:, :whole] for g in gates] + [g[:, whole:] for g in gates], axis=1)


def joined_weight(shards, channels):
    per = 2 * TAPS // len(shards)
    rows, columns = shards[0].shape[0] * len(shards) // 2, shards[0].shape[1]
    joined = None
    for which, shard in enumerate(shards):

        def kernel(*refs, which=which):
            first = lax.rem(lax.axis_index("row") + which, len(shards)) * per
            if which == 0:
                in_ref, out_ref, held_ref, sems = refs

                def copy(j):
                    block = pl.ds(j * channels, channels)
                    return pltpu.make_async_copy(in_ref.at[block], held_ref.at[block], sems.at[j])

                for j in range(per):
                    copy(j).start()
            else:
                _, held_ref, out_ref = refs

            for j in range(per):
                if which == 0:
                    copy(j).wait()
                block = first + j
                value = gate_order(held_ref[pl.ds(j * channels, channels), :], channels)
                tap = pl.multiple_of(lax.div(block, 2) * channels, 16)
                out_ref[lax.rem(block, 2), pl.ds(tap, channels), :] = value

        source = pltpu.with_memory_space_constraint(shard, pltpu.HBM) if which == 0 else shard
        scratch = [pltpu.VMEM(shard.shape, BF), pltpu.SemaphoreType.DMA((per,))]
        joined = pl.pallas_call(
            kernel,
            out_shape=pltpu.VMEM((2, rows, columns), BF),
            in_specs=[HBM] if joined is None else [VMEM, VMEM],
            out_specs=VMEM,
            scratch_shapes=scratch if which == 0 else [],
            input_output_aliases={} if joined is None else {0: 0},
            compiler_params=pltpu.CompilerParams(vmem_limit_bytes=LIMIT),
        )(*([] if joined is None else [joined]), source)
    return joined


def window_levels(features, gate_weight, gate_bias):
    batch, frames, tile_rows, tile_cols, channels = features.shape
    _, row, _ = (lax.axis_index(a) for a in ("section", "row", "col"))
    row_size = lax.axis_size("row")
    groups = row_size // batch
    place = row % batch
    row_halo = HALO if groups > 1 else 0
    height = tile_rows * batch + 2 * row_halo
    wide, good = tile_cols + 2 * HALO, [tile_cols + 2 * k for k in range(STEPS)]

    if groups == 1 and batch == 2:
        pieces = paired_pieces(features)
    else:
        window = gather_sequence(features)
        if groups > 1:
            window = with_halo(window, "row", 1, batch)
        window = jnp.swapaxes(with_halo(window, "col", 2, 1), 1, 2)
        pieces = window.reshape(frames, height * wide, channels)

    own_weight = gate_weight[0]
    if row_size == 2 and own_weight.shape[0] % channels == 0:
        shards = [own_weight, lax.ppermute(own_weight, "row", [(0, 1), (1, 0)])]
    else:
        shards = [lax.all_gather(own_weight, "row", axis=0, tiled=True)]

    weight = joined_weight(shards, channels)
    weight = pltpu.with_memory_space_constraint(weight, pltpu.VMEM)
    plan = Plan(weight, gate_bias, height, channels, batch, tile_rows, tile_cols, row_halo)

    h00, c00 = plan.step(0, [(pieces, 0, wide, 0)], good[5], outs=("hidden", "memory"))
    x10 = section_send(h00, (0, 1, 3, 2))
    h01, s01 = plan.step(
        0, [(pieces, 1, wide, 0), (h00, None, good[5], 1)], good[4], memory=(c00, None, good[5]),
        outs=("hidden", "both"), both_cols=good[3],
    )
    x11 = section_send(h01, (0, 1, 3, 2))
    h10, c10, p11 = plan.step(
        1, [(x10, None, good[5], 0)], good[4], after=(1, good[3]), outs=("hidden", "memory")
    )
    (s11,) = plan.step(
        1, [(x11, None, good[4], 0)], good[3], gates_in=(p11, good[3]), memory=(c10, None, good[4]),
        outs=("both",), both_cols=good[3], relay=(0, s01),
    )
    x2 = section_send(s11, (1, 2, 0, 3))
    p30 = plan.partial(3, x2, 0, good[3], good[1], 1)
    h20, c20, p21 = plan.step(
        2, [(x2, 0, good[3], 0), (x2, 0, good[3], 1)], good[2], memory=(x2, 1, good[3]), keep=1,
        outs=("hidden", "memory"),
    )
    x30 = section_send(h20, (2, 3, 1, 0))
    (h21,) = plan.step(
        2, [(h20, None, good[2], 1)], good[1], gates_in=(p21, good[2]), memory=(c20, None, good[2]),
        outs=("hidden",),
    )
    h21, p30 = lax.optimization_barrier((h21, p30))
    x31 = section_send(h21, (2, 3), (0,), (1,))
    h30, c30, p31 = plan.step(
        3, [(x30, None, good[2], 0)], good[1], gates_in=(p30, good[1]), memory=(x2, 1, good[3]),
        after=(1, good[0]), outs=("hidden", "memory"),
    )
    tiles = plan.step(
        3, [(x31, None, good[1], 0)], good[0], gates_in=(p31, good[0]), memory=(c30, None, good[1]),
        outs=("tiles",),
        done=(
            ((h00, None, good[5]), (h01, None, good[4])),
            ((h10, None, good[4]), (s11, 0, good[3])),
            ((h20, None, good[2]), (h21, None, good[1])),
            ((h30, None, good[1]), (None, None, good[0])),
        ),
    )

    parts = [tiles[0]]
    for k in range(1, batch):
        parts.append(lax.ppermute(tiles[k], "row", group_pairs(row_size, batch, k)))
    result = []
    for q in range(batch):
        chosen = parts[0]
        for k in range(1, batch):
            chosen = jnp.where((place - q) % batch == k, parts[k], chosen)
        result.append(chosen)
    return jnp.stack(result)[None]


def solution(mesh):
    return jax.shard_map(
        window_levels,
        mesh=mesh,
        in_specs=(P(None, None, "row", "col", None), P("section", "row", None), P("section", None)),
        out_specs=P("section", None, None, "row", "col", None),
        check_vma=False,
    )
```

```python
import jax
import jax.numpy as jnp
from jax import lax
from jax.experimental import pallas as pl
from jax.experimental.pallas import tpu as pltpu
from jax.sharding import PartitionSpec as P


HALO = 8
EDGE = 6
TAPS = 9
LANES = 128
BF = jnp.bfloat16
F32 = jnp.float32
VMEM = pl.BlockSpec(memory_space=pltpu.VMEM)
HBM = pl.BlockSpec(memory_space=pltpu.HBM)
LIMIT = 12 * 1024 * 1024
STEPS = 6


def section_send(block, *routes):
    pairs = [(r[i], r[(i + 1) % len(r)]) for r in routes for i in range(len(r))]
    return lax.ppermute(block, "section", pairs)


class Position:
    def __init__(self, batch):
        row = lax.axis_index("row")
        self.section, self.col, self.last_col = (
            lax.axis_index("section"), lax.axis_index("col"), lax.axis_size("col") - 1,
        )
        self.place, self.group = lax.rem(row, batch), lax.div(row, batch)
        self.last_group = lax.axis_size("row") // batch - 1


def group_pairs(size, batch, k):
    return [(i, i - i % batch + (i % batch + k) % batch) for i in range(size)]


def gather_sequence(features):
    batch = features.shape[0]
    size = lax.axis_size("row")
    place = lax.axis_index("row") % batch
    parts = [lax.dynamic_index_in_dim(features, place, 0, keepdims=False)]
    for k in range(1, batch):
        sent = lax.dynamic_index_in_dim(features, (place + k) % batch, 0, keepdims=False)
        parts.append(lax.ppermute(sent, "row", group_pairs(size, batch, k)))
    stacked = jnp.stack(parts)
    blocks = [
        lax.dynamic_index_in_dim(stacked, (place - q) % batch, 0, keepdims=False)
        for q in range(batch)
    ]
    return jnp.concatenate(blocks, axis=1)


def with_halo(array, axis, dim, stride):
    size, length = lax.axis_size(axis), array.shape[dim]
    up = [(i, i + stride) for i in range(size - stride)]
    down = [(j, i) for i, j in up]
    last = lax.slice_in_dim(array, length - HALO, length, axis=dim)
    first = lax.slice_in_dim(array, 0, HALO, axis=dim)
    before = lax.ppermute(last, axis, up)
    after = lax.ppermute(first, axis, down)
    return jnp.concatenate([before, array, after], axis=dim)


def paired_pieces(features):
    batch, frames, tile_rows, tile_cols, channels = features.shape
    cols = lax.axis_size("col")
    partner = lax.ppermute(features, "row", [(0, 1), (1, 0)])

    def take(in_ref, out_ref, sem):
        copy = pltpu.make_async_copy(in_ref, out_ref, sem)
        copy.start()
        copy.wait()

    own = pl.pallas_call(
        take,
        out_shape=pltpu.VMEM(features.shape, features.dtype),
        in_specs=[HBM],
        out_specs=VMEM,
        scratch_shapes=[pltpu.SemaphoreType.DMA(())],
        compiler_params=pltpu.CompilerParams(vmem_limit_bytes=LIMIT),
        name="take",
    )(pltpu.with_memory_space_constraint(features, pltpu.HBM))

    def kernel(own_ref, partner_ref, out_ref):
        right = lax.axis_index("row") == 0
        for which, ref in enumerate((own_ref, partner_ref)):
            for frame in range(frames):
                for b in range(batch):
                    sides = []
                    for i in range(tile_rows):
                        row = ref[b, frame, i].astype(F32)
                        sides.append(jnp.where(right, row[tile_cols - EDGE :], row[:EDGE]))
                    side = jnp.concatenate(sides).astype(BF)
                    out_ref[which, frame, :, pl.ds(b * channels, channels)] = side

    edge = pl.pallas_call(
        kernel,
        out_shape=jax.ShapeDtypeStruct((2, frames, tile_rows * EDGE, batch * channels), BF),
        in_specs=[VMEM, VMEM],
        out_specs=VMEM,
        compiler_params=pltpu.CompilerParams(vmem_limit_bytes=LIMIT),
        name="edge",
    )(own, partner)
    up = list(range(cols))
    ring = up + [cols + c for c in reversed(up)]
    pairs = [(ring[i], ring[(i + 1) % len(ring)]) for i in range(len(ring))]
    side = lax.ppermute(edge, ("row", "col"), pairs)
    other = lax.ppermute(side, "row", [(0, 1), (1, 0)])
    return [own, partner, side, other]


def sigmoid(x):
    return 0.5 * jnp.tanh(0.5 * x) + 0.5


class Plan:
    def __init__(self, weight, bias, height, channels, batch, tile_rows, tile_cols, row_halo):
        self.weight, self.bias = weight, bias
        self.height, self.channels, self.batch = height, channels, batch
        self.tile_rows, self.tile_cols, self.row_halo = tile_rows, tile_cols, row_halo

    def lanes(self):
        return [(k, min(LANES, self.channels - k)) for k in range(0, self.channels, LANES)]

    def load(self, ref, index, info, stage_ref, turn_ref, cols):
        channels, height = self.channels, self.height
        pixels = cols * height
        if not isinstance(ref, list):
            value = ref[...] if index is None else ref[index]
            if value.shape[-1] == channels:
                stage_ref[pl.ds(8, pixels), :] = value.astype(F32)
            else:
                half = pixels // 2
                for k in range(2):
                    part = value[:, k * channels : (k + 1) * channels]
                    stage_ref[pl.ds(8 + k * half, half), :] = part.astype(F32)
            return
        own, partner, side, other = ref
        rows, place, tile_cols = self.tile_rows, info.place, self.tile_cols
        first = place == 0
        left, right = info.col > 0, info.col < info.last_col

        def put(value, row, col):
            count = value.shape[0]
            for n, (lane, width) in enumerate(self.lanes()):
                part = value[:, lane : lane + width]
                if width < LANES:
                    part = jnp.concatenate([part, jnp.zeros((count, LANES - width), F32)], axis=1)
                turn_ref[n, pl.ds(col * height + row, count, stride=height), :] = part

        def mine(piece, k):
            value = piece[k, index].astype(F32)
            return jnp.where(first, value[:, :channels], value[:, channels:])

        sides = [(mine(side, k), mine(other, k)) for k in range(2)]

        for i in range(rows):
            a, b = own[place, index, i].astype(F32), partner[place, index, i].astype(F32)
            put(jnp.where(first, a, b), i, EDGE)
            put(jnp.where(first, b, a), rows + i, EDGE)
            for k in range(2):
                a, b = (v[i * EDGE : (i + 1) * EDGE] for v in sides[k])
                put(jnp.where(left, jnp.where(first, a, b), 0.0), k * rows + i, 0)
                put(jnp.where(right, jnp.where(first, b, a), 0.0), (1 - k) * rows + i, EDGE + tile_cols)
        for n, (lane, width) in enumerate(self.lanes()):
            value = turn_ref[n, pl.ds(0, pixels), :]
            stage_ref[pl.ds(8, pixels), pl.ds(lane, width)] = value[:, :width]

    def spread(self, stage_ref, shift_ref, patch_ref, cols, out_cols):
        channels, height = self.channels, self.height
        inset = (cols - out_cols) // 2
        used = (out_cols + 2) * height
        start = 8 + (inset - 1) * height
        row = lax.broadcasted_iota(jnp.int32, (out_cols + 2, height, channels), 1)
        for k, offset in enumerate((-1, 1)):
            value = stage_ref[pl.ds(start + offset, used), :].reshape(out_cols + 2, height, channels)
            value = jnp.where(row == (0 if k == 0 else height - 1), 0.0, value)
            shift_ref[k, pl.ds(0, used), :] = value.reshape(used, channels)
        pixels = out_cols * height
        for tap in range(TAPS):
            row_tap, col_tap = tap // 3, tap % 3
            if row_tap == 1:
                value = stage_ref[pl.ds(start + col_tap * height, pixels), :]
            else:
                value = shift_ref[row_tap // 2, pl.ds(col_tap * height, pixels), :]
            patch_ref[pl.ds(0, pixels), pl.ds(tap * channels, channels)] = value.astype(BF)

    def ranges(self):
        split = self.channels // LANES * LANES * 4
        return (0, split), (split, 4 * self.channels - split)

    def product(self, weight_ref, part, patch_ref, cols, lane, width):
        return jnp.dot(
            patch_ref[pl.ds(0, cols * self.height), :],
            weight_ref[part, :, pl.ds(lane, width)],
            preferred_element_type=F32,
        )

    def cell(self, total, before):
        width = total.shape[-1] // 4
        if width % LANES == 0:
            gate = [total[:, k * width : (k + 1) * width] for k in range(4)]
            cell = sigmoid(gate[0]) * jnp.tanh(gate[2])
            if before is not None:
                cell = cell + sigmoid(gate[1]) * before
            return sigmoid(gate[3]) * jnp.tanh(cell), cell
        first, second = sigmoid(total[:, : 2 * width]), total[:, 2 * width :]
        low = lax.broadcasted_iota(jnp.int32, second.shape, 1) < width
        scale = jnp.where(low, 1.0, 0.5)
        second = scale * jnp.tanh(scale * second) + jnp.where(low, 0.0, 0.5)
        cell = (first * second)[:, :width]
        if before is not None:
            cell = cell + pltpu.roll(first, width, 1)[:, :width] * before
        return pltpu.roll(second, width, 1)[:, :width] * jnp.tanh(cell), cell

    def update(self, info, gates, bias_ref, memory, cols, stage_ref, cell_ref, lane, width):
        ch, height = width // 4, self.height
        first = lane // 4
        bias = gate_order(bias_ref[...], self.channels)[:, lane : lane + width]
        halo = (cols - self.tile_cols) // 2
        pieces = [(0, halo, info.col > 0)]
        pieces += [(halo + c, 4, None) for c in range(0, self.tile_cols, 4)]
        pieces += [(cols - halo, halo, info.col < info.last_col)]

        def part(ref, ref_cols, col, count, lane, width):
            start = (col + (ref_cols - cols) // 2) * height
            return ref[pl.ds(start, count * height), pl.ds(lane, width)]

        for col, count, inside in pieces:
            if count == 0:
                continue
            total = bias
            for ref, ref_cols in gates:
                total = total + part(ref, ref_cols, col, count, lane, width)
            before = None
            if memory is not None:
                before = part(*memory, col, count, first, ch).astype(F32)
            hidden, cell = self.cell(total, before)
            if inside is not None:
                hidden = jnp.where(inside, hidden, 0.0)
            if self.row_halo:
                row = lax.broadcasted_iota(jnp.int32, (count, height, ch), 1)
                top = jnp.where(info.group == 0, self.row_halo, 0)
                bottom = jnp.where(info.group == info.last_group, height - self.row_halo, height)
                hidden = hidden.reshape(count, height, ch)
                hidden = jnp.where((row >= top) & (row < bottom), hidden, 0.0)
                hidden = hidden.reshape(count * height, ch)
            stage_ref[pl.ds(8 + col * height, count * height), pl.ds(first, ch)] = hidden
            if cell_ref is not None:
                cell_ref[pl.ds(col * height, count * height), pl.ds(first, ch)] = cell

    def pack(self, source_ref, offset, cols, out_ref, out_cols):
        half, channels = out_cols * self.height // 2, self.channels
        start = offset + (cols - out_cols) // 2 * self.height
        for k in range(2):
            value = source_ref[pl.ds(start + k * half, half), :]
            out_ref[:, pl.ds(k * channels, channels)] = value.astype(BF)

    def tiles(self, info, stage_ref, turn_ref, cols, frame, outs):
        halo, pixels = (cols - self.tile_cols) // 2, self.tile_cols * self.height
        for n, (lane, width) in enumerate(self.lanes()):
            value = stage_ref[pl.ds(8 + halo * self.height, pixels), pl.ds(lane, width)]
            if width < LANES:
                value = jnp.concatenate([value, jnp.zeros((pixels, LANES - width), F32)], axis=1)
            turn_ref[n, pl.ds(0, pixels), :] = value
        for i in range(self.tile_rows):
            rows = []
            for b in range(self.batch):
                start = self.row_halo + b * self.tile_rows + i
                row = [
                    turn_ref[n, pl.ds(start, self.tile_cols, stride=self.height), :][:, :width]
                    for n, (_, width) in enumerate(self.lanes())
                ]
                rows.append(jnp.concatenate(row, axis=1))
            for k, out in enumerate(outs):
                value = rows[0]
                for b in range(1, self.batch):
                    value = jnp.where(lax.rem(info.place + k, self.batch) == b, rows[b], value)
                out[frame, i] = value.astype(BF)

    def scratch(self, widest, cols, patches=1):
        pixels, channels = cols * self.height, self.channels
        return [
            pltpu.VMEM((widest * self.height + 16, channels), F32),
            pltpu.VMEM((2, (cols + 2) * self.height, channels), F32),
            pltpu.VMEM((pixels, 4 * channels), F32),
            pltpu.VMEM((widest * self.height + 16, channels), F32),
            pltpu.VMEM((len(self.lanes()), widest * self.height, LANES), F32),
        ] + [pltpu.VMEM((pixels, TAPS * channels), BF)] * patches

    def step(self, turn, terms, cols, gates_in=None, memory=None, keep=None, after=None, outs=(),
             both_cols=None, done=None, relay=None):
        channels, batch, height = self.channels, self.batch, self.height
        pixels = height * cols
        operands = [self.weight, self.bias]
        specs = [VMEM, VMEM]
        seen = {}

        def place_of(array):
            if array is None:
                return None
            if isinstance(array, list):
                return [place_of(a) for a in array]
            if id(array) not in seen:
                seen[id(array)] = len(operands)
                operands.append(array)
                specs.append(VMEM)
            return seen[id(array)]

        term_at = [place_of(t[0]) for t in terms]
        gates_at = place_of(gates_in[0]) if gates_in is not None else None
        memory_at = place_of(memory[0]) if memory is not None else None
        done_at = [[place_of(f[0]) for f in frames] for frames in done] if done else None
        relay_at = place_of(relay[1]) if relay is not None else None
        shapes, names = [], []

        def add(name, shape, dtype):
            shapes.append(jax.ShapeDtypeStruct(shape, dtype))
            names.append(name)

        for name in outs:
            if name == "hidden":
                add(name, (pixels // 2, 2 * channels), BF)
            elif name == "both":
                add(name, (2, both_cols * height // 2, 2 * channels), BF)
            elif name == "memory":
                add(name, (pixels, channels), F32)
            elif name == "tiles":
                for k in range(batch):
                    add(f"tile{k}", (len(done[0]), self.tile_rows, self.tile_cols, channels), BF)
        if keep is not None:
            add("keep", (pixels, 4 * channels), F32)
        if after is not None:
            add("after", (height * after[1], 4 * channels), F32)
        count = len(operands)
        widest = max([t[2] for t in terms] + [f[2] for frames in done or () for f in frames] + [cols])
        if memory is not None:
            widest = max(widest, memory[2])

        def kernel(*refs):
            ins, out = refs[:count], dict(zip(names, refs[count : count + len(shapes)]))
            stage_ref, shift_ref, sum_ref, before_ref, turn_ref, *patch_refs = refs[
                count + len(shapes) :
            ]
            weight_ref, bias_ref = ins[:2]
            info = Position(batch)

            def ref_of(at):
                return [ref_of(a) for a in at] if isinstance(at, list) else ins[at]

            @pl.when(info.section == turn)
            def _():
                last, patches = None, []
                for (_, index, span, part), at in zip(terms, term_at):
                    if (at, index) != last:
                        patches.append(patch_refs[len(patches)])
                        self.load(ref_of(at), index, info, stage_ref, turn_ref, span)
                        self.spread(stage_ref, shift_ref, patches[-1], span, cols)
                    else:
                        patches.append(patches[-1])
                    last = (at, index)
                for lane, wide in self.ranges():
                    total = None
                    for n, (_, _, _, part) in enumerate(terms):
                        term = self.product(weight_ref, part, patches[n], cols, lane, wide)
                        total = term if total is None else total + term
                        if keep == n + 1:
                            out["keep"][:, pl.ds(lane, wide)] = total
                    sum_ref[:, pl.ds(lane, wide)] = total
                gates = [(sum_ref, cols)]
                if gates_in is not None:
                    gates.append((ins[gates_at], gates_in[1]))
                before = None
                if memory is not None:
                    ref = ins[memory_at]
                    if ref.shape[-1] == channels:
                        before = (ref, memory[2])
                    else:
                        self.load(ref, memory[1], info, before_ref, None, memory[2])
                        before = (before_ref.at[pl.ds(8, memory[2] * height), :], memory[2])
                both = out.get("both")
                cell_ref = out.get("memory", before_ref.at[pl.ds(0, pixels), :] if both is not None else None)
                for lane, wide in self.ranges():
                    self.update(
                        info, gates, bias_ref, before, cols, stage_ref, cell_ref, lane, wide
                    )
                if "hidden" in out:
                    self.pack(stage_ref, 8, cols, out["hidden"], cols)
                if both is not None:
                    self.pack(stage_ref, 8, cols, both.at[0], both_cols)
                    self.pack(cell_ref, 0, cols, both.at[1], both_cols)
                if after is not None:
                    self.spread(stage_ref, shift_ref, patch_refs[0], cols, after[1])
                    out["after"][...] = self.product(
                        weight_ref, after[0], patch_refs[0], after[1], 0, 4 * channels
                    )

            if relay is not None:

                @pl.when(info.section == relay[0])
                def _():
                    out["both"][...] = ins[relay_at][...]

            if done is not None:
                tile_refs = [out[f"tile{k}"] for k in range(batch)]
                for section, frames in enumerate(done):

                    @pl.when(info.section == section)
                    def _():
                        for frame, (array, index, span) in reversed(list(enumerate(frames))):
                            if array is not None:
                                source = ins[done_at[section][frame]]
                                self.load(source, index, info, stage_ref, None, span)
                            self.tiles(info, stage_ref, turn_ref, span, frame, tile_refs)

        return pl.pallas_call(
            kernel,
            out_shape=shapes,
            in_specs=specs,
            out_specs=[VMEM] * len(shapes),
            scratch_shapes=self.scratch(widest, cols, len(set(map(id, (t[0] for t in terms))))),
            cost_estimate=self.cost(pixels, len(terms) + (after is not None)),
            compiler_params=pltpu.CompilerParams(vmem_limit_bytes=LIMIT),
        )(*operands)

    def cost(self, pixels, products):
        return pl.CostEstimate(
            flops=8 * pixels * TAPS * self.channels * self.channels * products,
            bytes_accessed=pixels * self.channels * 2, transcendentals=0,
        )

    def partial(self, turn, array, index, cols, out_cols, part):
        pixels, channels = self.height * out_cols, self.channels

        def kernel(weight_ref, in_ref, out_ref, stage_ref, shift_ref, *rest):
            patch_ref = rest[-1]
            info = Position(self.batch)

            @pl.when(info.section == turn)
            def _():
                self.load(in_ref, index, info, stage_ref, None, cols)
                self.spread(stage_ref, shift_ref, patch_ref, cols, out_cols)
                out_ref[...] = self.product(
                    weight_ref, part, patch_ref, out_cols, 0, 4 * channels
                )

        return pl.pallas_call(
            kernel,
            out_shape=jax.ShapeDtypeStruct((pixels, 4 * channels), F32),
            in_specs=[VMEM, VMEM],
            out_specs=VMEM,
            scratch_shapes=self.scratch(cols, out_cols),
            cost_estimate=self.cost(pixels, 1),
            compiler_params=pltpu.CompilerParams(vmem_limit_bytes=LIMIT),
        )(self.weight, array)


def gate_order(value, channels):
    whole = channels // LANES * LANES
    gates = [value[:, k * channels : (k + 1) * channels] for k in range(4)]
    return jnp.concatenate([g[:, :whole] for g in gates] + [g[:, whole:] for g in gates], axis=1)


def joined_weight(shards, channels):
    per = 2 * TAPS // len(shards)
    rows, columns = shards[0].shape[0] * len(shards) // 2, shards[0].shape[1]
    joined = None
    for which, shard in enumerate(shards):

        def kernel(*refs, which=which):
            first = lax.rem(lax.axis_index("row") + which, len(shards)) * per
            if which == 0:
                in_ref, out_ref, held_ref, sems = refs

                def copy(j):
                    block = pl.ds(j * channels, channels)
                    return pltpu.make_async_copy(in_ref.at[block], held_ref.at[block], sems.at[j])

                for j in range(per):
                    copy(j).start()
            else:
                _, held_ref, out_ref = refs

            for j in range(per):
                if which == 0:
                    copy(j).wait()
                block = first + j
                value = gate_order(held_ref[pl.ds(j * channels, channels), :], channels)
                tap = pl.multiple_of(lax.div(block, 2) * channels, 16)
                out_ref[lax.rem(block, 2), pl.ds(tap, channels), :] = value

        source = pltpu.with_memory_space_constraint(shard, pltpu.HBM) if which == 0 else shard
        scratch = [pltpu.VMEM(shard.shape, BF), pltpu.SemaphoreType.DMA((per,))]
        joined = pl.pallas_call(
            kernel,
            out_shape=pltpu.VMEM((2, rows, columns), BF),
            in_specs=[HBM] if joined is None else [VMEM, VMEM],
            out_specs=VMEM,
            scratch_shapes=scratch if which == 0 else [],
            input_output_aliases={} if joined is None else {0: 0},
            compiler_params=pltpu.CompilerParams(vmem_limit_bytes=LIMIT),
        )(*([] if joined is None else [joined]), source)
    return joined


def finished(parts, *shape):
    batch = len(parts)

    def kernel(*refs):
        out_ref, sems = refs[batch:]
        place = lax.rem(lax.axis_index("row"), batch)
        copies = []
        for k, ref in enumerate(refs[:batch]):
            target = out_ref.at[0, lax.rem(place - k + batch, batch)]
            copies.append(pltpu.make_async_copy(ref, target, sems.at[k]))
            copies[-1].start()
        for copy in copies:
            copy.wait()

    return pl.pallas_call(
        kernel,
        out_shape=jax.ShapeDtypeStruct((1, batch) + shape, BF),
        in_specs=[VMEM] * batch,
        out_specs=pl.BlockSpec(memory_space=pl.ANY),
        scratch_shapes=[pltpu.SemaphoreType.DMA((batch,))],
        compiler_params=pltpu.CompilerParams(vmem_limit_bytes=LIMIT),
        name="finish",
    )(*parts)


def window_levels(features, gate_weight, gate_bias):
    batch, frames, tile_rows, tile_cols, channels = features.shape
    section, row, col = (lax.axis_index(a) for a in ("section", "row", "col"))
    row_size = lax.axis_size("row")
    groups = row_size // batch
    row_halo = HALO if groups > 1 else 0
    height = tile_rows * batch + 2 * row_halo
    good = [tile_cols + 2 * k for k in range(STEPS)]

    if groups == 1 and batch == 2:
        pieces, wide = paired_pieces(features), tile_cols + 2 * EDGE
    else:
        window, wide = gather_sequence(features), tile_cols + 2 * HALO
        if groups > 1:
            window = with_halo(window, "row", 1, batch)
        window = jnp.swapaxes(with_halo(window, "col", 2, 1), 1, 2)
        pieces = window.reshape(frames, height * wide, channels)

    own_weight = gate_weight[0]
    if row_size == 2 and own_weight.shape[0] % channels == 0:
        shards = [own_weight, lax.ppermute(own_weight, "row", [(0, 1), (1, 0)])]
    else:
        shards = [lax.all_gather(own_weight, "row", axis=0, tiled=True)]

    weight = joined_weight(shards, channels)
    weight = pltpu.with_memory_space_constraint(weight, pltpu.VMEM)
    plan = Plan(weight, gate_bias, height, channels, batch, tile_rows, tile_cols, row_halo)

    h00, c00 = plan.step(0, [(pieces, 0, wide, 0)], good[5], outs=("hidden", "memory"))
    x10 = section_send(h00, (0, 1, 3, 2))
    h01, s01 = plan.step(
        0, [(pieces, 1, wide, 0), (h00, None, good[5], 1)], good[4], memory=(c00, None, good[5]),
        outs=("hidden", "both"), both_cols=good[3],
    )
    x11 = section_send(h01, (0, 1, 3, 2))
    h10, c10, p11 = plan.step(
        1, [(x10, None, good[5], 0)], good[4], after=(1, good[3]), outs=("hidden", "memory")
    )
    (s11,) = plan.step(
        1, [(x11, None, good[4], 0)], good[3], gates_in=(p11, good[3]), memory=(c10, None, good[4]),
        outs=("both",), both_cols=good[3], relay=(0, s01),
    )
    x2 = section_send(s11, (1, 2, 0, 3))
    p30 = plan.partial(3, x2, 0, good[3], good[1], 1)
    h20, c20, p21 = plan.step(
        2, [(x2, 0, good[3], 0), (x2, 0, good[3], 1)], good[2], memory=(x2, 1, good[3]), keep=1,
        outs=("hidden", "memory"),
    )
    x30 = section_send(h20, (2, 3), (0, 1))
    (h21,) = plan.step(
        2, [(h20, None, good[2], 1)], good[1], gates_in=(p21, good[2]), memory=(c20, None, good[2]),
        outs=("hidden",),
    )
    x31 = section_send(h21, (2, 3, 1, 0))
    h30, c30, p31 = plan.step(
        3, [(x30, None, good[2], 0)], good[1], gates_in=(p30, good[1]), memory=(x2, 1, good[3]),
        after=(1, good[0]), outs=("hidden", "memory"),
    )
    tiles = plan.step(
        3, [(x31, None, good[1], 0)], good[0], gates_in=(p31, good[0]), memory=(c30, None, good[1]),
        outs=("tiles",),
        done=(
            ((h00, None, good[5]), (h01, None, good[4])),
            ((h10, None, good[4]), (s11, 0, good[3])),
            ((h20, None, good[2]), (h21, None, good[1])),
            ((h30, None, good[1]), (None, None, good[0])),
        ),
    )

    parts = [tiles[0]]
    for k in range(1, batch):
        parts.append(lax.ppermute(tiles[k], "row", group_pairs(row_size, batch, k)))
    return finished(parts, frames, tile_rows, tile_cols, channels)


def solution(mesh):
    return jax.shard_map(
        window_levels,
        mesh=mesh,
        in_specs=(P(None, None, "row", "col", None), P("section", "row", None), P("section", None)),
        out_specs=P("section", None, None, "row", "col", None),
        check_vma=False,
    )
```

```python
import jax
import jax.numpy as jnp
from jax import lax
from jax.experimental import pallas as pl
from jax.experimental.pallas import tpu as pltpu
from jax.sharding import PartitionSpec as P


HALO = 8
EDGE = 6
TAPS = 9
LANES = 128
BF = jnp.bfloat16
F32 = jnp.float32
VMEM = pl.BlockSpec(memory_space=pltpu.VMEM)
HBM = pl.BlockSpec(memory_space=pltpu.HBM)
LIMIT = 12 * 1024 * 1024
STEPS = 6


def section_send(block, *routes):
    pairs = [(r[i], r[(i + 1) % len(r)]) for r in routes for i in range(len(r))]
    return lax.ppermute(block, "section", pairs)


class Position:
    def __init__(self, batch):
        row = lax.axis_index("row")
        self.section, self.col, self.last_col = (
            lax.axis_index("section"), lax.axis_index("col"), lax.axis_size("col") - 1,
        )
        self.place, self.group = lax.rem(row, batch), lax.div(row, batch)
        self.last_group = lax.axis_size("row") // batch - 1


def group_pairs(size, batch, k):
    return [(i, i - i % batch + (i % batch + k) % batch) for i in range(size)]


def gather_sequence(features):
    batch = features.shape[0]
    size = lax.axis_size("row")
    place = lax.axis_index("row") % batch
    parts = [lax.dynamic_index_in_dim(features, place, 0, keepdims=False)]
    for k in range(1, batch):
        sent = lax.dynamic_index_in_dim(features, (place + k) % batch, 0, keepdims=False)
        parts.append(lax.ppermute(sent, "row", group_pairs(size, batch, k)))
    stacked = jnp.stack(parts)
    blocks = [
        lax.dynamic_index_in_dim(stacked, (place - q) % batch, 0, keepdims=False)
        for q in range(batch)
    ]
    return jnp.concatenate(blocks, axis=1)


def with_halo(array, axis, dim, stride):
    size, length = lax.axis_size(axis), array.shape[dim]
    up = [(i, i + stride) for i in range(size - stride)]
    down = [(j, i) for i, j in up]
    last = lax.slice_in_dim(array, length - HALO, length, axis=dim)
    first = lax.slice_in_dim(array, 0, HALO, axis=dim)
    before = lax.ppermute(last, axis, up)
    after = lax.ppermute(first, axis, down)
    return jnp.concatenate([before, array, after], axis=dim)


def paired_pieces(features):
    batch, frames, tile_rows, tile_cols, channels = features.shape
    cols = lax.axis_size("col")
    partner = lax.ppermute(features, "row", [(0, 1), (1, 0)])

    def take(in_ref, out_ref, sem):
        copy = pltpu.make_async_copy(in_ref, out_ref, sem)
        copy.start()
        copy.wait()

    own = pl.pallas_call(
        take,
        out_shape=pltpu.VMEM(features.shape, features.dtype),
        in_specs=[HBM],
        out_specs=VMEM,
        scratch_shapes=[pltpu.SemaphoreType.DMA(())],
        compiler_params=pltpu.CompilerParams(vmem_limit_bytes=LIMIT),
        name="take",
    )(pltpu.with_memory_space_constraint(features, pltpu.HBM))

    def kernel(own_ref, partner_ref, out_ref):
        right = lax.axis_index("row") == 0
        for which, ref in enumerate((own_ref, partner_ref)):
            for frame in range(frames):
                for b in range(batch):
                    sides = []
                    for i in range(tile_rows):
                        row = ref[b, frame, i].astype(F32)
                        sides.append(jnp.where(right, row[tile_cols - EDGE :], row[:EDGE]))
                    side = jnp.concatenate(sides).astype(BF)
                    out_ref[which, frame, :, pl.ds(b * channels, channels)] = side

    edge = pl.pallas_call(
        kernel,
        out_shape=jax.ShapeDtypeStruct((2, frames, tile_rows * EDGE, batch * channels), BF),
        in_specs=[VMEM, VMEM],
        out_specs=VMEM,
        compiler_params=pltpu.CompilerParams(vmem_limit_bytes=LIMIT),
        name="edge",
    )(own, partner)
    up = list(range(cols))
    ring = up + [cols + c for c in reversed(up)]
    pairs = [(ring[i], ring[(i + 1) % len(ring)]) for i in range(len(ring))]
    side = lax.ppermute(edge, ("row", "col"), pairs)
    other = lax.ppermute(side, "row", [(0, 1), (1, 0)])
    return [own, partner, side, other]


def sigmoid(x):
    return 0.5 * jnp.tanh(0.5 * x) + 0.5


class Plan:
    def __init__(self, weight, bias, height, channels, batch, tile_rows, tile_cols, row_halo):
        self.weight, self.bias = weight, bias
        self.height, self.channels, self.batch = height, channels, batch
        self.tile_rows, self.tile_cols, self.row_halo = tile_rows, tile_cols, row_halo

    def lanes(self):
        return [(k, min(LANES, self.channels - k)) for k in range(0, self.channels, LANES)]

    def load(self, ref, index, info, stage_ref, turn_ref, cols):
        channels, height = self.channels, self.height
        pixels = cols * height
        if not isinstance(ref, list):
            value = ref[...] if index is None else ref[index]
            if value.shape[-1] == channels:
                stage_ref[pl.ds(8, pixels), :] = value.astype(F32)
            else:
                half = pixels // 2
                for k in range(2):
                    part = value[:, k * channels : (k + 1) * channels]
                    stage_ref[pl.ds(8 + k * half, half), :] = part.astype(F32)
            return
        own, partner, side, other = ref
        rows, place, tile_cols = self.tile_rows, info.place, self.tile_cols
        first = place == 0
        left, right = info.col > 0, info.col < info.last_col

        def put(value, row, col):
            count = value.shape[0]
            for n, (lane, width) in enumerate(self.lanes()):
                part = value[:, lane : lane + width]
                if width < LANES:
                    part = jnp.concatenate([part, jnp.zeros((count, LANES - width), F32)], axis=1)
                turn_ref[n, pl.ds(col * height + row, count, stride=height), :] = part

        def mine(piece, k):
            value = piece[k, index].astype(F32)
            return jnp.where(first, value[:, :channels], value[:, channels:])

        sides = [(mine(side, k), mine(other, k)) for k in range(2)]

        for i in range(rows):
            a, b = own[place, index, i].astype(F32), partner[place, index, i].astype(F32)
            put(jnp.where(first, a, b), i, EDGE)
            put(jnp.where(first, b, a), rows + i, EDGE)
            for k in range(2):
                a, b = (v[i * EDGE : (i + 1) * EDGE] for v in sides[k])
                put(jnp.where(left, jnp.where(first, a, b), 0.0), k * rows + i, 0)
                put(jnp.where(right, jnp.where(first, b, a), 0.0), (1 - k) * rows + i, EDGE + tile_cols)
        for n, (lane, width) in enumerate(self.lanes()):
            value = turn_ref[n, pl.ds(0, pixels), :]
            stage_ref[pl.ds(8, pixels), pl.ds(lane, width)] = value[:, :width]

    def spread(self, stage_ref, shift_ref, patch_ref, cols, out_cols):
        channels, height = self.channels, self.height
        inset = (cols - out_cols) // 2
        used = (out_cols + 2) * height
        start = 8 + (inset - 1) * height
        row = lax.broadcasted_iota(jnp.int32, (out_cols + 2, height, channels), 1)
        for k, offset in enumerate((-1, 1)):
            value = stage_ref[pl.ds(start + offset, used), :].reshape(out_cols + 2, height, channels)
            value = jnp.where(row == (0 if k == 0 else height - 1), 0.0, value)
            shift_ref[k, pl.ds(0, used), :] = value.reshape(used, channels)
        pixels = out_cols * height
        for tap in range(TAPS):
            row_tap, col_tap = tap // 3, tap % 3
            if row_tap == 1:
                value = stage_ref[pl.ds(start + col_tap * height, pixels), :]
            else:
                value = shift_ref[row_tap // 2, pl.ds(col_tap * height, pixels), :]
            patch_ref[pl.ds(0, pixels), pl.ds(tap * channels, channels)] = value.astype(BF)

    def ranges(self):
        split = self.channels // LANES * LANES * 4
        return (0, split), (split, 4 * self.channels - split)

    def product(self, weight_ref, part, patch_ref, cols, lane, width):
        return jnp.dot(
            patch_ref[pl.ds(0, cols * self.height), :],
            weight_ref[part, :, pl.ds(lane, width)],
            preferred_element_type=F32,
        )

    def cell(self, total, before):
        width = total.shape[-1] // 4
        if width % LANES == 0:
            gate = [total[:, k * width : (k + 1) * width] for k in range(4)]
            cell = sigmoid(gate[0]) * jnp.tanh(gate[2])
            if before is not None:
                cell = cell + sigmoid(gate[1]) * before
            return sigmoid(gate[3]) * jnp.tanh(cell), cell
        first, second = sigmoid(total[:, : 2 * width]), total[:, 2 * width :]
        low = lax.broadcasted_iota(jnp.int32, second.shape, 1) < width
        scale = jnp.where(low, 1.0, 0.5)
        second = scale * jnp.tanh(scale * second) + jnp.where(low, 0.0, 0.5)
        cell = (first * second)[:, :width]
        if before is not None:
            cell = cell + pltpu.roll(first, width, 1)[:, :width] * before
        return pltpu.roll(second, width, 1)[:, :width] * jnp.tanh(cell), cell

    def update(self, info, gates, bias_ref, memory, cols, stage_ref, cell_ref, lane, width):
        ch, height = width // 4, self.height
        first = lane // 4
        bias = gate_order(bias_ref[...], self.channels)[:, lane : lane + width]
        halo = (cols - self.tile_cols) // 2
        pieces = [(0, halo, info.col > 0)]
        pieces += [(halo + c, 4, None) for c in range(0, self.tile_cols, 4)]
        pieces += [(cols - halo, halo, info.col < info.last_col)]

        def part(ref, ref_cols, col, count, lane, width):
            start = (col + (ref_cols - cols) // 2) * height
            return ref[pl.ds(start, count * height), pl.ds(lane, width)]

        for col, count, inside in pieces:
            if count == 0:
                continue
            total = bias
            for ref, ref_cols in gates:
                total = total + part(ref, ref_cols, col, count, lane, width)
            before = None
            if memory is not None:
                before = part(*memory, col, count, first, ch).astype(F32)
            hidden, cell = self.cell(total, before)
            if inside is not None:
                hidden = jnp.where(inside, hidden, 0.0)
            if self.row_halo:
                row = lax.broadcasted_iota(jnp.int32, (count, height, ch), 1)
                top = jnp.where(info.group == 0, self.row_halo, 0)
                bottom = jnp.where(info.group == info.last_group, height - self.row_halo, height)
                hidden = hidden.reshape(count, height, ch)
                hidden = jnp.where((row >= top) & (row < bottom), hidden, 0.0)
                hidden = hidden.reshape(count * height, ch)
            stage_ref[pl.ds(8 + col * height, count * height), pl.ds(first, ch)] = hidden
            if cell_ref is not None:
                cell_ref[pl.ds(col * height, count * height), pl.ds(first, ch)] = cell

    def pack(self, source_ref, offset, cols, out_ref, out_cols):
        half, channels = out_cols * self.height // 2, self.channels
        start = offset + (cols - out_cols) // 2 * self.height
        for k in range(2):
            value = source_ref[pl.ds(start + k * half, half), :]
            out_ref[:, pl.ds(k * channels, channels)] = value.astype(BF)

    def tiles(self, info, stage_ref, turn_ref, cols, frame, outs):
        halo, pixels = (cols - self.tile_cols) // 2, self.tile_cols * self.height
        for n, (lane, width) in enumerate(self.lanes()):
            value = stage_ref[pl.ds(8 + halo * self.height, pixels), pl.ds(lane, width)]
            if width < LANES:
                value = jnp.concatenate([value, jnp.zeros((pixels, LANES - width), F32)], axis=1)
            turn_ref[n, pl.ds(0, pixels), :] = value
        for i in range(self.tile_rows):
            rows = []
            for b in range(self.batch):
                start = self.row_halo + b * self.tile_rows + i
                row = [
                    turn_ref[n, pl.ds(start, self.tile_cols, stride=self.height), :][:, :width]
                    for n, (_, width) in enumerate(self.lanes())
                ]
                rows.append(jnp.concatenate(row, axis=1))
            for k, out in enumerate(outs):
                value = rows[0]
                for b in range(1, self.batch):
                    value = jnp.where(lax.rem(info.place + k, self.batch) == b, rows[b], value)
                out[frame, i] = value.astype(BF)

    def scratch(self, widest, cols, patches=1):
        pixels, channels = cols * self.height, self.channels
        return [
            pltpu.VMEM((widest * self.height + 16, channels), F32),
            pltpu.VMEM((2, (cols + 2) * self.height, channels), F32),
            pltpu.VMEM((pixels, 4 * channels), F32),
            pltpu.VMEM((widest * self.height + 16, channels), F32),
            pltpu.VMEM((len(self.lanes()), widest * self.height, LANES), F32),
        ] + [pltpu.VMEM((pixels, TAPS * channels), BF)] * patches

    def step(self, turn, terms, cols, gates_in=None, memory=None, keep=None, after=None, outs=(),
             both_cols=None, done=None, relay=None):
        channels, batch, height = self.channels, self.batch, self.height
        pixels = height * cols
        operands = [self.weight, self.bias]
        specs = [VMEM, VMEM]
        seen = {}

        def place_of(array):
            if array is None:
                return None
            if isinstance(array, list):
                return [place_of(a) for a in array]
            if id(array) not in seen:
                seen[id(array)] = len(operands)
                operands.append(array)
                specs.append(VMEM)
            return seen[id(array)]

        term_at = [place_of(t[0]) for t in terms]
        gates_at = place_of(gates_in[0]) if gates_in is not None else None
        memory_at = place_of(memory[0]) if memory is not None else None
        done_at = [[place_of(f[0]) for f in frames] for frames in done] if done else None
        relay_at = place_of(relay[1]) if relay is not None else None
        shapes, names = [], []

        def add(name, shape, dtype):
            shapes.append(jax.ShapeDtypeStruct(shape, dtype))
            names.append(name)

        for name in outs:
            if name == "hidden":
                add(name, (pixels // 2, 2 * channels), BF)
            elif name == "both":
                add(name, (2, both_cols * height // 2, 2 * channels), BF)
            elif name == "memory":
                add(name, (pixels, channels), F32)
            elif name == "tiles":
                for k in range(batch):
                    add(f"tile{k}", (len(done[0]), self.tile_rows, self.tile_cols, channels), BF)
        if keep is not None:
            add("keep", (pixels, 4 * channels), F32)
        if after is not None:
            add("after", (height * after[1], 4 * channels), F32)
        count = len(operands)
        widest = max([t[2] for t in terms] + [f[2] for frames in done or () for f in frames] + [cols])
        if memory is not None:
            widest = max(widest, memory[2])

        def kernel(*refs):
            ins, out = refs[:count], dict(zip(names, refs[count : count + len(shapes)]))
            stage_ref, shift_ref, sum_ref, before_ref, turn_ref, *patch_refs = refs[
                count + len(shapes) :
            ]
            weight_ref, bias_ref = ins[:2]
            info = Position(batch)

            def ref_of(at):
                return [ref_of(a) for a in at] if isinstance(at, list) else ins[at]

            @pl.when(info.section == turn)
            def _():
                last, patches = None, []
                for (_, index, span, part), at in zip(terms, term_at):
                    if (at, index) != last:
                        patches.append(patch_refs[len(patches)])
                        self.load(ref_of(at), index, info, stage_ref, turn_ref, span)
                        self.spread(stage_ref, shift_ref, patches[-1], span, cols)
                    else:
                        patches.append(patches[-1])
                    last = (at, index)
                for lane, wide in self.ranges():
                    total = None
                    for n, (_, _, _, part) in enumerate(terms):
                        term = self.product(weight_ref, part, patches[n], cols, lane, wide)
                        total = term if total is None else total + term
                        if keep == n + 1:
                            out["keep"][:, pl.ds(lane, wide)] = total
                    sum_ref[:, pl.ds(lane, wide)] = total
                gates = [(sum_ref, cols)]
                if gates_in is not None:
                    gates.append((ins[gates_at], gates_in[1]))
                before = None
                if memory is not None:
                    ref = ins[memory_at]
                    if ref.shape[-1] == channels:
                        before = (ref, memory[2])
                    else:
                        self.load(ref, memory[1], info, before_ref, None, memory[2])
                        before = (before_ref.at[pl.ds(8, memory[2] * height), :], memory[2])
                both = out.get("both")
                cell_ref = out.get("memory", before_ref.at[pl.ds(0, pixels), :] if both is not None else None)
                for lane, wide in self.ranges():
                    self.update(
                        info, gates, bias_ref, before, cols, stage_ref, cell_ref, lane, wide
                    )
                if "hidden" in out:
                    self.pack(stage_ref, 8, cols, out["hidden"], cols)
                if both is not None:
                    self.pack(stage_ref, 8, cols, both.at[0], both_cols)
                    self.pack(cell_ref, 0, cols, both.at[1], both_cols)
                if after is not None:
                    self.spread(stage_ref, shift_ref, patch_refs[0], cols, after[1])
                    out["after"][...] = self.product(
                        weight_ref, after[0], patch_refs[0], after[1], 0, 4 * channels
                    )

            if relay is not None:

                @pl.when(info.section == relay[0])
                def _():
                    out["both"][...] = ins[relay_at][...]

            if done is not None:
                tile_refs = [out[f"tile{k}"] for k in range(batch)]
                for section, frames in enumerate(done):

                    @pl.when(info.section == section)
                    def _():
                        for frame, (array, index, span) in reversed(list(enumerate(frames))):
                            if array is not None:
                                source = ins[done_at[section][frame]]
                                self.load(source, index, info, stage_ref, None, span)
                            self.tiles(info, stage_ref, turn_ref, span, frame, tile_refs)

        return pl.pallas_call(
            kernel,
            out_shape=shapes,
            in_specs=specs,
            out_specs=[VMEM] * len(shapes),
            scratch_shapes=self.scratch(widest, cols, len(set(map(id, (t[0] for t in terms))))),
            cost_estimate=self.cost(pixels, len(terms) + (after is not None)),
            compiler_params=pltpu.CompilerParams(vmem_limit_bytes=LIMIT),
        )(*operands)

    def cost(self, pixels, products):
        return pl.CostEstimate(
            flops=8 * pixels * TAPS * self.channels * self.channels * products,
            bytes_accessed=pixels * self.channels * 2, transcendentals=0,
        )

    def partial(self, turn, array, index, cols, out_cols, part):
        pixels, channels = self.height * out_cols, self.channels

        def kernel(weight_ref, in_ref, out_ref, stage_ref, shift_ref, *rest):
            patch_ref = rest[-1]
            info = Position(self.batch)

            @pl.when(info.section == turn)
            def _():
                self.load(in_ref, index, info, stage_ref, None, cols)
                self.spread(stage_ref, shift_ref, patch_ref, cols, out_cols)
                out_ref[...] = self.product(
                    weight_ref, part, patch_ref, out_cols, 0, 4 * channels
                )

        return pl.pallas_call(
            kernel,
            out_shape=jax.ShapeDtypeStruct((pixels, 4 * channels), F32),
            in_specs=[VMEM, VMEM],
            out_specs=VMEM,
            scratch_shapes=self.scratch(cols, out_cols),
            cost_estimate=self.cost(pixels, 1),
            compiler_params=pltpu.CompilerParams(vmem_limit_bytes=LIMIT),
        )(self.weight, array)


def gate_order(value, channels):
    whole = channels // LANES * LANES
    gates = [value[:, k * channels : (k + 1) * channels] for k in range(4)]
    return jnp.concatenate([g[:, :whole] for g in gates] + [g[:, whole:] for g in gates], axis=1)


def joined_weight(shards, channels):
    per = 2 * TAPS // len(shards)
    rows, columns = shards[0].shape[0] * len(shards) // 2, shards[0].shape[1]
    joined = None
    for which, shard in enumerate(shards):

        def kernel(*refs, which=which):
            first = lax.rem(lax.axis_index("row") + which, len(shards)) * per
            if which == 0:
                in_ref, out_ref, held_ref, sems = refs

                def copy(j):
                    block = pl.ds(j * channels, channels)
                    return pltpu.make_async_copy(in_ref.at[block], held_ref.at[block], sems.at[j])

                for j in range(per):
                    copy(j).start()
            else:
                _, held_ref, out_ref = refs

            for j in range(per):
                if which == 0:
                    copy(j).wait()
                block = first + j
                value = gate_order(held_ref[pl.ds(j * channels, channels), :], channels)
                tap = pl.multiple_of(lax.div(block, 2) * channels, 16)
                out_ref[lax.rem(block, 2), pl.ds(tap, channels), :] = value

        source = pltpu.with_memory_space_constraint(shard, pltpu.HBM) if which == 0 else shard
        scratch = [pltpu.VMEM(shard.shape, BF), pltpu.SemaphoreType.DMA((per,))]
        joined = pl.pallas_call(
            kernel,
            out_shape=pltpu.VMEM((2, rows, columns), BF),
            in_specs=[HBM] if joined is None else [VMEM, VMEM],
            out_specs=VMEM,
            scratch_shapes=scratch if which == 0 else [],
            input_output_aliases={} if joined is None else {0: 0},
            compiler_params=pltpu.CompilerParams(vmem_limit_bytes=LIMIT),
        )(*([] if joined is None else [joined]), source)
    return joined


def finished(parts, *shape):
    batch = len(parts)

    def kernel(*refs):
        out_ref, sems = refs[batch:]
        place = lax.rem(lax.axis_index("row"), batch)
        copies = []
        for k, ref in enumerate(refs[:batch]):
            target = out_ref.at[0, lax.rem(place - k + batch, batch)]
            copies.append(pltpu.make_async_copy(ref, target, sems.at[k]))
            copies[-1].start()
        for copy in copies:
            copy.wait()

    return pl.pallas_call(
        kernel,
        out_shape=jax.ShapeDtypeStruct((1, batch) + shape, BF),
        in_specs=[VMEM] * batch,
        out_specs=pl.BlockSpec(memory_space=pl.ANY),
        scratch_shapes=[pltpu.SemaphoreType.DMA((batch,))],
        compiler_params=pltpu.CompilerParams(vmem_limit_bytes=LIMIT),
        name="finish",
    )(*parts)


def window_levels(features, gate_weight, gate_bias):
    batch, frames, tile_rows, tile_cols, channels = features.shape
    section, row, col = (lax.axis_index(a) for a in ("section", "row", "col"))
    row_size = lax.axis_size("row")
    groups = row_size // batch
    row_halo = HALO if groups > 1 else 0
    height = tile_rows * batch + 2 * row_halo
    good = [tile_cols + 2 * k for k in range(STEPS)]

    if groups == 1 and batch == 2:
        pieces, wide = paired_pieces(features), tile_cols + 2 * EDGE
    else:
        window, wide = gather_sequence(features), tile_cols + 2 * HALO
        if groups > 1:
            window = with_halo(window, "row", 1, batch)
        window = jnp.swapaxes(with_halo(window, "col", 2, 1), 1, 2)
        pieces = window.reshape(frames, height * wide, channels)

    own_weight = gate_weight[0]
    if row_size == 2 and own_weight.shape[0] % channels == 0:
        shards = [own_weight, lax.ppermute(own_weight, "row", [(0, 1), (1, 0)])]
    else:
        shards = [lax.all_gather(own_weight, "row", axis=0, tiled=True)]

    weight = joined_weight(shards, channels)
    weight = pltpu.with_memory_space_constraint(weight, pltpu.VMEM)
    plan = Plan(weight, gate_bias, height, channels, batch, tile_rows, tile_cols, row_halo)

    h00, c00 = plan.step(0, [(pieces, 0, wide, 0)], good[5], outs=("hidden", "memory"))
    x10 = section_send(h00, (0, 1), (2, 3))
    h01, s01 = plan.step(
        0, [(pieces, 1, wide, 0), (h00, None, good[5], 1)], good[4], memory=(c00, None, good[5]),
        outs=("hidden", "both"), both_cols=good[3],
    )
    x11 = section_send(h01, (0, 1), (2, 3))
    h10, c10, p11 = plan.step(
        1, [(x10, None, good[5], 0)], good[4], after=(1, good[3]), outs=("hidden", "memory")
    )
    (s11,) = plan.step(
        1, [(x11, None, good[4], 0)], good[3], gates_in=(p11, good[3]), memory=(c10, None, good[4]),
        outs=("both",), both_cols=good[3], relay=(0, s01),
    )
    x2 = section_send(s11, (1, 2, 0, 3))
    p30 = plan.partial(3, x2, 0, good[3], good[1], 1)
    h20, c20, p21 = plan.step(
        2, [(x2, 0, good[3], 0), (x2, 0, good[3], 1)], good[2], memory=(x2, 1, good[3]), keep=1,
        outs=("hidden", "memory"),
    )
    x30 = section_send(h20, (2, 3), (0, 1))
    (h21,) = plan.step(
        2, [(h20, None, good[2], 1)], good[1], gates_in=(p21, good[2]), memory=(c20, None, good[2]),
        outs=("hidden",),
    )
    x31 = section_send(h21, (2, 3), (0, 1))
    h30, c30, p31 = plan.step(
        3, [(x30, None, good[2], 0)], good[1], gates_in=(p30, good[1]), memory=(x2, 1, good[3]),
        after=(1, good[0]), outs=("hidden", "memory"),
    )
    tiles = plan.step(
        3, [(x31, None, good[1], 0)], good[0], gates_in=(p31, good[0]), memory=(c30, None, good[1]),
        outs=("tiles",),
        done=(
            ((h00, None, good[5]), (h01, None, good[4])),
            ((h10, None, good[4]), (s11, 0, good[3])),
            ((h20, None, good[2]), (h21, None, good[1])),
            ((h30, None, good[1]), (None, None, good[0])),
        ),
    )

    parts = [tiles[0]]
    for k in range(1, batch):
        parts.append(lax.ppermute(tiles[k], "row", group_pairs(row_size, batch, k)))
    return finished(parts, frames, tile_rows, tile_cols, channels)


def solution(mesh):
    return jax.shard_map(
        window_levels,
        mesh=mesh,
        in_specs=(P(None, None, "row", "col", None), P("section", "row", None), P("section", None)),
        out_specs=P("section", None, None, "row", "col", None),
        check_vma=False,
    )
```
